256 devices in a mesh: dp: 8 (over x_lo, y), tensor: 32 (over z, x_hi, core).
Axes of the slice: x: 4 (x_hi: 2, x_lo: 2; x = x_hi * 2 + x_lo), y: 4, z: 8, core: 2. Of those that a mesh axis runs over, the one named last changes fastest.
Arguments:
- tokens: bfloat16 [4096, 4096], P(('dp', 'tensor')), may hold values from -24 to 24
- weight: bfloat16 [4096, 28672], P(None, 'tensor'), may hold values from -0.125 to 0.125
- block_mask: int32 [64, 448], replicated, may hold values from 0 to 1, as said below
- act_grad: bfloat16 [4096, 28672], P('dp', 'tensor'), may hold values from -6 to 6
Outputs:
- act: bfloat16 [4096, 28672], P('dp', 'tensor')
- x_grad: bfloat16 [4096, 4096], P(('dp', 'tensor'))
- weight_grad: float32 [4096, 28672], P('dp', 'tensor')
The draws below stay inside these ranges and needn't reach their ends.
Inputs may be any that keep to these rules, and one draw needn't show every extreme that they name: `block_mask`: split block rows into 8 equal consecutive groups and block columns into 32; each such region keeps at most 70 blocks, and some region keeps exactly 70.
All inputs are finite; a program needn't handle non-finite values.
Results may differ from the reference program's by a relative error of at most 0.015.
Values may be sent and summed in bfloat16 or wider, within the bound.
No kernel may reach another device: no remote copies, remote signals or barrier semaphores. Data moves between devices by JAX's collectives and lax.ppermute only.
A program may use at most 128 MiB of HBM per device.

```python
import jax
import jax.numpy as jnp
from jax import lax

D = 4096
FFW = 28672
BLOCK = 64
TG = 512
TOKENS = 4096
CAP = 70
N_DP = 8
N_TENSOR = 32


def draw_block_mask(key, part):
    region_rows = D // (N_DP * BLOCK)
    region_cols = FFW // (N_TENSOR * BLOCK)
    region = region_rows * region_cols
    regions = N_DP * N_TENSOR
    key_count = jax.random.fold_in(key, 11)
    key_top = jax.random.fold_in(key, 12)
    key_rank = jax.random.fold_in(key, 13)
    counts = jax.random.randint(key_count, (regions,), region * 3 // 8, CAP + 1)
    chosen = jax.random.randint(key_top, (), 0, regions)
    counts = jnp.where(jnp.arange(regions) == chosen, CAP, counts)
    rank_keys = jax.random.split(key_rank, regions)
    ranks = jax.vmap(lambda single: jax.random.permutation(single, region))(rank_keys)
    kept = (ranks < counts[:, None]).astype(jnp.int32)
    kept = kept.reshape(N_DP, N_TENSOR, region_rows, region_cols).transpose(0, 2, 1, 3)
    return kept.reshape(N_DP * region_rows, N_TENSOR * region_cols)


def spiked(values, key, source, target, blocks, factor):
    def block_of(axis_at):
        return (jnp.arange(values.shape[axis_at]) // (values.shape[axis_at] // blocks)).reshape((-1,) + (1,) * (values.ndim - 1 - axis_at))

    one_side = jax.random.permutation(key, blocks)[block_of(target)]
    other_side = (block_of(target) + blocks // 2) % blocks
    return jnp.where((block_of(source) == one_side) | (block_of(source) == other_side), factor * values, values)


def steps_of(rng, extent, cuts, smallest, top_value):
    level = 1.0
    for dim, shards_of in cuts:
        draws = jax.random.uniform(jax.random.fold_in(jax.random.fold_in(rng, 6), dim), (shards_of,), jnp.float32, smallest / len(cuts), top_value / len(cuts))
        level = level * jnp.repeat(jnp.exp(draws), extent[dim] // shards_of).reshape((-1,) + (1,) * (len(extent) - 1 - dim))
    return level


def bell_draw(rng, dims, scale, bound, shards=(), dtype=jnp.bfloat16):
    factor_of = steps_of(rng, dims, shards, -0.22, 0.18) if shards else 1.0
    array = jax.random.normal(rng, dims, jnp.float32) * scale * factor_of
    return jnp.minimum(jnp.maximum(array, -bound), bound).astype(dtype)


def bell_draw_with(key, extent, deviation, limit, pieces, heavy, held_as=jnp.bfloat16):
    array = deviation * jax.random.normal(key, extent, jnp.float32)
    if pieces:
        array = array * steps_of(key, extent, pieces, -0.22, 0.18)
    return jnp.clip(spiked(array, jax.random.fold_in(key, 3), *heavy), -limit, limit).astype(held_as)


def setup_inputs(seed: int = 0) -> dict:
    keys = jax.random.split(jax.random.key(seed), 5)
    return {
        "tokens": bell_draw_with(keys[0], (TOKENS, D), 1.0, 24.0, ((0, 256),), (0, 1, 256, 6.0)),
        "weight": bell_draw(keys[1], (D, FFW), (D // 2) ** -0.5, 0.125, ((1, 32),)),
        "block_mask": draw_block_mask(jax.random.fold_in(keys[4], 71), 0),
        "act_grad": bell_draw_with(keys[3], (TOKENS, FFW), 1.0, 6.0, ((0, 8), (1, 32)), (1, 0, 32, 2.75)),
    }


def reference(tokens, weight, block_mask, act_grad):
    expand = jnp.repeat(jnp.repeat(block_mask, BLOCK, axis=0), BLOCK, axis=1).astype(jnp.bfloat16)
    masked = weight * expand
    pre = jnp.dot(tokens, masked, preferred_element_type=jnp.float32)
    sigma = jax.nn.sigmoid(pre)
    act = (pre * sigma).astype(jnp.bfloat16)
    pre_grad = (act_grad.astype(jnp.float32) * sigma * (1.0 + pre * (1.0 - sigma))).astype(jnp.bfloat16)
    width = FFW // N_TENSOR
    grad_groups = pre_grad.reshape(TOKENS, N_TENSOR, width).transpose(1, 0, 2)
    weight_groups = masked.reshape(D, N_TENSOR, width).transpose(1, 0, 2)

    def add_group(total, pair):
        group_grad, group_weight = pair
        partial_sum = lax.dot_general(group_grad, group_weight, (((1,), (1,)), ((), ())), preferred_element_type=jnp.float32)
        partial_sum = lax.optimization_barrier(partial_sum.astype(jnp.bfloat16)).astype(jnp.float32)
        return total + partial_sum, None

    total, unused = lax.scan(add_group, jnp.zeros((TOKENS, D), jnp.float32), (grad_groups, weight_groups))
    x_grad = total.astype(jnp.bfloat16)
    token_groups = tokens.reshape(N_DP, TG, D)
    pre_groups = pre_grad.reshape(N_DP, TG, FFW)

    def add_data(total, pair):
        group_tokens, group_pre = pair
        partial_sum = lax.dot_general(group_tokens, group_pre, (((0,), (0,)), ((), ())), preferred_element_type=jnp.float32)
        partial_sum = lax.optimization_barrier(partial_sum.astype(jnp.bfloat16)).astype(jnp.float32)
        return total + partial_sum, None

    summed, unused_two = lax.scan(add_data, jnp.zeros((D, FFW), jnp.float32), (token_groups, pre_groups))
    weight_grad = expand.astype(jnp.float32) * summed
    return (act, x_grad, weight_grad)
```

```python
import functools

import jax
import jax.numpy as jnp
from jax import lax
from jax.experimental import pallas as pl
from jax.experimental.pallas import tpu as pltpu
from jax.sharding import PartitionSpec as P

BLOCK = 64
CAP = 70
NZ = 8
NY = 4
F32 = jnp.float32
BF16 = jnp.bfloat16


def tensor_perm(dz, dx, dc):
    pairs = []
    for z in range(NZ):
        for xh in range(2):
            for core in range(2):
                source = (z * 2 + xh) * 2 + core
                target = (((z + dz) % NZ) * 2 + (xh ^ dx)) * 2 + (core ^ dc)
                pairs.append((source, target))
    return pairs


def dp_perm(dx, dy):
    return [
        (xl * NY + y, (xl ^ dx) * NY + (y + dy) % NY) for xl in range(2) for y in range(NY)
    ]


def params(n_axes):
    return pltpu.CompilerParams(dimension_semantics=("arbitrary",) * n_axes)


def mask_kernel(t_ref, w_ref, m_ref, o_ref):
    blocks = m_ref.shape[1]
    width = w_ref.shape[1]
    rows = lax.broadcasted_iota(jnp.int32, (blocks, width), 0)
    cols = lax.broadcasted_iota(jnp.int32, (blocks, width), 1)
    pick = (rows == t_ref[0] + lax.div(cols, BLOCK)).astype(BF16)
    expanded = jnp.dot(m_ref[...].astype(F32).astype(BF16), pick, preferred_element_type=F32)
    for i in range(8):
        row = jnp.broadcast_to(expanded[i : i + 1, :], (BLOCK, width)).astype(BF16)
        o_ref[i * BLOCK : (i + 1) * BLOCK, :] = w_ref[i * BLOCK : (i + 1) * BLOCK, :] * row


def masked_weight(t_first, weight, block_mask):
    d, width = weight.shape
    blocks = block_mask.shape[1]
    return pl.pallas_call(
        mask_kernel,
        out_shape=jax.ShapeDtypeStruct((d, width), BF16),
        grid_spec=pltpu.PrefetchScalarGridSpec(
            num_scalar_prefetch=1,
            grid=(d // 512,),
            in_specs=[
                pl.BlockSpec((512, width), lambda s, t: (s, 0)),
                pl.BlockSpec((8, blocks), lambda s, t: (s, 0)),
            ],
            out_specs=pl.BlockSpec((512, width), lambda s, t: (s, 0)),
        ),
        compiler_params=params(1),
        cost_estimate=pl.CostEstimate(
            flops=d * width, bytes_accessed=4 * d * width, transcendentals=0
        ),
        name="mask_weight",
    )(t_first, weight, block_mask)


def forward_kernel(idx_ref, x0, x1, x2, x3, w_ref, g_ref, act_ref, p_ref, pt_ref, acc_ref):
    step = pl.program_id(0)

    @pl.when(step == 0)
    def _():
        acc_ref[...] = jnp.zeros_like(acc_ref)

    x = jnp.concatenate([x0[...], x1[...], x2[...], x3[...]], axis=0)
    acc_ref[...] += jnp.dot(x, w_ref[...], preferred_element_type=F32)

    @pl.when(step == pl.num_programs(0) - 1)
    def _():
        for n in range(32):
            at = idx_ref[n]
            pre = acc_ref[n * 16 : (n + 1) * 16, :]
            s = jax.nn.sigmoid(pre)
            act_ref[at] = (pre * s).astype(BF16)
            grad = g_ref[at].astype(F32) * s * (1.0 + pre * (1.0 - s))
            p_ref[n * 16 : (n + 1) * 16, :] = grad.astype(BF16)
        for c in range(7):
            tile = p_ref[:, c * 128 : (c + 1) * 128].astype(F32)
            pt_ref[c * 128 : (c + 1) * 128, :] = jnp.transpose(tile).astype(BF16)


def forward(idx, xs, masked, act_grad):
    d, width = masked.shape
    kb = 512
    full = lambda s, i: (0, 0)
    return pl.pallas_call(
        forward_kernel,
        out_shape=(
            jax.ShapeDtypeStruct((32, 16, width), BF16),
            jax.ShapeDtypeStruct((512, width), BF16),
            jax.ShapeDtypeStruct((width, 512), BF16),
        ),
        grid_spec=pltpu.PrefetchScalarGridSpec(
            num_scalar_prefetch=1,
            grid=(d // kb,),
            in_specs=[pl.BlockSpec((128, kb), lambda s, i: (0, s))] * 4
            + [
                pl.BlockSpec((kb, width), lambda s, i: (s, 0)),
                pl.BlockSpec((32, 16, width), lambda s, i: (0, 0, 0)),
            ],
            out_specs=(
                pl.BlockSpec((32, 16, width), lambda s, i: (0, 0, 0)),
                pl.BlockSpec((512, width), full),
                pl.BlockSpec((width, 512), full),
            ),
            scratch_shapes=[pltpu.VMEM((512, width), F32)],
        ),
        compiler_params=params(1),
        cost_estimate=pl.CostEstimate(
            flops=2 * 512 * d * width, bytes_accessed=2 * d * (width + 512), transcendentals=0
        ),
        name="forward",
    )(idx, *xs, masked, act_grad)


def xgrad_other_kernel(p_ref, w_ref, o_ref):
    o_ref[...] = lax.dot_general(
        p_ref[...], w_ref[...], (((1,), (1,)), ((), ())), preferred_element_type=F32
    ).astype(BF16)


def xgrad_own_kernel(p_ref, w_ref, r_ref, *outs):
    part = lax.dot_general(
        p_ref[...], w_ref[...], (((1,), (1,)), ((), ())), preferred_element_type=F32
    )
    total = part.astype(BF16).astype(F32) + r_ref[...].astype(F32)
    for k in range(NZ):
        outs[k][0:16, :] = total[k * 16 : (k + 1) * 16, :].astype(BF16)
        outs[k][16:32, :] = total[128 + k * 16 : 128 + (k + 1) * 16, :].astype(BF16)


def xgrad(p, masked, received):
    d, width = masked.shape
    nb = 512
    own = received is not None
    in_specs = [
        pl.BlockSpec((256, width), lambda s: (0 if own else 1, 0)),
        pl.BlockSpec((nb, width), lambda s: (s, 0)),
    ]
    if own:
        in_specs.append(pl.BlockSpec((256, nb), lambda s: (0, s)))
        out_shape = [jax.ShapeDtypeStruct((32, d), BF16)] * NZ
        out_specs = [pl.BlockSpec((32, nb), lambda s: (0, s))] * NZ
    else:
        out_shape = jax.ShapeDtypeStruct((256, d), BF16)
        out_specs = pl.BlockSpec((256, nb), lambda s: (0, s))
    args = (p, masked, received) if own else (p, masked)
    return pl.pallas_call(
        xgrad_own_kernel if own else xgrad_other_kernel,
        out_shape=out_shape,
        grid=(d // nb,),
        in_specs=in_specs,
        out_specs=out_specs,
        compiler_params=params(1),
        cost_estimate=pl.CostEstimate(
            flops=2 * 256 * d * width, bytes_accessed=2 * d * (width + 256), transcendentals=0
        ),
        name="xgrad_own" if own else "xgrad_other",
    )(*args)


def wgrad_kernel(first, dest_ref, list_ref, pt_ref, x0, x1, x2, x3, *rest):
    outs, (acc_ref,) = rest[:-1], rest[-1:]
    step = pl.program_id(0)
    x = jnp.concatenate([x0[...], x1[...], x2[...], x3[...]], axis=0)
    acc_ref[...] = jnp.dot(pt_ref[...], x, preferred_element_type=F32)
    dest = dest_ref[first + step]
    left = lax.broadcasted_iota(jnp.int32, (32, 128), 1) < BLOCK

    for n, out in enumerate(outs):

        @pl.when(step == n)
        def _():
            def pack(s, carry):
                b = list_ref[dest, s]
                i = lax.div(b, 14)
                j = b - i * 14
                h = lax.rem(i, 2)
                row = pl.multiple_of(j * BLOCK, BLOCK)
                lane = pl.multiple_of(lax.div(i, 2) * 128, 128)
                top = acc_ref[pl.ds(row, 32), pl.ds(lane, 128)]
                low = acc_ref[pl.ds(row + 32, 32), pl.ds(lane, 128)]
                top = pltpu.roll(top, h * BLOCK, 1)
                low = pltpu.roll(low, (1 - h) * BLOCK, 1)
                out[s] = jnp.where(left, top, low).astype(BF16)
                return carry

            lax.fori_loop(0, CAP, pack, 0, unroll=2)


def wgrad(first, count, dests, lists, pt, xs):
    width = pt.shape[0]
    xblock = pl.BlockSpec((128, 512), lambda s, dest, lst: (0, dest[first + s]))
    return pl.pallas_call(
        functools.partial(wgrad_kernel, first),
        out_shape=[jax.ShapeDtypeStruct((CAP, 32, 128), BF16)] * count,
        grid_spec=pltpu.PrefetchScalarGridSpec(
            num_scalar_prefetch=2,
            grid=(count,),
            in_specs=[pl.BlockSpec((width, 512), lambda s, dest, lst: (0, 0))] + [xblock] * 4,
            out_specs=[pl.BlockSpec((CAP, 32, 128), lambda s, dest, lst: (0, 0, 0))] * count,
            scratch_shapes=[pltpu.VMEM((width, 512), F32)],
        ),
        compiler_params=params(1),
        cost_estimate=pl.CostEstimate(
            flops=2 * 512 * 512 * width * count,
            bytes_accessed=count * (512 * 1024 + CAP * 8192) + 1024 * width,
            transcendentals=0,
        ),
        name="wgrad",
    )(dests, lists, pt, *xs)


def unpack_kernel(own_ref, list_ref, count_ref, *refs):
    parts, out, buf = refs[:8], refs[8], refs[9]
    own = own_ref[0]
    buf[...] = jnp.zeros_like(buf)
    lanes = lax.broadcasted_iota(jnp.int32, (32, 128), 1)

    def place(s, carry):
        b = list_ref[own, s]
        i = lax.div(b, 14)
        j = b - i * 14
        h = lax.rem(i, 2)
        row = pl.multiple_of(j * BLOCK, BLOCK)
        lane = pl.multiple_of(lax.div(i, 2) * 128, 128)
        total = parts[0][s].astype(F32)
        for part in parts[1:]:
            total = total + part[s].astype(F32)
        here = lax.div(lanes, BLOCK) == h
        top = buf.at[pl.ds(row, 32), pl.ds(lane, 128)]
        low = buf.at[pl.ds(row + 32, 32), pl.ds(lane, 128)]
        top[...] = jnp.where(here, pltpu.roll(total, h * BLOCK, 1), top[...])
        low[...] = jnp.where(here, pltpu.roll(total, (1 - h) * BLOCK, 1), low[...])
        return carry

    lax.fori_loop(0, count_ref[own], place, 0)
    for c in range(4):
        out[c * 128 : (c + 1) * 128, :] = jnp.transpose(buf[:, c * 128 : (c + 1) * 128])


def unpack(own, lists, counts, parts, width):
    packed = pl.BlockSpec((CAP, 32, 128), lambda s, a, b, c: (0, 0, 0))
    return pl.pallas_call(
        unpack_kernel,
        out_shape=jax.ShapeDtypeStruct((512, width), F32),
        grid_spec=pltpu.PrefetchScalarGridSpec(
            num_scalar_prefetch=3,
            grid=(1,),
            in_specs=[packed] * 8,
            out_specs=pl.BlockSpec((512, width), lambda s, a, b, c: (0, 0)),
            scratch_shapes=[pltpu.VMEM((width, 512), F32)],
        ),
        compiler_params=params(1),
        cost_estimate=pl.CostEstimate(
            flops=8 * CAP * 4096, bytes_accessed=8 * CAP * 8192 + 2048 * width, transcendentals=0
        ),
        name="unpack",
    )(own, lists, counts, *parts)


def kept_lists(block_mask, t):
    mask = lax.dynamic_slice(block_mask, (0, t * 14), (64, 14)).reshape(8, 112)
    kept = mask != 0
    tri = jnp.arange(112)[:, None] <= jnp.arange(112)[None, :]
    rank = jnp.dot(kept.astype(BF16), tri.astype(BF16), preferred_element_type=F32)
    rank = rank.astype(jnp.int32)
    slot = jnp.arange(1, CAP + 1, dtype=jnp.int32)
    hit = kept[:, None, :] & (rank[:, None, :] == slot[None, :, None])
    at = jnp.arange(112, dtype=jnp.int32)
    lists = jnp.sum(jnp.where(hit, at[None, None, :], 0), axis=2, dtype=jnp.int32)
    return lists, rank[:, 111]


def body(tokens, weight, block_mask, act_grad):
    width = weight.shape[1]
    t = lax.axis_index("tensor").astype(jnp.int32)
    g = lax.axis_index("dp").astype(jnp.int32)
    z, xh, core = t // 4, (t // 2) % 2, t % 2
    xl, y = g // NY, g % NY

    own = [tokens] * NZ
    for k in (1, 7, 2, 6, 3, 5, 4):
        own[k] = lax.ppermute(tokens, "tensor", tensor_perm(k, 0, 0))
    across = [lax.ppermute(own[k], "tensor", tensor_perm(0, 1, 0)) for k in range(NZ)]
    x0 = jnp.concatenate(own, axis=0)
    x1 = jnp.concatenate(across, axis=0)
    x2 = lax.ppermute(x0, "tensor", tensor_perm(0, 0, 1))
    x3 = lax.ppermute(x1, "tensor", tensor_perm(0, 0, 1))
    xs = (x0, x1, x2, x3)

    masked = masked_weight((t * 14).reshape(1), weight, block_mask)
    lists, counts = kept_lists(block_mask, t)

    n = jnp.arange(32, dtype=jnp.int32)
    zk = (z - n % 8) % 8
    idx = (zk * 2 + (xh ^ (n // 8) % 2)) * 2 + (core ^ (n // 16))
    act, p, pt = forward(idx, xs, masked, act_grad.reshape(32, 16, width))

    other = xgrad(p, masked, None)
    received = lax.ppermute(other, "tensor", tensor_perm(0, 0, 1))

    order = [(1, 2), (1, 1), (1, 3), (0, 2), (1, 0), (0, 1), (0, 3), (0, 0)]
    dests = jnp.stack([(xl ^ a) * NY + (y + b) % NY for a, b in order])
    first = wgrad(0, 4, dests, lists, pt, xs)
    parts = [lax.ppermute(v, "dp", dp_perm(*o)) for v, o in zip(first, order[:4])]

    blocks = xgrad(p, masked, received)
    second = wgrad(4, 4, dests, lists, pt, xs)
    parts += [lax.ppermute(v, "dp", dp_perm(*o)) for v, o in zip(second[:3], order[4:7])]
    parts.append(second[3])

    total = blocks[0].astype(F32)
    for k in range(1, NZ):
        total = total + lax.ppermute(blocks[k], "tensor", tensor_perm(NZ - k, 0, 0)).astype(F32)
    last = lax.ppermute(total[16:].astype(BF16), "tensor", tensor_perm(0, 1, 0))
    x_grad = (total[:16].astype(BF16).astype(F32) + last.astype(F32)).astype(BF16)

    weight_grad = unpack(g.reshape(1), lists, counts, parts, width)
    return (act.reshape(512, width), x_grad, weight_grad)


def solution(mesh):
    return jax.shard_map(
        body,
        mesh=mesh,
        in_specs=(P(("dp", "tensor"), None), P(None, "tensor"), P(), P("dp", "tensor")),
        out_specs=(P("dp", "tensor"), P(("dp", "tensor"), None), P("dp", "tensor")),
        check_vma=False,
    )
```

```python
import functools

import jax
import jax.numpy as jnp
from jax import lax
from jax.experimental import pallas as pl
from jax.experimental.pallas import tpu as pltpu
from jax.sharding import PartitionSpec as P

BLOCK = 64
CAP = 70
NZ = 8
NY = 4
F32 = jnp.float32
BF16 = jnp.bfloat16


VMEM = pl.BlockSpec(memory_space=pltpu.VMEM)
SMEM = pl.BlockSpec(memory_space=pltpu.SMEM)


def tensor_perm(dz, dx, dc, split=False):
    pairs = []
    for z in range(NZ):
        for xh in range(2):
            for core in range(2):
                shift = -dz if split and core else dz
                source = (z * 2 + xh) * 2 + core
                target = (((z + shift) % NZ) * 2 + (xh ^ dx)) * 2 + (core ^ dc)
                pairs.append((source, target))
    return pairs


def dp_perm(dx, dy):
    return [
        (xl * NY + y, (xl ^ dx) * NY + (y + dy) % NY) for xl in range(2) for y in range(NY)
    ]


def move(x, dz=0, dx=0, dc=0):
    return lax.ppermute(x, "tensor", tensor_perm(dz, dx, dc, split=True))


def call(kernel, name, n_scalar, out_shape, args, flops, scratch=(), after=(), limit=12):
    n_args, n_after = len(args), len(after)

    def run(*refs):
        kernel(*refs[:n_args], *refs[n_args + n_after :])

    n_out = len(out_shape) if isinstance(out_shape, (tuple, list)) else 1
    out_specs = [VMEM] * n_out if isinstance(out_shape, (tuple, list)) else VMEM
    moved = sum(a.size * a.dtype.itemsize for a in args)
    return pl.pallas_call(
        run,
        out_shape=out_shape,
        in_specs=[SMEM] * n_scalar
        + [VMEM] * (n_args - n_scalar)
        + [pl.BlockSpec(memory_space=pl.ANY)] * n_after,
        out_specs=out_specs,
        scratch_shapes=list(scratch),
        compiler_params=pltpu.CompilerParams(vmem_limit_bytes=limit << 20),
        cost_estimate=pl.CostEstimate(flops=flops, bytes_accessed=moved, transcendentals=0),
        name=name,
    )(*args, *after)


def mask_kernel(t_ref, w_ref, m_ref, o_ref, e_ref):
    n_rows, blocks = m_ref.shape
    width = w_ref.shape[1]
    rows = lax.broadcasted_iota(jnp.int32, (blocks, width), 0)
    cols = lax.broadcasted_iota(jnp.int32, (blocks, width), 1)
    pick = (rows == t_ref[0] + lax.div(cols, BLOCK)).astype(BF16)
    e_ref[...] = jnp.dot(m_ref[...].astype(F32).astype(BF16), pick, preferred_element_type=F32)

    @pl.loop(0, n_rows // 8)
    def _(g):
        eight = e_ref[pl.ds(pl.multiple_of(g * 8, 8), 8), :]
        for i in range(8):
            at = pl.ds(pl.multiple_of(g * 512 + i * BLOCK, BLOCK), BLOCK)
            row = jnp.broadcast_to(eight[i : i + 1, :], (BLOCK, width)).astype(BF16)
            o_ref[at, :] = w_ref[at, :] * row


def forward_kernel(idx_ref, x0, x1, x2, x3, w_ref, g_ref, act_ref, p_ref, pt_ref, acc_ref):
    d = w_ref.shape[0]
    kb = 1024

    def product(s):
        cols = pl.ds(pl.multiple_of(s * kb, kb), kb)
        x = jnp.concatenate([x0[:, cols], x1[:, cols], x2[:, cols], x3[:, cols]], axis=0)
        return jnp.dot(x, w_ref[cols, :], preferred_element_type=F32)

    acc_ref[...] = product(0)

    @pl.loop(1, d // kb)
    def _(s):
        acc_ref[...] += product(s)

    @pl.loop(0, 32)
    def _(n):
        at = idx_ref[n]
        rows = pl.ds(pl.multiple_of(n * 16, 16), 16)
        pre = acc_ref[rows, :]
        s = jax.nn.sigmoid(pre)
        act_ref[at] = (pre * s).astype(BF16)
        grad = g_ref[at].astype(F32) * s * (1.0 + pre * (1.0 - s))
        acc_ref[rows, :] = grad
        p_ref[rows, :] = grad.astype(BF16)

    for c in range(7):
        cols = slice(c * 128, (c + 1) * 128)
        pt_ref[cols, :] = jnp.transpose(acc_ref[:, cols]).astype(BF16)


def xgrad_other_kernel(p_ref, w_ref, o_ref):
    @pl.loop(0, w_ref.shape[0] // 512)
    def _(s):
        cols = pl.ds(pl.multiple_of(s * 512, 512), 512)
        o_ref[:, cols] = lax.dot_general(
            p_ref[256:512, :],
            w_ref[cols, :],
            (((1,), (1,)), ((), ())),
            preferred_element_type=F32,
        ).astype(BF16)


def xgrad_own_kernel(p_ref, w_ref, r_ref, near1, near2, near3, far, home):
    @pl.loop(0, w_ref.shape[0] // 512)
    def _(s):
        cols = pl.ds(pl.multiple_of(s * 512, 512), 512)
        part = lax.dot_general(
            p_ref[0:256, :],
            w_ref[cols, :],
            (((1,), (1,)), ((), ())),
            preferred_element_type=F32,
        )
        total = (part + r_ref[:, cols].astype(F32)).astype(BF16)
        for q in range(2):
            base = q * 128
            home[q * 16 : q * 16 + 16, cols] = total[base : base + 16, :]
            far[q * 16 : q * 16 + 16, cols] = total[base + 16 : base + 32, :]
            for k, near in enumerate((near1, near2, near3)):
                first = base + 32 + k * 32
                near[q * 32 : q * 32 + 32, cols] = total[first : first + 32, :]


def sum_kernel(near1, near2, near3, far, home, to_core, kept):
    @pl.loop(0, home.shape[1] // 512)
    def _(s):
        cols = pl.ds(pl.multiple_of(s * 512, 512), 512)
        for q in range(2):
            own = slice(q * 32, q * 32 + 16)
            other = slice(q * 32 + 16, q * 32 + 32)
            rows = slice(q * 16, q * 16 + 16)
            total = home[rows, cols].astype(F32) + far[rows, cols].astype(F32)
            away = near1[other, cols].astype(F32) + near2[other, cols].astype(F32)
            for near in (near1, near2, near3):
                total = total + near[own, cols].astype(F32)
            to_core[rows, cols] = (away + near3[other, cols].astype(F32)).astype(BF16)
            kept[rows, cols] = total


def sum_core_kernel(kept, received, to_x, out):
    @pl.loop(0, kept.shape[1] // 512)
    def _(s):
        cols = pl.ds(pl.multiple_of(s * 512, 512), 512)
        total = kept[:, cols] + received[:, cols].astype(F32)
        out[:, cols] = total[0:16, :]
        to_x[:, cols] = total[16:32, :].astype(BF16)


def wgrad_kernel(first, dest_ref, row_ref, lane_ref, half_ref, pt_ref, x0, x1, x2, x3, *rest):
    outs, acc_ref, buf = rest[:-2], rest[-2], rest[-1]
    left = lax.broadcasted_iota(jnp.int32, (32, 128), 1) < BLOCK
    for n, out in enumerate(outs):
        dest = dest_ref[first + n]
        cols = pl.ds(pl.multiple_of(dest * 512, 512), 512)
        x = jnp.concatenate([x0[:, cols], x1[:, cols], x2[:, cols], x3[:, cols]], axis=0)
        acc_ref[...] = jnp.dot(pt_ref[...], x, preferred_element_type=F32)

        @pl.loop(0, 28)
        def _(i):
            rows = pl.ds(pl.multiple_of(i * 32, 32), 32)
            for c in range(4):
                lanes = slice(c * 128, (c + 1) * 128)
                value = acc_ref[rows, lanes]
                buf[0, rows, lanes] = value.astype(BF16)
                buf[1, rows, lanes] = pltpu.roll(value, BLOCK, 1).astype(BF16)

        def pack(s, carry):
            row = pl.multiple_of(row_ref[dest, s], BLOCK)
            lane = pl.multiple_of(lane_ref[dest, s], 128)
            h = half_ref[dest, s]
            top = buf[h, pl.ds(row, 32), pl.ds(lane, 128)]
            low = buf[1 - h, pl.ds(row + 32, 32), pl.ds(lane, 128)]
            out[s] = jnp.where(left, top, low)
            return carry

        lax.fori_loop(0, CAP, pack, 0, unroll=7)


def wgrad(first, count, scalars, pt, xs, after):
    width = pt.shape[0]
    return call(
        functools.partial(wgrad_kernel, first),
        "wgrad",
        4,
        [jax.ShapeDtypeStruct((CAP, 32, 128), BF16)] * count,
        (*scalars, pt, *xs),
        2 * 512 * 512 * width * count,
        scratch=(pltpu.VMEM((width, 512), F32), pltpu.VMEM((2, width, 512), BF16)),
        after=after,
    )


def unpack_kernel(own_ref, row_ref, lane_ref, half_ref, count_ref, *refs):
    parts, out, buf = refs[:8], refs[8], refs[9]
    own = own_ref[0]
    buf[...] = jnp.zeros_like(buf)
    left = lax.broadcasted_iota(jnp.int32, (32, 128), 1) < BLOCK

    def place(s, carry):
        row = pl.multiple_of(row_ref[own, s], BLOCK)
        lane = pl.multiple_of(lane_ref[own, s], 128)
        h = half_ref[own, s]
        total = parts[0][s].astype(F32)
        for part in parts[1:]:
            total = total + part[s].astype(F32)
        other = pltpu.roll(total, BLOCK, 1)
        top = buf.at[pl.ds(row, 32), pl.ds(lane, 128)]
        low = buf.at[pl.ds(row + 32, 32), pl.ds(lane, 128)]

        @pl.when(h == 0)
        def _():
            top[...] = jnp.where(left, total, top[...])
            low[...] = jnp.where(left, other, low[...])

        @pl.when(h == 1)
        def _():
            top[...] = jnp.where(left, top[...], other)
            low[...] = jnp.where(left, low[...], total)

        return carry

    lax.fori_loop(0, count_ref[own], place, 0)
    for c in range(4):
        out[c * 128 : (c + 1) * 128, :] = jnp.transpose(buf[:, c * 128 : (c + 1) * 128])


def kept_lists(block_mask, t):
    mask = lax.dynamic_slice(block_mask, (0, t * 14), (64, 14)).reshape(8, 112)
    kept = mask != 0
    tri = jnp.arange(112)[:, None] <= jnp.arange(112)[None, :]
    rank = jnp.dot(kept.astype(BF16), tri.astype(BF16), preferred_element_type=F32)
    rank = rank.astype(jnp.int32)
    slot = jnp.arange(1, CAP + 1, dtype=jnp.int32)
    hit = kept[:, None, :] & (rank[:, None, :] == slot[None, :, None])
    at = jnp.arange(112, dtype=jnp.int32)
    code = (at % 14) * BLOCK + (at // 28) * (128 << 10) + ((at // 14) % 2 << 20)
    code = jnp.sum(jnp.where(hit, code[None, None, :], 0), axis=2, dtype=jnp.int32)
    return code & 1023, (code >> 10) & 1023, code >> 20, rank[:, 111]


def body(tokens, weight, block_mask, act_grad):
    d, width = weight.shape
    t = lax.axis_index("tensor").astype(jnp.int32)
    g = lax.axis_index("dp").astype(jnp.int32)
    z, xh, core = t >> 2, (t >> 1) & 1, t & 1
    xl, y = g >> 2, g & 3

    partner = move(tokens, dc=1)
    home = move(tokens, dx=1)
    chip = jnp.concatenate([tokens, partner], axis=0)
    near = [move(chip, dz=k) for k in (1, 2, 3)]
    far = move(tokens, dz=4)

    masked = call(
        mask_kernel,
        "mask_weight",
        1,
        jax.ShapeDtypeStruct((d, width), BF16),
        ((t * 14).reshape(1), weight, block_mask),
        d * width,
        scratch=(pltpu.VMEM((64, width), F32),),
        after=(chip,),
    )
    row, lane, half, counts = kept_lists(block_mask, t)

    n = jnp.arange(32, dtype=jnp.int32)
    slot = n & 7
    dist = jnp.where(slot == 0, 0, jnp.where(slot == 1, 4, slot >> 1))
    flip = jnp.where(slot > 1, slot & 1, 0)
    gather_core = core ^ (n >> 4)
    zk = (z - (1 - 2 * gather_core) * dist) & (NZ - 1)
    idx = zk * 4 + (xh ^ ((n >> 3) & 1)) * 2 + (gather_core ^ flip)
    order = [(1, 2), (1, 1), (1, 3), (0, 2), (1, 0), (0, 1), (0, 3), (0, 0)]
    dx = jnp.array([o[0] for o in order], jnp.int32)
    dy = jnp.array([o[1] for o in order], jnp.int32)
    dests = (xl ^ dx) * NY + ((y + dy) & (NY - 1))

    near[0], masked, row, lane, half, counts, idx, dests = lax.optimization_barrier(
        (near[0], masked, row, lane, half, counts, idx, dests)
    )
    scalars = (dests, row, lane, half)

    near_x = [move(v, dx=1) for v in near]
    far_x = move(far, dx=1)
    x0 = jnp.concatenate([tokens, far, *near], axis=0)
    x1 = jnp.concatenate([home, far_x, *near_x], axis=0)
    xs = (x0, x1, move(x0, dc=1), move(x1, dc=1))

    act, p, pt = call(
        forward_kernel,
        "forward",
        1,
        (
            jax.ShapeDtypeStruct((32, 16, width), BF16),
            jax.ShapeDtypeStruct((512, width), BF16),
            jax.ShapeDtypeStruct((width, 512), BF16),
        ),
        (idx, *xs, masked, act_grad.reshape(32, 16, width)),
        2 * 512 * d * width,
        scratch=(pltpu.VMEM((512, width), F32),),
    )

    other = call(
        xgrad_other_kernel,
        "xgrad_other",
        0,
        jax.ShapeDtypeStruct((256, d), BF16),
        (p, masked),
        2 * 256 * d * width,
    )
    received = move(other, dc=1)
    packed = wgrad(0, 2, scalars, pt, xs, (other,))
    parts = [lax.ppermute(v, "dp", dp_perm(*o)) for v, o in zip(packed, order)]

    near1, near2, near3, far, home = call(
        xgrad_own_kernel,
        "xgrad_own",
        0,
        [jax.ShapeDtypeStruct((64, d), BF16)] * 3 + [jax.ShapeDtypeStruct((32, d), BF16)] * 2,
        (p, masked, received),
        2 * 256 * d * width,
        after=(packed[0],),
    )
    back = [move(v, dz=NZ - k) for k, v in ((3, near3), (2, near2), (1, near1))]
    back_far = move(far, dz=4)

    previous = near1
    for first in (2, 4, 6):
        packed = wgrad(first, 2, scalars, pt, xs, (previous,))
        previous = packed[0]
        for v, o in zip(packed, order[first : first + 2]):
            parts.append(v if o == (0, 0) else lax.ppermute(v, "dp", dp_perm(*o)))

    to_core, kept = call(
        sum_kernel,
        "sum_z",
        0,
        (jax.ShapeDtypeStruct((32, d), BF16), jax.ShapeDtypeStruct((32, d), F32)),
        (*back, back_far, home),
        6 * 64 * d,
    )
    to_x, kept = call(
        sum_core_kernel,
        "sum_core",
        0,
        (jax.ShapeDtypeStruct((16, d), BF16), jax.ShapeDtypeStruct((16, d), F32)),
        (kept, move(to_core, dc=1)),
        32 * d,
    )
    x_grad = (kept + move(to_x, dx=1).astype(F32)).astype(BF16)

    weight_grad = call(
        unpack_kernel,
        "unpack",
        5,
        jax.ShapeDtypeStruct((512, width), F32),
        (g.reshape(1), row, lane, half, counts, *parts),
        8 * CAP * 4096,
        scratch=(pltpu.VMEM((width, 512), F32),),
    )
    return (act.reshape(512, width), x_grad, weight_grad)


def solution(mesh):
    return jax.shard_map(
        body,
        mesh=mesh,
        in_specs=(P(("dp", "tensor"), None), P(None, "tensor"), P(), P("dp", "tensor")),
        out_specs=(P("dp", "tensor"), P(("dp", "tensor"), None), P("dp", "tensor")),
        check_vma=False,
    )
```

```python
import functools

import jax
import jax.numpy as jnp
from jax import lax
from jax.experimental import pallas as pl
from jax.experimental.pallas import tpu as pltpu
from jax.sharding import PartitionSpec as P


BLOCK = 64
CAP = 70
PAIRS = CAP // 2
NZ = 8
NY = 4
F32 = jnp.float32
BF16 = jnp.bfloat16


VMEM = pl.BlockSpec(memory_space=pltpu.VMEM)
SMEM = pl.BlockSpec(memory_space=pltpu.SMEM)


def tensor_perm(dz, dx, dc, split=False):
    pairs = []
    for z in range(NZ):
        for xh in range(2):
            for core in range(2):
                shift = -dz if split and core else dz
                source = (z * 2 + xh) * 2 + core
                target = (((z + shift) % NZ) * 2 + (xh ^ dx)) * 2 + (core ^ dc)
                pairs.append((source, target))
    return pairs


def dp_perm(dx, dy):
    return [
        (xl * NY + y, (xl ^ dx) * NY + (y + dy) % NY) for xl in range(2) for y in range(NY)
    ]


def move(x, dz=0, dx=0, dc=0):
    return lax.ppermute(x, "tensor", tensor_perm(dz, dx, dc, split=True))


def move_dp(x, dx, dy):
    return lax.ppermute(x, "dp", dp_perm(dx, dy))


def call(kernel, n_scalar, out_shape, args, flops, scratch=(), after=(), limit=12):
    n_args, n_after = len(args), len(after)

    def run(*refs):
        kernel(*refs[:n_args], *refs[n_args + n_after :])

    n_out = len(out_shape) if isinstance(out_shape, (tuple, list)) else 1
    out_specs = [VMEM] * n_out if isinstance(out_shape, (tuple, list)) else VMEM
    moved = sum(a.size * a.dtype.itemsize for a in args)
    return pl.pallas_call(
        run,
        out_shape=out_shape,
        in_specs=[SMEM] * n_scalar
        + [VMEM] * (n_args - n_scalar)
        + [pl.BlockSpec(memory_space=pl.ANY)] * n_after,
        out_specs=out_specs,
        scratch_shapes=list(scratch),
        compiler_params=pltpu.CompilerParams(vmem_limit_bytes=limit << 20),
        cost_estimate=pl.CostEstimate(flops=flops, bytes_accessed=moved, transcendentals=0),
    )(*args, *after)


def tick_kernel(x_ref, o_ref):
    o_ref[...] = jnp.full(o_ref.shape, x_ref[0], F32)


def mask_kernel(t_ref, w_ref, m_ref, o_ref, e_ref):
    n_rows, blocks = m_ref.shape
    width = w_ref.shape[1]
    rows = lax.broadcasted_iota(jnp.int32, (blocks, width), 0)
    cols = lax.broadcasted_iota(jnp.int32, (blocks, width), 1)
    pick = (rows == t_ref[0] + lax.div(cols, BLOCK)).astype(BF16)
    e_ref[...] = jnp.dot(m_ref[...].astype(F32).astype(BF16), pick, preferred_element_type=F32)

    @pl.loop(0, n_rows // 8)
    def _(g):
        eight = e_ref[pl.ds(pl.multiple_of(g * 8, 8), 8), :]
        for i in range(8):
            at = pl.ds(pl.multiple_of(g * 512 + i * BLOCK, BLOCK), BLOCK)
            row = jnp.broadcast_to(eight[i : i + 1, :], (BLOCK, width)).astype(BF16)
            o_ref[at, :] = w_ref[at, :] * row


def forward_kernel(first, count, idx_ref, xa, xb, w_ref, g_ref, *rest):
    act_ref, p_ref, pt_ref, acc_ref = rest[-4:]
    d = w_ref.shape[0]
    kb = 1024

    def product(s):
        cols = pl.ds(pl.multiple_of(s * kb, kb), kb)
        x = jnp.concatenate([xa[:, cols], xb[:, cols]], axis=0)
        return jnp.dot(x, w_ref[cols, :], preferred_element_type=F32)

    acc_ref[...] = product(0)

    @pl.loop(1, d // kb)
    def _(s):
        acc_ref[...] += product(s)

    @pl.loop(0, count)
    def _(n):
        at = idx_ref[first + n]
        rows = pl.ds(pl.multiple_of(n * 16, 16), 16)
        pre = acc_ref[rows, :]
        s = jax.nn.sigmoid(pre)
        act = (pre * s).astype(BF16)
        if first:
            act_ref[at] = act
            act_ref[idx_ref[n]] = rest[0][n]
        else:
            act_ref[n] = act
        grad = g_ref[at].astype(F32) * s * (1.0 + pre * (1.0 - s))
        acc_ref[rows, :] = grad
        p_ref[rows, :] = grad.astype(BF16)

    for c in range(7):
        cols = slice(c * 128, (c + 1) * 128)
        pt_ref[cols, :] = jnp.transpose(acc_ref[:, cols]).astype(BF16)


def forward(first, idx, xa, xb, masked, act_grad, acts=(), after=()):
    d, width = masked.shape
    blocks = 32 if first else 16
    return call(
        functools.partial(forward_kernel, first, 16),
        1,
        (
            jax.ShapeDtypeStruct((blocks, 16, width), BF16),
            jax.ShapeDtypeStruct((256, width), BF16),
            jax.ShapeDtypeStruct((width, 256), BF16),
        ),
        (idx, xa, xb, masked, act_grad, *acts),
        2 * 256 * d * width,
        scratch=(pltpu.VMEM((256, width), F32),),
        after=after,
    )


def xgrad_kernel(p_ref, w_ref, own_ref, other_ref):
    @pl.loop(0, w_ref.shape[0] // 512)
    def _(s):
        cols = pl.ds(pl.multiple_of(s * 512, 512), 512)
        part = lax.dot_general(
            p_ref[...], w_ref[cols, :], (((1,), (1,)), ((), ())), preferred_element_type=F32
        )
        own_ref[:, cols] = part[:128, :]
        other_ref[:, cols] = part[128:, :].astype(BF16)


def xgrad(p, masked, after=()):
    d, width = masked.shape
    return call(
        xgrad_kernel,
        0,
        (jax.ShapeDtypeStruct((128, d), F32), jax.ShapeDtypeStruct((128, d), BF16)),
        (p, masked),
        2 * 256 * d * width,
        after=after,
    )


def mix_kernel(own_ref, r_ref, near1, near2, near3, far, home):
    @pl.loop(0, own_ref.shape[1] // 512)
    def _(s):
        cols = pl.ds(pl.multiple_of(s * 512, 512), 512)
        total = (own_ref[:, cols] + r_ref[:, cols].astype(F32)).astype(BF16)
        home[:, cols] = total[0:16, :]
        far[:, cols] = total[16:32, :]
        near1[:, cols] = total[32:64, :]
        near2[:, cols] = total[64:96, :]
        near3[:, cols] = total[96:128, :]


def send_back(own, other, after):
    d = own.shape[1]
    near1, near2, near3, far, home = call(
        mix_kernel,
        0,
        [jax.ShapeDtypeStruct((32, d), BF16)] * 3 + [jax.ShapeDtypeStruct((16, d), BF16)] * 2,
        (own, move(other, dc=1)),
        128 * d,
        after=after,
    )
    back = []
    for k, v in ((3, near3), (2, near2), (1, near1), (4, far)):
        back.append(move(v, dz=NZ - k))
    return near1, [*back, home]


def sum_kernel(*refs):
    halves, to_core, kept = (refs[0:5], refs[5:10]), refs[10], refs[11]

    @pl.loop(0, kept.shape[1] // 512)
    def _(s):
        cols = pl.ds(pl.multiple_of(s * 512, 512), 512)
        for q, (*nears, far, home) in enumerate(halves):
            rows = slice(q * 16, q * 16 + 16)
            total = home[:, cols].astype(F32) + far[:, cols].astype(F32)
            away = jnp.zeros_like(total)
            for near in nears:
                total = total + near[0:16, cols].astype(F32)
                away = away + near[16:32, cols].astype(F32)
            to_core[rows, cols] = away.astype(BF16)
            kept[rows, cols] = total


def sum_core_kernel(kept, received, to_x, out):
    @pl.loop(0, kept.shape[1] // 512)
    def _(s):
        cols = pl.ds(pl.multiple_of(s * 512, 512), 512)
        total = kept[:, cols] + received[:, cols].astype(F32)
        out[:, cols] = total[0:16, :]
        to_x[:, cols] = total[16:32, :].astype(BF16)


def place_of(code):
    return (
        pl.multiple_of(code & 1023, BLOCK),
        pl.multiple_of((code >> 10) & 1023, 128),
        code >> 20,
    )


def wgrad_kernel(first, dest_ref, code_ref, odd_ref, pa, pb, x0, x1, x2, x3, *rest):
    outs, acc_ref = rest[:-1], rest[-1]
    last = acc_ref.shape[0] - BLOCK
    left = lax.broadcasted_iota(jnp.int32, (BLOCK, 128), 1) < BLOCK
    for n, out in enumerate(outs):
        dest = dest_ref[first + n]
        cols = pl.ds(pl.multiple_of(dest * 512, 512), 512)
        xa = jnp.concatenate([x0[:, cols], x2[:, cols]], axis=0)
        xb = jnp.concatenate([x1[:, cols], x3[:, cols]], axis=0)
        acc_ref[...] = jnp.dot(pa[...], xa, preferred_element_type=F32) + jnp.dot(
            pb[...], xb, preferred_element_type=F32
        )

        def tiles(s):
            row, lane, h = place_of(code_ref[dest, s])
            row = pl.multiple_of(jnp.minimum(row, last), BLOCK)
            row2, lane2, h2 = place_of(code_ref[dest, PAIRS + s])
            row2 = pl.multiple_of(jnp.minimum(row2, last), BLOCK)
            return (
                acc_ref[pl.ds(row, BLOCK), pl.ds(lane, 128)],
                acc_ref[pl.ds(row2, BLOCK), pl.ds(lane2, 128)],
                h,
                h2,
            )

        def pack(s, carry):
            one, two, _, _ = tiles(s)
            out[s] = jnp.where(left, one, two).astype(BF16)
            return carry

        def repack(n, carry):
            s = PAIRS - 1 - n
            one, two, h, h2 = tiles(s)
            one = pltpu.roll(one, h * BLOCK, 1)
            two = pltpu.roll(two, (1 - h2) * BLOCK, 1)
            out[s] = jnp.where(left, one, two).astype(BF16)
            return carry

        lax.fori_loop(0, PAIRS, pack, 0, unroll=5)
        lax.fori_loop(0, odd_ref[dest], repack, 0)


def wgrad(first, count, scalars, pa, pb, xs, after):
    width = pa.shape[0]
    return call(
        functools.partial(wgrad_kernel, first),
        3,
        [jax.ShapeDtypeStruct((PAIRS, BLOCK, 128), BF16)] * count,
        (*scalars, pa, pb, *xs),
        2 * 512 * 512 * width * count,
        scratch=(pltpu.VMEM((width, 512), F32),),
        after=after,
    )


def unpack_kernel(own_ref, code_ref, *refs):
    parts, out, buf = refs[:8], refs[8], refs[9]
    own = own_ref[0]
    width = out.shape[1]
    buf[...] = jnp.zeros_like(buf)
    half = lax.broadcasted_iota(jnp.int32, (BLOCK, 128), 1) // BLOCK

    def place(s, carry):
        total = parts[0][s].astype(F32)
        for part in parts[1:]:
            total = total + part[s].astype(F32)
        row, lane, h = place_of(code_ref[own, s])
        at = buf.at[pl.ds(row, BLOCK), pl.ds(lane, 128)]
        at[...] = jnp.where(half == h, pltpu.roll(total, h * BLOCK, 1), at[...])
        row, lane, h = place_of(code_ref[own, PAIRS + s])
        at = buf.at[pl.ds(row, BLOCK), pl.ds(lane, 128)]
        at[...] = jnp.where(half == h, pltpu.roll(total, (1 - h) * BLOCK, 1), at[...])
        return carry

    lax.fori_loop(0, PAIRS, place, 0)
    for c in range(4):
        lanes = slice(c * 128, (c + 1) * 128)
        out[lanes, :] = jnp.transpose(buf[0:width, lanes])


def kept_codes(block_mask, t, width):
    mask = lax.dynamic_slice(block_mask, (0, t * 14), (64, 14)).reshape(8, 112)
    kept = mask != 0
    at = jnp.arange(112, dtype=jnp.int32)
    i = jnp.array([b // 14 for b in range(112)], jnp.int32)
    j = at - i * 14
    h = i & 1
    before = (at[:, None] <= at[None, :]) & (h[:, None] == h[None, :])
    rank = jnp.dot(kept.astype(BF16), before.astype(BF16), preferred_element_type=F32)
    rank = rank.astype(jnp.int32) - 1
    extra = rank >= PAIRS
    slot = jnp.where(extra, 3 * PAIRS - 1 - PAIRS * h - rank, rank + PAIRS * h)
    hit = kept[:, None, :] & (slot[:, None, :] == jnp.arange(CAP, dtype=jnp.int32)[None, :, None])
    code = j * BLOCK + (i >> 1) * (128 << 10) + (h << 20) - width
    code = jnp.sum(jnp.where(hit, code[None, None, :], 0), axis=2, dtype=jnp.int32) + width
    odd = jnp.sum((kept & extra).astype(jnp.int32), axis=1, dtype=jnp.int32)
    return code, odd


def layer(tokens, weight, block_mask, act_grad):
    d, width = weight.shape
    t = lax.axis_index("tensor").astype(jnp.int32)
    g = lax.axis_index("dp").astype(jnp.int32)
    z, xh, core = t >> 2, (t >> 1) & 1, t & 1
    xl, y = g >> 2, g & 3

    partner = move(tokens, dc=1)
    home = move(tokens, dx=1)
    chip = jnp.concatenate([tokens, partner], axis=0)
    t, chip = lax.optimization_barrier((t, chip))
    near = [move(chip, dz=k) for k in (1, 2, 3)]
    far = move(chip[:16], dz=4)

    masked = call(
        mask_kernel,
        1,
        jax.ShapeDtypeStruct((d, width), BF16),
        ((t * 14).reshape(1), weight, block_mask),
        d * width,
        scratch=(pltpu.VMEM((64, width), F32),),
    )
    code, odd = kept_codes(block_mask, t, width)

    n = jnp.arange(32, dtype=jnp.int32)
    slot = n & 7
    dist = jnp.where(slot == 0, 0, jnp.where(slot == 1, 4, slot >> 1))
    flip = jnp.where(slot > 1, slot & 1, 0)
    gather_core = core ^ ((n >> 3) & 1)
    zk = (z - (1 - 2 * gather_core) * dist) & (NZ - 1)
    idx = zk * 4 + (xh ^ (n >> 4)) * 2 + (gather_core ^ flip)
    order = [(1, 2), (0, 2), (1, 1), (0, 3), (1, 3), (0, 1), (1, 0), (0, 0)]
    dx = jnp.array([o[0] for o in order], jnp.int32)
    dy = jnp.array([o[1] for o in order], jnp.int32)
    dests = (xl ^ dx) * NY + ((y + dy) & (NY - 1))

    near[0], masked, code, odd, idx, dests = lax.optimization_barrier(
        (near[0], masked, code, odd, idx, dests)
    )
    scalars = (dests, code, odd)

    tick = call(tick_kernel, 1, jax.ShapeDtypeStruct((8, 128), F32), (dests,), 0)
    near_x = [move(near[k], dx=1) for k in range(3)]
    far_x = move(far, dx=1)
    x0 = jnp.concatenate([tokens, far, *near], axis=0)
    x2 = move(x0, dc=1)
    x1 = jnp.concatenate([home, far_x, *near_x], axis=0)
    x3 = move(x1, dc=1)
    xs = (x0, x1, x2, x3)

    grads = act_grad.reshape(32, 16, width)
    act, p, pa = forward(0, idx, x0, x2, masked, grads, after=(tick,))
    own_a, other_a = xgrad(p, masked)
    act, p, pb = forward(16, idx, x1, x3, masked, grads, (act,), (other_a,))

    parts = []

    def pack_two(first, after):
        packed = wgrad(first, 2, scalars, pa, pb, xs, after)
        for v, o in zip(packed, order[first : first + 2]):
            parts.append(v if o == (0, 0) else move_dp(v, *o))
        return (packed[0],)

    done = pack_two(0, ())
    done, back_a = send_back(own_a, other_a, done)
    done = pack_two(2, (done,))
    own_b, other_b = xgrad(p, masked, done)
    done = pack_two(4, (other_b,))
    done, back_b = send_back(own_b, other_b, done)
    pack_two(6, (done,))

    to_core, kept = call(
        sum_kernel,
        0,
        (jax.ShapeDtypeStruct((32, d), BF16), jax.ShapeDtypeStruct((32, d), F32)),
        (*back_a, *back_b),
        10 * 32 * d,
    )
    to_x, kept = call(
        sum_core_kernel,
        0,
        (jax.ShapeDtypeStruct((16, d), BF16), jax.ShapeDtypeStruct((16, d), F32)),
        (kept, move(to_core, dc=1)),
        32 * d,
    )
    x_grad = (kept + move(to_x, dx=1).astype(F32)).astype(BF16)

    weight_grad = call(
        unpack_kernel,
        2,
        jax.ShapeDtypeStruct((512, width), F32),
        (g.reshape(1), code, *parts),
        8 * CAP * 4096,
        scratch=(pltpu.VMEM((width + BLOCK, 512), F32),),
    )
    return (act.reshape(512, width), x_grad, weight_grad)


def solution(mesh):
    return jax.shard_map(
        layer,
        mesh=mesh,
        in_specs=(P(("dp", "tensor"), None), P(None, "tensor"), P(), P("dp", "tensor")),
        out_specs=(P("dp", "tensor"), P(("dp", "tensor"), None), P("dp", "tensor")),
        check_vma=False,
    )
```

```python
import functools

import jax
import jax.numpy as jnp
from jax import lax
from jax.experimental import pallas as pl
from jax.experimental.pallas import tpu as pltpu
from jax.sharding import PartitionSpec as P


BLOCK = 64
CAP = 70
PAIRS = CAP // 2
NZ = 8
NY = 4
F32 = jnp.float32
BF16 = jnp.bfloat16


VMEM = pl.BlockSpec(memory_space=pltpu.VMEM)
SMEM = pl.BlockSpec(memory_space=pltpu.SMEM)


def tensor_perm(dz, dx, dc, split=False):
    pairs = []
    for z in range(NZ):
        for xh in range(2):
            for core in range(2):
                shift = -dz if split and core else dz
                source = (z * 2 + xh) * 2 + core
                target = (((z + shift) % NZ) * 2 + (xh ^ dx)) * 2 + (core ^ dc)
                pairs.append((source, target))
    return pairs


def dp_perm(dx, dy):
    return [
        (xl * NY + y, (xl ^ dx) * NY + (y + dy) % NY) for xl in range(2) for y in range(NY)
    ]


def move(x, dz=0, dx=0, dc=0):
    return lax.ppermute(x, "tensor", tensor_perm(dz, dx, dc, split=True))


def move_dp(x, dx, dy):
    return lax.ppermute(x, "dp", dp_perm(dx, dy))


def call(kernel, n_scalar, out_shape, args, flops, scratch=(), after=(), limit=12, out_space=VMEM):
    n_args, n_after = len(args), len(after)

    def run(*refs):
        kernel(*refs[:n_args], *refs[n_args + n_after :])

    n_out = len(out_shape) if isinstance(out_shape, (tuple, list)) else 1
    out_specs = [VMEM] * n_out if isinstance(out_shape, (tuple, list)) else out_space
    moved = sum(a.size * a.dtype.itemsize for a in args)
    return pl.pallas_call(
        run,
        out_shape=out_shape,
        in_specs=[SMEM] * n_scalar
        + [VMEM] * (n_args - n_scalar)
        + [pl.BlockSpec(memory_space=pl.ANY)] * n_after,
        out_specs=out_specs,
        scratch_shapes=list(scratch),
        compiler_params=pltpu.CompilerParams(vmem_limit_bytes=limit << 20),
        cost_estimate=pl.CostEstimate(flops=flops, bytes_accessed=moved, transcendentals=0),
    )(*args, *after)


def tick_kernel(o_ref):
    o_ref[...] = jnp.zeros_like(o_ref)


def join_kernel(a_ref, b_ref, o_ref):
    o_ref[0:16, :] = a_ref[...]
    o_ref[16:32, :] = b_ref[...]


def mask_kernel(t_ref, w_ref, m_ref, o_ref, e_ref):
    n_rows, blocks = m_ref.shape
    width = w_ref.shape[1]
    rows = lax.broadcasted_iota(jnp.int32, (blocks, width), 0)
    cols = lax.broadcasted_iota(jnp.int32, (blocks, width), 1)
    pick = (rows == t_ref[0] + lax.div(cols, BLOCK)).astype(BF16)
    e_ref[...] = jnp.dot(m_ref[...].astype(F32).astype(BF16), pick, preferred_element_type=F32)

    @pl.loop(0, n_rows // 8)
    def _(g):
        eight = e_ref[pl.ds(pl.multiple_of(g * 8, 8), 8), :]
        for i in range(8):
            at = pl.ds(pl.multiple_of(g * 512 + i * BLOCK, BLOCK), BLOCK)
            row = jnp.broadcast_to(eight[i : i + 1, :], (BLOCK, width)).astype(BF16)
            o_ref[at, :] = w_ref[at, :] * row


def forward_kernel(first, count, idx_ref, xa, xb, w_ref, g_ref, *rest):
    act_ref, p_ref, pt_ref, acc_ref = rest[-4:]
    d = w_ref.shape[0]
    kb = 1024

    def product(s):
        cols = pl.ds(pl.multiple_of(s * kb, kb), kb)
        x = jnp.concatenate([xa[:, cols], xb[:, cols]], axis=0)
        return jnp.dot(x, w_ref[cols, :], preferred_element_type=F32)

    acc_ref[...] = product(0)

    @pl.loop(1, d // kb)
    def _(s):
        acc_ref[...] += product(s)

    @pl.loop(0, count)
    def _(n):
        at = idx_ref[first + n]
        rows = pl.ds(pl.multiple_of(n * 16, 16), 16)
        pre = acc_ref[rows, :]
        s = jax.nn.sigmoid(pre)
        act = (pre * s).astype(BF16)
        if first:
            act_ref[at] = act
            act_ref[idx_ref[n]] = rest[0][n]
        else:
            act_ref[n] = act
        grad = g_ref[at].astype(F32) * s * (1.0 + pre * (1.0 - s))
        acc_ref[rows, :] = grad
        p_ref[rows, :] = grad.astype(BF16)

    for c in range(7):
        cols = slice(c * 128, (c + 1) * 128)
        pt_ref[cols, :] = jnp.transpose(acc_ref[:, cols]).astype(BF16)


def forward(first, idx, xa, xb, masked, act_grad, acts=(), after=()):
    d, width = masked.shape
    blocks = 32 if first else 16
    return call(
        functools.partial(forward_kernel, first, 16),
        1,
        (
            jax.ShapeDtypeStruct((blocks, 16, width), BF16),
            jax.ShapeDtypeStruct((256, width), BF16),
            jax.ShapeDtypeStruct((width, 256), BF16),
        ),
        (idx, xa, xb, masked, act_grad, *acts),
        2 * 256 * d * width,
        scratch=(pltpu.VMEM((256, width), F32),),
        after=after,
    )


def xgrad_kernel(p_ref, w_ref, own_ref, other_ref):
    @pl.loop(0, w_ref.shape[0] // 512)
    def _(s):
        cols = pl.ds(pl.multiple_of(s * 512, 512), 512)
        part = lax.dot_general(
            p_ref[...], w_ref[cols, :], (((1,), (1,)), ((), ())), preferred_element_type=F32
        )
        own_ref[:, cols] = part[:128, :]
        other_ref[:, cols] = part[128:, :].astype(BF16)


def xgrad(p, masked, after=()):
    d, width = masked.shape
    return call(
        xgrad_kernel,
        0,
        (jax.ShapeDtypeStruct((128, d), F32), jax.ShapeDtypeStruct((128, d), BF16)),
        (p, masked),
        2 * 256 * d * width,
        after=after,
    )


def mix_kernel(own_ref, r_ref, near1, near2, near3, far, home):
    @pl.loop(0, own_ref.shape[1] // 512)
    def _(s):
        cols = pl.ds(pl.multiple_of(s * 512, 512), 512)
        total = (own_ref[:, cols] + r_ref[:, cols].astype(F32)).astype(BF16)
        home[:, cols] = total[0:16, :]
        far[:, cols] = total[16:32, :]
        near1[:, cols] = total[32:64, :]
        near2[:, cols] = total[64:96, :]
        near3[:, cols] = total[96:128, :]


def send_back(own, other, after):
    d = own.shape[1]
    near1, near2, near3, far, home = call(
        mix_kernel,
        0,
        [jax.ShapeDtypeStruct((32, d), BF16)] * 3 + [jax.ShapeDtypeStruct((16, d), BF16)] * 2,
        (own, move(other, dc=1)),
        128 * d,
        after=after,
    )
    back = []
    for k, v in ((3, near3), (2, near2), (1, near1), (4, far)):
        back.append(move(v, dz=NZ - k))
    return near1, [*back, home]


def sum_kernel(*refs):
    halves, to_core, kept = (refs[0:5], refs[5:10]), refs[10], refs[11]

    @pl.loop(0, kept.shape[1] // 512)
    def _(s):
        cols = pl.ds(pl.multiple_of(s * 512, 512), 512)
        for q, (*nears, far, home) in enumerate(halves):
            rows = slice(q * 16, q * 16 + 16)
            total = home[:, cols].astype(F32) + far[:, cols].astype(F32)
            away = jnp.zeros_like(total)
            for near in nears:
                total = total + near[0:16, cols].astype(F32)
                away = away + near[16:32, cols].astype(F32)
            to_core[rows, cols] = away.astype(BF16)
            kept[rows, cols] = total


def sum_core_kernel(kept, received, to_x, out):
    @pl.loop(0, kept.shape[1] // 512)
    def _(s):
        cols = pl.ds(pl.multiple_of(s * 512, 512), 512)
        total = kept[:, cols] + received[:, cols].astype(F32)
        out[:, cols] = total[0:16, :]
        to_x[:, cols] = total[16:32, :].astype(BF16)


def place_of(code):
    return (
        pl.multiple_of(code & 1023, BLOCK),
        pl.multiple_of((code >> 10) & 1023, 128),
        code >> 20,
    )


def wgrad_kernel(first, dest_ref, code_ref, odd_ref, pa, pb, x0, x1, x2, x3, *rest):
    outs, acc_ref = rest[:-1], rest[-1]
    last = acc_ref.shape[0] - BLOCK
    left = lax.broadcasted_iota(jnp.int32, (BLOCK, 128), 1) < BLOCK
    for n, out in enumerate(outs):
        dest = dest_ref[first + n]
        cols = pl.ds(pl.multiple_of(dest * 512, 512), 512)
        xa = jnp.concatenate([x0[:, cols], x2[:, cols]], axis=0)
        xb = jnp.concatenate([x1[:, cols], x3[:, cols]], axis=0)
        acc_ref[...] = jnp.dot(pa[...], xa, preferred_element_type=F32) + jnp.dot(
            pb[...], xb, preferred_element_type=F32
        )

        def tiles(s):
            row, lane, h = place_of(code_ref[dest, s])
            row = pl.multiple_of(jnp.minimum(row, last), BLOCK)
            row2, lane2, h2 = place_of(code_ref[dest, PAIRS + s])
            row2 = pl.multiple_of(jnp.minimum(row2, last), BLOCK)
            return (
                acc_ref[pl.ds(row, BLOCK), pl.ds(lane, 128)],
                acc_ref[pl.ds(row2, BLOCK), pl.ds(lane2, 128)],
                h,
                h2,
            )

        def pack(s, carry):
            one, two, _, _ = tiles(s)
            out[s] = jnp.where(left, one, two).astype(BF16)
            return carry

        def repack(n, carry):
            s = PAIRS - 1 - n
            one, two, h, h2 = tiles(s)
            one = pltpu.roll(one, h * BLOCK, 1)
            two = pltpu.roll(two, (1 - h2) * BLOCK, 1)
            out[s] = jnp.where(left, one, two).astype(BF16)
            return carry

        lax.fori_loop(0, PAIRS, pack, 0, unroll=5)
        lax.fori_loop(0, odd_ref[dest], repack, 0)


def wgrad(first, count, scalars, pa, pb, xs, after):
    width = pa.shape[0]
    return call(
        functools.partial(wgrad_kernel, first),
        3,
        [jax.ShapeDtypeStruct((PAIRS, BLOCK, 128), BF16)] * count,
        (*scalars, pa, pb, *xs),
        2 * 512 * 512 * width * count,
        scratch=(pltpu.VMEM((width, 512), F32),),
        after=after,
    )


def presum_kernel(*refs):
    parts, out = refs[:-1], refs[-1]

    @pl.loop(0, PAIRS)
    def _(s):
        total = parts[0][s].astype(F32)
        for part in parts[1:]:
            total = total + part[s].astype(F32)
        out[s] = total


def unpack_kernel(own_ref, code_ref, *refs):
    parts, (out, buf, turned, sems) = refs[:-4], refs[-4:]
    own = own_ref[0]
    width = turned.shape[1]
    buf[...] = jnp.zeros_like(buf)
    half = lax.broadcasted_iota(jnp.int32, (BLOCK, 128), 1) // BLOCK

    def place(s, carry):
        total = parts[0][s]
        for part in parts[1:]:
            total = total + part[s].astype(F32)
        row, lane, h = place_of(code_ref[own, s])
        at = buf.at[pl.ds(row, BLOCK), pl.ds(lane, 128)]
        at[...] = jnp.where(half == h, pltpu.roll(total, h * BLOCK, 1), at[...])
        row, lane, h = place_of(code_ref[own, PAIRS + s])
        at = buf.at[pl.ds(row, BLOCK), pl.ds(lane, 128)]
        at[...] = jnp.where(half == h, pltpu.roll(total, (1 - h) * BLOCK, 1), at[...])
        return carry

    lax.fori_loop(0, PAIRS, place, 0)
    copies = []
    for c in range(4):
        lanes = slice(c * 128, (c + 1) * 128)
        turned[lanes, :] = jnp.transpose(buf[0:width, lanes])
        copies.append(pltpu.make_async_copy(turned.at[lanes], out.at[lanes], sems.at[c]))
        copies[-1].start()
    for copy in copies:
        copy.wait()


def kept_codes(block_mask, t, width):
    mask = lax.dynamic_slice(block_mask, (0, t * 14), (64, 14)).reshape(8, 112)
    kept = mask != 0
    at = jnp.arange(112, dtype=jnp.int32)
    i = jnp.array([b // 14 for b in range(112)], jnp.int32)
    j = at - i * 14
    h = i & 1
    before = (at[:, None] <= at[None, :]) & (h[:, None] == h[None, :])
    rank = jnp.dot(kept.astype(BF16), before.astype(BF16), preferred_element_type=F32)
    rank = rank.astype(jnp.int32) - 1
    extra = rank >= PAIRS
    slot = jnp.where(extra, 3 * PAIRS - 1 - PAIRS * h - rank, rank + PAIRS * h)
    hit = kept[:, None, :] & (slot[:, None, :] == jnp.arange(CAP, dtype=jnp.int32)[None, :, None])
    code = j * BLOCK + (i >> 1) * (128 << 10) + (h << 20) - width
    code = jnp.sum(jnp.where(hit, code[None, None, :], 0), axis=2, dtype=jnp.int32) + width
    odd = jnp.sum((kept & extra).astype(jnp.int32), axis=1, dtype=jnp.int32)
    return code, odd


def layer(tokens, weight, block_mask, act_grad):
    d, width = weight.shape
    t = lax.axis_index("tensor").astype(jnp.int32)
    g = lax.axis_index("dp").astype(jnp.int32)

    partner = move(tokens, dc=1)
    home = move(tokens, dx=1)
    chip = call(join_kernel, 0, jax.ShapeDtypeStruct((32, d), BF16), (tokens, partner), 0)
    t, g, chip = lax.optimization_barrier((t, g, chip))
    z, xh, core = t >> 2, (t >> 1) & 1, t & 1
    xl, y = g >> 2, g & 3
    near = [move(chip, dz=k) for k in (1, 2, 3)]
    far = move(chip[:16], dz=4)

    n = jnp.arange(32, dtype=jnp.int32)
    slot = n & 7
    dist = jnp.where(slot == 0, 0, jnp.where(slot == 1, 4, slot >> 1))
    flip = jnp.where(slot > 1, slot & 1, 0)
    gather_core = core ^ ((n >> 3) & 1)
    zk = (z - (1 - 2 * gather_core) * dist) & (NZ - 1)
    idx = zk * 4 + (xh ^ (n >> 4)) * 2 + (gather_core ^ flip)
    order = [(1, 2), (0, 2), (1, 1), (0, 3), (1, 3), (0, 1), (1, 0), (0, 0)]
    dx = jnp.array([o[0] for o in order], jnp.int32)
    dy = jnp.array([o[1] for o in order], jnp.int32)
    dests = (xl ^ dx) * NY + ((y + dy) & (NY - 1))

    ticks = [call(tick_kernel, 0, jax.ShapeDtypeStruct((8, 128), F32), (), 0) for _ in range(3)]
    t_mask, ticks[2] = lax.optimization_barrier((t, ticks[2]))
    t_list, ticks[1] = lax.optimization_barrier((t, ticks[1]))
    masked = call(
        mask_kernel,
        1,
        jax.ShapeDtypeStruct((d, width), BF16),
        ((t_mask * 14).reshape(1), weight, block_mask),
        d * width,
        scratch=(pltpu.VMEM((64, width), F32),),
    )
    code, odd = kept_codes(block_mask, t_list, width)
    near[2], masked, code, odd, idx, dests = lax.optimization_barrier(
        (near[2], masked, code, odd, idx, dests)
    )
    scalars = (dests, code, odd)

    near_x = [move(near[k], dx=1) for k in range(3)]
    far_x = move(far, dx=1)
    x0 = jnp.concatenate([tokens, far, *near], axis=0)
    x2 = move(x0, dc=1)
    x1 = jnp.concatenate([home, far_x, *near_x], axis=0)
    x3 = move(x1, dc=1)
    xs = (x0, x1, x2, x3)

    grads = act_grad.reshape(32, 16, width)
    act, p, pa = forward(0, idx, x0, x2, masked, grads, after=ticks)
    own_a, other_a = xgrad(p, masked)
    act, p, pb = forward(16, idx, x1, x3, masked, grads, (act,), (other_a,))

    parts = []

    def pack_two(first, after):
        packed = wgrad(first, 2, scalars, pa, pb, xs, after)
        for v, o in zip(packed, order[first : first + 2]):
            parts.append(v if o == (0, 0) else move_dp(v, *o))
        return (packed[0],)

    done = pack_two(0, ())
    done, back_a = send_back(own_a, other_a, done)
    done = pack_two(2, (done,))
    own_b, other_b = xgrad(p, masked, done)
    done = pack_two(4, (other_b,))
    done, back_b = send_back(own_b, other_b, done)
    pack_two(6, (done,))

    early = call(
        presum_kernel,
        0,
        jax.ShapeDtypeStruct((PAIRS, BLOCK, 128), F32),
        (parts[7], *parts[:4]),
        5 * CAP * 4096,
    )
    to_core, kept = call(
        sum_kernel,
        0,
        (jax.ShapeDtypeStruct((32, d), BF16), jax.ShapeDtypeStruct((32, d), F32)),
        (*back_a, *back_b),
        10 * 32 * d,
        after=(early,),
    )
    to_x, kept = call(
        sum_core_kernel,
        0,
        (jax.ShapeDtypeStruct((16, d), BF16), jax.ShapeDtypeStruct((16, d), F32)),
        (kept, move(to_core, dc=1)),
        32 * d,
    )
    x_grad = (kept + move(to_x, dx=1).astype(F32)).astype(BF16)

    weight_grad = call(
        unpack_kernel,
        2,
        jax.ShapeDtypeStruct((512, width), F32),
        (g.reshape(1), code, early, *parts[4:7]),
        8 * CAP * 4096,
        scratch=(
            pltpu.VMEM((width + BLOCK, 512), F32),
            pltpu.VMEM((512, width), F32),
            pltpu.SemaphoreType.DMA((4,)),
        ),
        out_space=pl.BlockSpec(memory_space=pl.ANY),
    )
    return (act.reshape(512, width), x_grad, weight_grad)


def solution(mesh):
    return jax.shard_map(
        layer,
        mesh=mesh,
        in_specs=(P(("dp", "tensor"), None), P(None, "tensor"), P(), P("dp", "tensor")),
        out_specs=(P("dp", "tensor"), P(("dp", "tensor"), None), P("dp", "tensor")),
        check_vma=False,
    )
```

```python
import functools

import jax
import jax.numpy as jnp
from jax import lax
from jax.experimental import pallas as pl
from jax.experimental.pallas import tpu as pltpu
from jax.sharding import PartitionSpec as P


BLOCK = 64
CAP = 70
PAIRS = CAP // 2
NZ = 8
NY = 4
F32 = jnp.float32
BF16 = jnp.bfloat16


VMEM = pl.BlockSpec(memory_space=pltpu.VMEM)
SMEM = pl.BlockSpec(memory_space=pltpu.SMEM)


def tensor_perm(dz, dx, dc, split=False):
    pairs = []
    for z in range(NZ):
        for xh in range(2):
            for core in range(2):
                shift = -dz if split and core else dz
                source = (z * 2 + xh) * 2 + core
                target = (((z + shift) % NZ) * 2 + (xh ^ dx)) * 2 + (core ^ dc)
                pairs.append((source, target))
    return pairs


def dp_perm(dx, dy):
    return [
        (xl * NY + y, (xl ^ dx) * NY + (y + dy) % NY) for xl in range(2) for y in range(NY)
    ]


def move(x, dz=0, dx=0, dc=0):
    return lax.ppermute(x, "tensor", tensor_perm(dz, dx, dc, split=True))


def move_dp(x, dx, dy):
    return lax.ppermute(x, "dp", dp_perm(dx, dy))


def call(kernel, n_scalar, out_shape, args, flops, scratch=(), after=(), limit=12, out_space=VMEM):
    n_args, n_after = len(args), len(after)

    def run(*refs):
        kernel(*refs[:n_args], *refs[n_args + n_after :])

    n_out = len(out_shape) if isinstance(out_shape, (tuple, list)) else 1
    out_specs = [VMEM] * n_out if isinstance(out_shape, (tuple, list)) else out_space
    moved = sum(a.size * a.dtype.itemsize for a in args)
    return pl.pallas_call(
        run,
        out_shape=out_shape,
        in_specs=[SMEM] * n_scalar
        + [VMEM] * (n_args - n_scalar)
        + [pl.BlockSpec(memory_space=pl.ANY)] * n_after,
        out_specs=out_specs,
        scratch_shapes=list(scratch),
        compiler_params=pltpu.CompilerParams(vmem_limit_bytes=limit << 20),
        cost_estimate=pl.CostEstimate(flops=flops, bytes_accessed=moved, transcendentals=0),
    )(*args, *after)


def tick_kernel(o_ref):
    o_ref[...] = jnp.zeros_like(o_ref)


def join_kernel(*refs):
    parts, out = refs[:-1], refs[-1]
    at = 0
    for part in parts:
        out[at : at + part.shape[0], :] = part[...]
        at += part.shape[0]


def join(*parts):
    rows = sum(part.shape[0] for part in parts)
    shape = jax.ShapeDtypeStruct((rows, parts[0].shape[1]), BF16)
    return call(join_kernel, 0, shape, parts, 0)


def mask_kernel(t_ref, w_ref, m_ref, o_ref, e_ref):
    n_rows, blocks = m_ref.shape
    width = w_ref.shape[1]
    rows = lax.broadcasted_iota(jnp.int32, (blocks, width), 0)
    cols = lax.broadcasted_iota(jnp.int32, (blocks, width), 1)
    pick = (rows == t_ref[0] + lax.div(cols, BLOCK)).astype(BF16)
    e_ref[...] = jnp.dot(m_ref[...].astype(F32).astype(BF16), pick, preferred_element_type=F32)

    @pl.loop(0, n_rows // 8)
    def _(g):
        eight = e_ref[pl.ds(pl.multiple_of(g * 8, 8), 8), :]
        for i in range(8):
            at = pl.ds(pl.multiple_of(g * 512 + i * BLOCK, BLOCK), BLOCK)
            row = jnp.broadcast_to(eight[i : i + 1, :], (BLOCK, width)).astype(BF16)
            o_ref[at, :] = w_ref[at, :] * row


def forward_kernel(first, count, idx_ref, xa, xb, w_ref, g_ref, *rest):
    act_ref, p_ref, acc_ref = rest[-3:]
    d = w_ref.shape[0]
    kb = 1024

    def product(s):
        cols = pl.ds(pl.multiple_of(s * kb, kb), kb)
        x = jnp.concatenate([xa[:, cols], xb[:, cols]], axis=0)
        return jnp.dot(x, w_ref[cols, :], preferred_element_type=F32)

    acc_ref[...] = product(0)

    @pl.loop(1, d // kb)
    def _(s):
        acc_ref[...] += product(s)

    @pl.loop(0, count)
    def _(n):
        at = idx_ref[first + n]
        rows = pl.ds(pl.multiple_of(n * 16, 16), 16)
        pre = acc_ref[rows, :]
        s = jax.nn.sigmoid(pre)
        act = (pre * s).astype(BF16)
        if first:
            act_ref[at] = act
            act_ref[idx_ref[n]] = rest[0][n]
        else:
            act_ref[n] = act
        grad = g_ref[at].astype(F32) * s * (1.0 + pre * (1.0 - s))
        p_ref[rows, :] = grad.astype(BF16)


def forward(first, idx, xa, xb, masked, act_grad, acts=(), after=()):
    d, width = masked.shape
    blocks = 32 if first else 16
    return call(
        functools.partial(forward_kernel, first, 16),
        1,
        (
            jax.ShapeDtypeStruct((blocks, 16, width), BF16),
            jax.ShapeDtypeStruct((256, width), BF16),
        ),
        (idx, xa, xb, masked, act_grad, *acts),
        2 * 256 * d * width,
        scratch=(pltpu.VMEM((256, width), F32),),
        after=after,
    )


def xgrad_kernel(p_ref, w_ref, own_ref, other_ref):
    @pl.loop(0, w_ref.shape[0] // 512)
    def _(s):
        cols = pl.ds(pl.multiple_of(s * 512, 512), 512)
        part = lax.dot_general(
            p_ref[...], w_ref[cols, :], (((1,), (1,)), ((), ())), preferred_element_type=F32
        )
        own_ref[:, cols] = part[:128, :]
        other_ref[:, cols] = part[128:, :].astype(BF16)


def xgrad(p, masked, after=()):
    d, width = masked.shape
    return call(
        xgrad_kernel,
        0,
        (jax.ShapeDtypeStruct((128, d), F32), jax.ShapeDtypeStruct((128, d), BF16)),
        (p, masked),
        2 * 256 * d * width,
        after=after,
    )


def mix_kernel(own_ref, r_ref, near1, near2, near3, far, home):
    @pl.loop(0, own_ref.shape[1] // 512)
    def _(s):
        cols = pl.ds(pl.multiple_of(s * 512, 512), 512)
        total = (own_ref[:, cols] + r_ref[:, cols].astype(F32)).astype(BF16)
        home[:, cols] = total[0:16, :]
        far[:, cols] = total[16:32, :]
        near1[:, cols] = total[32:64, :]
        near2[:, cols] = total[64:96, :]
        near3[:, cols] = total[96:128, :]


def mix(own, received, after):
    d = own.shape[1]
    return call(
        mix_kernel,
        0,
        [jax.ShapeDtypeStruct((32, d), BF16)] * 3 + [jax.ShapeDtypeStruct((16, d), BF16)] * 2,
        (own, received),
        128 * d,
        after=after,
    )


def hop_kernel(near, received, out):
    @pl.loop(0, near.shape[1] // 512)
    def _(s):
        cols = pl.ds(pl.multiple_of(s * 512, 512), 512)
        out[:, cols] = (near[:, cols].astype(F32) + received[:, cols].astype(F32)).astype(BF16)


def hop(near, received, after):
    shape = jax.ShapeDtypeStruct(near.shape, BF16)
    return call(hop_kernel, 0, shape, (near, received), near.size, after=after)


def sum_kernel(*refs):
    halves, to_core, kept = (refs[0:3], refs[3:6]), refs[6], refs[7]

    @pl.loop(0, kept.shape[1] // 512)
    def _(s):
        cols = pl.ds(pl.multiple_of(s * 512, 512), 512)
        for q, (near, far, home) in enumerate(halves):
            rows = slice(q * 16, q * 16 + 16)
            total = home[:, cols].astype(F32) + far[:, cols].astype(F32)
            kept[rows, cols] = total + near[0:16, cols].astype(F32)
            to_core[rows, cols] = near[16:32, cols]


def sum_core_kernel(kept, received, to_x, out):
    @pl.loop(0, kept.shape[1] // 512)
    def _(s):
        cols = pl.ds(pl.multiple_of(s * 512, 512), 512)
        total = kept[:, cols] + received[:, cols].astype(F32)
        out[:, cols] = total[0:16, :]
        to_x[:, cols] = total[16:32, :].astype(BF16)


def place_of(code):
    return (
        pl.multiple_of(code & 1023, BLOCK),
        pl.multiple_of((code >> 10) & 1023, 128),
        code >> 20,
    )


def wgrad_kernel(first, dest_ref, code_ref, odd_ref, pa, pb, x0, x1, x2, x3, *rest):
    outs, acc_ref = rest[:-1], rest[-1]
    left = lax.broadcasted_iota(jnp.int32, (BLOCK, 128), 1) < BLOCK
    over_rows = (((0,), (0,)), ((), ()))
    for n, out in enumerate(outs):
        dest = dest_ref[first + n]
        cols = pl.ds(pl.multiple_of(dest * 512, 512), 512)
        xa = jnp.concatenate([x0[:, cols], x2[:, cols]], axis=0)
        xb = jnp.concatenate([x1[:, cols], x3[:, cols]], axis=0)
        acc_ref[...] = lax.dot_general(
            xa, pa[...], over_rows, preferred_element_type=F32
        ) + lax.dot_general(xb, pb[...], over_rows, preferred_element_type=F32)

        def tiles(s):
            row, lane, h = place_of(code_ref[dest, s])
            row2, lane2, h2 = place_of(code_ref[dest, PAIRS + s])
            return (
                acc_ref[pl.ds(row, BLOCK), pl.ds(lane, 128)],
                acc_ref[pl.ds(row2, BLOCK), pl.ds(lane2, 128)],
                h & 1,
                h2 & 1,
            )

        def pack(s, carry):
            one, two, _, _ = tiles(s)
            out[s] = jnp.where(left, one, two).astype(BF16)
            return carry

        def repack(n, carry):
            s = PAIRS - 1 - n
            one, two, h, h2 = tiles(s)
            one = pltpu.roll(one, h * BLOCK, 1)
            two = pltpu.roll(two, (1 - h2) * BLOCK, 1)
            out[s] = jnp.where(left, one, two).astype(BF16)
            return carry

        lax.fori_loop(0, PAIRS, pack, 0, unroll=5)
        lax.fori_loop(0, odd_ref[dest], repack, 0)


def wgrad(first, count, scalars, pa, pb, xs, after):
    width = pa.shape[1]
    return call(
        functools.partial(wgrad_kernel, first),
        3,
        [jax.ShapeDtypeStruct((PAIRS, BLOCK, 128), BF16)] * count,
        (*scalars, pa, pb, *xs),
        2 * 512 * 512 * width * count,
        scratch=(pltpu.VMEM((512, width), F32),),
        after=after,
    )


def presum_kernel(*refs):
    parts, out = refs[:-1], refs[-1]

    @pl.loop(0, PAIRS)
    def _(s):
        total = parts[0][s].astype(F32)
        for part in parts[1:]:
            total = total + part[s].astype(F32)
        out[s] = total


def unpack_kernel(own_ref, code_ref, *refs):
    parts, (out, buf, sems) = refs[:-3], refs[-3:]
    own = own_ref[0]
    buf[...] = jnp.zeros_like(buf)
    half = lax.broadcasted_iota(jnp.int32, (BLOCK, 128), 1) // BLOCK

    def place(s, carry):
        total = parts[0][s]
        for part in parts[1:]:
            total = total + part[s].astype(F32)
        row, lane, h = place_of(code_ref[own, s])
        at = buf.at[pl.ds(row, BLOCK), pl.ds(lane, 128)]
        at[...] = jnp.where(half == h, pltpu.roll(total, (h & 1) * BLOCK, 1), at[...])
        row, lane, h = place_of(code_ref[own, PAIRS + s])
        at = buf.at[pl.ds(row, BLOCK), pl.ds(lane, 128)]
        at[...] = jnp.where(half == h, pltpu.roll(total, (1 - (h & 1)) * BLOCK, 1), at[...])
        return carry

    lax.fori_loop(0, PAIRS, place, 0)
    copies = []
    for c in range(4):
        rows = slice(c * 128, (c + 1) * 128)
        copies.append(pltpu.make_async_copy(buf.at[rows], out.at[rows], sems.at[c]))
        copies[-1].start()
    for copy in copies:
        copy.wait()


def kept_codes(block_mask, t):
    mask = lax.dynamic_slice(block_mask, (0, t * 14), (64, 14)).reshape(8, 112)
    kept = mask != 0
    at = jnp.arange(112, dtype=jnp.int32)
    i = jnp.array([b // 14 for b in range(112)], jnp.int32)
    j = at - i * 14
    h = j & 1
    before = (at[:, None] <= at[None, :]) & (h[:, None] == h[None, :])
    rank = jnp.dot(kept.astype(BF16), before.astype(BF16), preferred_element_type=F32)
    rank = rank.astype(jnp.int32) - 1
    extra = rank >= PAIRS
    slot = jnp.where(extra, 3 * PAIRS - 1 - PAIRS * h - rank, rank + PAIRS * h)
    hit = kept[:, None, :] & (slot[:, None, :] == jnp.arange(CAP, dtype=jnp.int32)[None, :, None])
    code = i * BLOCK + (j >> 1) * (128 << 10) + ((h - 2) << 20)
    code = jnp.sum(jnp.where(hit, code[None, None, :], 0), axis=2, dtype=jnp.int32) + (2 << 20)
    odd = jnp.sum((kept & extra).astype(jnp.int32), axis=1, dtype=jnp.int32)
    return code, odd


def layer(tokens, weight, block_mask, act_grad):
    d, width = weight.shape
    t = lax.axis_index("tensor").astype(jnp.int32)
    g = lax.axis_index("dp").astype(jnp.int32)

    partner = move(tokens, dc=1)
    home = move(tokens, dx=1)
    chip = join(tokens, partner)
    t, g, chip = lax.optimization_barrier((t, g, chip))
    z, xh, core = t >> 2, (t >> 1) & 1, t & 1
    xl, y = g >> 2, g & 3
    near = [move(chip, dz=1)]
    near.append(move(near[0], dz=1))
    near.append(move(near[1], dz=1))
    far = move(tokens, dz=4)

    n = jnp.arange(32, dtype=jnp.int32)
    slot = n & 7
    dist = jnp.where(slot == 0, 0, jnp.where(slot == 1, 4, slot >> 1))
    flip = jnp.where(slot > 1, slot & 1, 0)
    gather_core = core ^ ((n >> 3) & 1)
    zk = (z - (1 - 2 * gather_core) * dist) & (NZ - 1)
    idx = zk * 4 + (xh ^ (n >> 4)) * 2 + (gather_core ^ flip)
    order = [(1, 2), (1, 0), (1, 1), (0, 2), (1, 3), (0, 1), (0, 3), (0, 0)]
    dx = jnp.array([o[0] for o in order], jnp.int32)
    dy = jnp.array([o[1] for o in order], jnp.int32)
    dests = (xl ^ dx) * NY + ((y + dy) & (NY - 1))

    ticks = [call(tick_kernel, 0, jax.ShapeDtypeStruct((8, 128), F32), (), 0) for _ in range(2)]
    t_list, ticks[0] = lax.optimization_barrier((t, ticks[0]))
    t_mask, ticks[1] = lax.optimization_barrier((t, ticks[1]))
    masked = call(
        mask_kernel,
        1,
        jax.ShapeDtypeStruct((d, width), BF16),
        ((t_mask * 14).reshape(1), weight, block_mask),
        d * width,
        scratch=(pltpu.VMEM((64, width), F32),),
    )
    code, odd = kept_codes(block_mask, t_list)
    code, odd, idx, dests, near[1] = lax.optimization_barrier((code, odd, idx, dests, near[1]))
    near[2], masked = lax.optimization_barrier((near[2], masked))
    scalars = (dests, code, odd)

    near_x = [move(near[k], dx=1) for k in range(3)]
    far_x = move(far, dx=1)
    x0 = join(tokens, far, *near)
    x2 = move(x0, dc=1)
    x1 = join(home, far_x, *near_x)
    x3 = move(x1, dc=1)
    xs = (x0, x1, x2, x3)

    grads = act_grad.reshape(32, 16, width)
    act, pa = forward(0, idx, x0, x2, masked, grads, after=ticks)
    own_a, other_a = xgrad(pa, masked)
    received_a = move(other_a, dc=1)
    act, pb = forward(16, idx, x1, x3, masked, grads, (act,), (other_a,))

    parts = []

    def pack_two(first, after):
        packed = wgrad(first, 2, scalars, pa, pb, xs, after)
        for v, o in zip(packed, order[first : first + 2]):
            parts.append(v if o == (0, 0) else move_dp(v, *o))
        return packed[0]

    def back(x, hops=1):
        return move(x, dz=NZ - hops)

    done = pack_two(0, ())
    a1, a2, a3, far_a, home_a = mix(own_a, received_a, (done,))
    ring_a, far_a = back(a3), back(far_a, 4)
    own_b, other_b = xgrad(pb, masked, (a3,))
    received_b = move(other_b, dc=1)
    done = pack_two(2, (other_b,))
    done = hop(a2, ring_a, (done,))
    ring_a = back(done)
    b1, b2, b3, far_b, home_b = mix(own_b, received_b, (done,))
    ring_b, far_b = back(b3), back(far_b, 4)
    done = pack_two(4, (b3,))
    done = hop(a1, ring_a, (done,))
    ring_a = back(done)
    done = hop(b2, ring_b, (done,))
    ring_b = back(done)
    done = pack_two(6, (done,))
    done = hop(b1, ring_b, (done,))
    ring_b = back(done)

    early = call(
        presum_kernel,
        0,
        jax.ShapeDtypeStruct((PAIRS, BLOCK, 128), F32),
        (parts[7], *parts[:4]),
        5 * CAP * 4096,
        after=(done,),
    )
    to_core, kept = call(
        sum_kernel,
        0,
        (jax.ShapeDtypeStruct((32, d), BF16), jax.ShapeDtypeStruct((32, d), F32)),
        (ring_a, far_a, home_a, ring_b, far_b, home_b),
        6 * 32 * d,
        after=(early,),
    )
    to_x, kept = call(
        sum_core_kernel,
        0,
        (jax.ShapeDtypeStruct((16, d), BF16), jax.ShapeDtypeStruct((16, d), F32)),
        (kept, move(to_core, dc=1)),
        32 * d,
    )
    x_grad = (kept + move(to_x, dx=1).astype(F32)).astype(BF16)

    weight_grad = call(
        unpack_kernel,
        2,
        jax.ShapeDtypeStruct((512, width), F32),
        (g.reshape(1), code, early, *parts[4:7]),
        8 * CAP * 4096,
        scratch=(
            pltpu.VMEM((512, width), F32),
            pltpu.SemaphoreType.DMA((4,)),
        ),
        out_space=pl.BlockSpec(memory_space=pl.ANY),
    )
    return (act.reshape(512, width), x_grad, weight_grad)


def solution(mesh):
    return jax.shard_map(
        layer,
        mesh=mesh,
        in_specs=(P(("dp", "tensor"), None), P(None, "tensor"), P(), P("dp", "tensor")),
        out_specs=(P("dp", "tensor"), P(("dp", "tensor"), None), P("dp", "tensor")),
        check_vma=False,
    )
```

```python
import functools

import jax
import jax.numpy as jnp
from jax import lax
from jax.experimental import pallas as pl
from jax.experimental.pallas import tpu as pltpu
from jax.sharding import PartitionSpec as P


BLOCK = 64
CAP = 70
PAIRS = CAP // 2
NZ = 8
NY = 4
F32 = jnp.float32
BF16 = jnp.bfloat16


VMEM = pl.BlockSpec(memory_space=pltpu.VMEM)
SMEM = pl.BlockSpec(memory_space=pltpu.SMEM)


def tensor_perm(dz, dx, dc, split=False):
    pairs = []
    for z in range(NZ):
        for xh in range(2):
            for core in range(2):
                shift = -dz if split and core else dz
                source = (z * 2 + xh) * 2 + core
                target = (((z + shift) % NZ) * 2 + (xh ^ dx)) * 2 + (core ^ dc)
                pairs.append((source, target))
    return pairs


def dp_perm(dx, dy):
    return [
        (xl * NY + y, (xl ^ dx) * NY + (y + dy) % NY) for xl in range(2) for y in range(NY)
    ]


def move(x, dz=0, dx=0, dc=0):
    return lax.ppermute(x, "tensor", tensor_perm(dz, dx, dc, split=True))


def move_dp(x, dx, dy):
    return lax.ppermute(x, "dp", dp_perm(dx, dy))


def call(
    kernel, n_scalar, out_shape, args, flops, scratch=(), after=(), limit=12, out_space=VMEM,
    space=VMEM,
):
    n_args, n_after = len(args), len(after)

    def run(*refs):
        kernel(*refs[:n_args], *refs[n_args + n_after :])

    n_out = len(out_shape) if isinstance(out_shape, (tuple, list)) else 1
    out_specs = [VMEM] * n_out if isinstance(out_shape, (tuple, list)) else out_space
    moved = sum(a.size * a.dtype.itemsize for a in args)
    return pl.pallas_call(
        run,
        out_shape=out_shape,
        in_specs=[SMEM] * n_scalar
        + [space] * (n_args - n_scalar)
        + [pl.BlockSpec(memory_space=pl.ANY)] * n_after,
        out_specs=out_specs,
        scratch_shapes=list(scratch),
        compiler_params=pltpu.CompilerParams(vmem_limit_bytes=limit << 20),
        cost_estimate=pl.CostEstimate(flops=flops, bytes_accessed=moved, transcendentals=0),
    )(*args, *after)


def tick_kernel(*refs):
    refs[-1][...] = jnp.zeros_like(refs[-1])


def join_kernel(*refs):
    parts, out = refs[:-1], refs[-1]
    at = 0
    for part in parts:
        out[at : at + part.shape[0], :] = part[...]
        at += part.shape[0]


def join(*parts):
    rows = sum(part.shape[0] for part in parts)
    shape = jax.ShapeDtypeStruct((rows, parts[0].shape[1]), BF16)
    return call(join_kernel, 0, shape, parts, 0)


def head_kernel(x_ref, o_ref):
    o_ref[...] = x_ref[0 : o_ref.shape[0], :]


def mask_kernel(t_ref, w_hbm, m_hbm, o_ref, m_ref, e_ref, sems):
    n_rows, blocks = m_ref.shape
    width = o_ref.shape[1]
    groups = n_rows // 8

    def part(g):
        rows = pl.ds(pl.multiple_of(g * 512, 512), 512)
        return pltpu.make_async_copy(w_hbm.at[rows], o_ref.at[rows], sems.at[g])

    mask_copy = pltpu.make_async_copy(m_hbm, m_ref, sems.at[groups])
    mask_copy.start()
    for g in range(groups):
        part(g).start()
    rows = lax.broadcasted_iota(jnp.int32, (blocks, width), 0)
    cols = lax.broadcasted_iota(jnp.int32, (blocks, width), 1)
    pick = (rows == t_ref[0] + lax.div(cols, BLOCK)).astype(BF16)
    mask_copy.wait()
    e_ref[...] = jnp.dot(m_ref[...].astype(F32).astype(BF16), pick, preferred_element_type=F32)

    @pl.loop(0, groups)
    def _(g):
        part(g).wait()
        eight = e_ref[pl.ds(pl.multiple_of(g * 8, 8), 8), :]
        for i in range(8):
            at = pl.ds(pl.multiple_of(g * 512 + i * BLOCK, BLOCK), BLOCK)
            row = jnp.broadcast_to(eight[i : i + 1, :], (BLOCK, width)).astype(BF16)
            o_ref[at, :] = o_ref[at, :] * row


def forward_kernel(first, count, idx_ref, xa, xb, w_ref, g_ref, *rest):
    act_ref, p_ref, acc_ref = rest[-3:]
    d = w_ref.shape[0]
    kb = 1024

    def product(s):
        cols = pl.ds(pl.multiple_of(s * kb, kb), kb)
        x = jnp.concatenate([xa[:, cols], xb[:, cols]], axis=0)
        return jnp.dot(x, w_ref[cols, :], preferred_element_type=F32)

    acc_ref[...] = product(0)

    @pl.loop(1, d // kb)
    def _(s):
        acc_ref[...] += product(s)

    @pl.loop(0, count)
    def _(n):
        at = idx_ref[first + n]
        rows = pl.ds(pl.multiple_of(n * 16, 16), 16)
        pre = acc_ref[rows, :]
        s = jax.nn.sigmoid(pre)
        act = (pre * s).astype(BF16)
        if first:
            act_ref[at] = act
            act_ref[idx_ref[n]] = rest[0][n]
        else:
            act_ref[n] = act
        grad = g_ref[at].astype(F32) * s * (1.0 + pre * (1.0 - s))
        p_ref[rows, :] = grad.astype(BF16)


def forward(first, idx, xa, xb, masked, act_grad, acts=(), after=()):
    d, width = masked.shape
    blocks = 32 if first else 16
    return call(
        functools.partial(forward_kernel, first, 16),
        1,
        (
            jax.ShapeDtypeStruct((blocks, 16, width), BF16),
            jax.ShapeDtypeStruct((256, width), BF16),
        ),
        (idx, xa, xb, masked, act_grad, *acts),
        2 * 256 * d * width,
        scratch=(pltpu.VMEM((256, width), F32),),
        after=after,
    )


def xgrad_kernel(p_ref, w_ref, own_ref, other_ref):
    @pl.loop(0, w_ref.shape[0] // 512)
    def _(s):
        cols = pl.ds(pl.multiple_of(s * 512, 512), 512)
        part = lax.dot_general(
            p_ref[...], w_ref[cols, :], (((1,), (1,)), ((), ())), preferred_element_type=F32
        )
        own_ref[:, cols] = part[:128, :]
        other_ref[:, cols] = part[128:, :].astype(BF16)


def xgrad(p, masked, after=()):
    d, width = masked.shape
    return call(
        xgrad_kernel,
        0,
        (jax.ShapeDtypeStruct((128, d), F32), jax.ShapeDtypeStruct((128, d), BF16)),
        (p, masked),
        2 * 256 * d * width,
        after=after,
    )


def mix_kernel(own_ref, r_ref, near1, near2, near3, far, home):
    @pl.loop(0, own_ref.shape[1] // 512)
    def _(s):
        cols = pl.ds(pl.multiple_of(s * 512, 512), 512)
        total = (own_ref[:, cols] + r_ref[:, cols].astype(F32)).astype(BF16)
        home[:, cols] = total[0:16, :]
        far[:, cols] = total[16:32, :]
        near1[:, cols] = total[32:64, :]
        near2[:, cols] = total[64:96, :]
        near3[:, cols] = total[96:128, :]


def mix(own, received, after):
    d = own.shape[1]
    return call(
        mix_kernel,
        0,
        [jax.ShapeDtypeStruct((32, d), BF16)] * 3 + [jax.ShapeDtypeStruct((16, d), BF16)] * 2,
        (own, received),
        128 * d,
        after=after,
    )


def hop_kernel(near, received, out):
    @pl.loop(0, near.shape[1] // 512)
    def _(s):
        cols = pl.ds(pl.multiple_of(s * 512, 512), 512)
        out[:, cols] = (near[:, cols].astype(F32) + received[:, cols].astype(F32)).astype(BF16)


def hop_far_kernel(near, received, out):
    @pl.loop(0, near.shape[1] // 512)
    def _(s):
        cols = pl.ds(pl.multiple_of(s * 512, 512), 512)
        total = near[0:16, cols].astype(F32) + received[:, cols].astype(F32)
        out[0:16, cols] = total.astype(BF16)
        out[16:32, cols] = near[16:32, cols]


def hop(near, received, after):
    shape = jax.ShapeDtypeStruct(near.shape, BF16)
    kernel = hop_kernel if near.shape == received.shape else hop_far_kernel
    return call(kernel, 0, shape, (near, received), near.size, after=after)


def sum_kernel(*refs):
    halves, to_core, kept = (refs[0:2], refs[2:4]), refs[4], refs[5]

    @pl.loop(0, kept.shape[1] // 512)
    def _(s):
        cols = pl.ds(pl.multiple_of(s * 512, 512), 512)
        for q, (near, home) in enumerate(halves):
            rows = slice(q * 16, q * 16 + 16)
            kept[rows, cols] = home[:, cols].astype(F32) + near[0:16, cols].astype(F32)
            to_core[rows, cols] = near[16:32, cols]


def sum_core_kernel(kept, received, to_x, out):
    @pl.loop(0, kept.shape[1] // 512)
    def _(s):
        cols = pl.ds(pl.multiple_of(s * 512, 512), 512)
        total = kept[:, cols] + received[:, cols].astype(F32)
        out[:, cols] = total[0:16, :]
        to_x[:, cols] = total[16:32, :].astype(BF16)


def place_of(code):
    return (
        pl.multiple_of(code & 1023, BLOCK),
        pl.multiple_of((code >> 10) & 1023, 128),
        code >> 20,
    )


def wgrad_kernel(first, dest_ref, code_ref, odd_ref, pa, pb, x0, x1, x2, x3, *rest):
    outs, acc_ref = rest[:-1], rest[-1]
    left = lax.broadcasted_iota(jnp.int32, (BLOCK, 128), 1) < BLOCK
    over_rows = (((0,), (0,)), ((), ()))
    for n, out in enumerate(outs):
        dest = dest_ref[first + n]
        cols = pl.ds(pl.multiple_of(dest * 512, 512), 512)
        xa = jnp.concatenate([x0[:, cols], x2[:, cols]], axis=0)
        xb = jnp.concatenate([x1[:, cols], x3[:, cols]], axis=0)
        acc_ref[...] = lax.dot_general(
            xa, pa[...], over_rows, preferred_element_type=F32
        ) + lax.dot_general(xb, pb[...], over_rows, preferred_element_type=F32)

        def tiles(s):
            row, lane, h = place_of(code_ref[dest, s])
            row2, lane2, h2 = place_of(code_ref[dest, PAIRS + s])
            return (
                acc_ref[pl.ds(row, BLOCK), pl.ds(lane, 128)],
                acc_ref[pl.ds(row2, BLOCK), pl.ds(lane2, 128)],
                h & 1,
                h2 & 1,
            )

        def pack(s, carry):
            one, two, _, _ = tiles(s)
            out[s] = jnp.where(left, one, two).astype(BF16)
            return carry

        def repack(n, carry):
            s = PAIRS - 1 - n
            one, two, h, h2 = tiles(s)
            one = pltpu.roll(one, h * BLOCK, 1)
            two = pltpu.roll(two, (1 - h2) * BLOCK, 1)
            out[s] = jnp.where(left, one, two).astype(BF16)
            return carry

        lax.fori_loop(0, PAIRS, pack, 0, unroll=5)
        lax.fori_loop(0, odd_ref[dest], repack, 0)


def wgrad(first, count, scalars, pa, pb, xs, after):
    width = pa.shape[1]
    return call(
        functools.partial(wgrad_kernel, first),
        3,
        [jax.ShapeDtypeStruct((PAIRS, BLOCK, 128), BF16)] * count,
        (*scalars, pa, pb, *xs),
        2 * 512 * 512 * width * count,
        scratch=(pltpu.VMEM((512, width), F32),),
        after=after,
    )


def presum_kernel(*refs):
    parts, out = refs[:-1], refs[-1]

    @pl.loop(0, PAIRS)
    def _(s):
        total = parts[0][s].astype(F32)
        for part in parts[1:]:
            total = total + part[s].astype(F32)
        out[s] = total


def unpack_kernel(own_ref, code_ref, *refs):
    parts, (out, buf, sems) = refs[:-3], refs[-3:]
    own = own_ref[0]
    buf[...] = jnp.zeros_like(buf)
    half = lax.broadcasted_iota(jnp.int32, (BLOCK, 128), 1) // BLOCK

    def place(s, carry):
        total = parts[0][s]
        for part in parts[1:]:
            total = total + part[s].astype(F32)
        other = pltpu.roll(total, BLOCK, 1)
        for side in range(2):
            row, lane, h = place_of(code_ref[own, side * PAIRS + s])
            value = jnp.where(h == side, total, other)
            at = buf.at[pl.ds(row, BLOCK), pl.ds(lane, 128)]
            pltpu.store(at, value, mask=half == h)
        return carry

    lax.fori_loop(0, PAIRS, place, 0, unroll=5)
    copies = []
    for c in range(4):
        rows = slice(c * 128, (c + 1) * 128)
        copies.append(pltpu.make_async_copy(buf.at[rows], out.at[rows], sems.at[c]))
        copies[-1].start()
    for copy in copies:
        copy.wait()


def slots_of(block_mask, t):
    mask = lax.dynamic_slice(block_mask, (0, t * 14), (64, 14)).reshape(8, 112)
    kept = mask != 0
    at = jnp.arange(112, dtype=jnp.int32)
    h = jnp.array([b % 14 % 2 for b in range(112)], jnp.int32)
    before = (at[:, None] <= at[None, :]) & (h[:, None] == h[None, :])
    rank = jnp.dot(kept.astype(BF16), before.astype(BF16), preferred_element_type=F32)
    rank = rank.astype(jnp.int32) - 1
    extra = rank >= PAIRS
    slot = jnp.where(extra, 3 * PAIRS - 1 - PAIRS * h - rank, rank + PAIRS * h)
    odd = jnp.sum((kept & extra).astype(jnp.int32), axis=1, dtype=jnp.int32)
    return jnp.where(kept, slot, -1), odd


def codes_of(slot):
    i = jnp.array([b // 14 for b in range(112)], jnp.int32)
    j = jnp.array([b % 14 for b in range(112)], jnp.int32)
    hit = slot[:, None, :] == jnp.arange(CAP, dtype=jnp.int32)[None, :, None]
    code = i * BLOCK + (j >> 1) * (128 << 10) + (((j & 1) - 2) << 20)
    return jnp.sum(jnp.where(hit, code[None, None, :], 0), axis=2, dtype=jnp.int32) + (2 << 20)


def layer(tokens, weight, block_mask, act_grad):
    d, width = weight.shape
    t = lax.axis_index("tensor").astype(jnp.int32)
    g = lax.axis_index("dp").astype(jnp.int32)

    partner = move(tokens, dc=1)
    home = move(tokens, dx=1)
    chip = join(tokens, partner)
    t, g, chip = lax.optimization_barrier((t, g, chip))
    z, xh, core = t >> 2, (t >> 1) & 1, t & 1
    xl, y = g >> 2, g & 3

    n = jnp.arange(32, dtype=jnp.int32)
    slot = n & 7
    dist = jnp.where(slot == 0, 0, jnp.where(slot == 1, 4, slot >> 1))
    flip = jnp.where(slot > 1, slot & 1, 0)
    gather_core = core ^ ((n >> 3) & 1)
    zk = (z - (1 - 2 * gather_core) * dist) & (NZ - 1)
    idx = zk * 4 + (xh ^ (n >> 4)) * 2 + (gather_core ^ flip)
    order = [(1, 0), (0, 2), (1, 1), (1, 3), (1, 2), (0, 1), (0, 3), (0, 0)]
    dx = jnp.array([o[0] for o in order], jnp.int32)
    dy = jnp.array([o[1] for o in order], jnp.int32)
    dests = (xl ^ dx) * NY + ((y + dy) & (NY - 1))

    def tick():
        return call(tick_kernel, 0, jax.ShapeDtypeStruct((8, 128), F32), (), 0)

    ticks = [tick() for _ in range(4)]
    near1 = move(chip, dz=1)
    t_slot, ticks[0] = lax.optimization_barrier((t, ticks[0]))
    slot, odd = slots_of(block_mask, t_slot)
    slot, odd, idx, dests, near1 = lax.optimization_barrier((slot, odd, idx, dests, near1))
    near2 = move(near1, dz=1)
    slot, ticks[1] = lax.optimization_barrier((slot, ticks[1]))
    code, near2 = lax.optimization_barrier((codes_of(slot), near2))
    scalars = (dests, code, odd)

    near3 = move(near2, dz=1)
    t_mask, ticks[2] = lax.optimization_barrier((t, ticks[2]))
    masked = call(
        mask_kernel,
        1,
        jax.ShapeDtypeStruct((d, width), BF16),
        ((t_mask * 14).reshape(1), weight, block_mask),
        d * width,
        scratch=(
            pltpu.VMEM(block_mask.shape, jnp.int32),
            pltpu.VMEM((block_mask.shape[0], width), F32),
            pltpu.SemaphoreType.DMA((9,)),
        ),
        space=pl.BlockSpec(memory_space=pl.ANY),
        limit=44,
    )
    near3, masked = lax.optimization_barrier((near3, masked))

    head = call(head_kernel, 0, jax.ShapeDtypeStruct((16, d), BF16), (near3,), 0)
    far = move(head, dz=1)
    cross = [move(v, dx=1) for v in (near1, near2, near3, far)]
    x0 = join(tokens, far, near1, near2, near3)
    x2 = move(x0, dc=1)
    x1 = join(home, cross[3], *cross[:3])
    x3 = move(x1, dc=1)
    xs = (x0, x1, x2, x3)

    grads = act_grad.reshape(32, 16, width)
    act, pa = forward(0, idx, x0, x2, masked, grads, after=ticks)
    own_a, other_a = xgrad(pa, masked)
    received_a = move(other_a, dc=1)
    act, pb = forward(16, idx, x1, x3, masked, grads, (act,), (other_a,))

    parts = []

    def pack(first, count, after):
        packed = wgrad(first, count, scalars, pa, pb, xs, (after,))
        for v, o in zip(packed, order[first : first + count]):
            parts.append(v if o == (0, 0) else move_dp(v, *o))
        return packed[0]

    def back(x):
        return move(x, dz=NZ - 1)

    done = pack(0, 1, other_a)
    done = pack(1, 2, done)
    a1, a2, a3, a4, home_a = mix(own_a, received_a, (done,))
    ring_a = back(a4)
    own_b, other_b = xgrad(pb, masked, (a4,))
    received_b = move(other_b, dc=1)
    done = hop(a3, ring_a, (other_b,))
    ring_a = back(done)
    done = pack(3, 2, done)
    b1, b2, b3, b4, home_b = mix(own_b, received_b, (done,))
    ring_b = back(b4)
    done = hop(a2, ring_a, (b4,))
    ring_a = back(done)
    done = pack(5, 2, done)
    done = hop(b3, ring_b, (done,))
    ring_b = back(done)
    done = hop(a1, ring_a, (done,))
    ring_a = back(done)
    done = pack(7, 1, done)
    done = hop(b2, ring_b, (done,))
    ring_b = back(done)
    done = hop(b1, ring_b, (done,))
    ring_b = back(done)

    early = call(
        presum_kernel,
        0,
        jax.ShapeDtypeStruct((PAIRS, BLOCK, 128), F32),
        (parts[7], *parts[:4]),
        5 * CAP * 4096,
        after=(done,),
    )
    to_core, kept = call(
        sum_kernel,
        0,
        (jax.ShapeDtypeStruct((32, d), BF16), jax.ShapeDtypeStruct((32, d), F32)),
        (ring_a, home_a, ring_b, home_b),
        4 * 32 * d,
        after=(early,),
    )
    to_x, kept = call(
        sum_core_kernel,
        0,
        (jax.ShapeDtypeStruct((16, d), BF16), jax.ShapeDtypeStruct((16, d), F32)),
        (kept, move(to_core, dc=1)),
        32 * d,
    )
    x_grad = (kept + move(to_x, dx=1).astype(F32)).astype(BF16)

    weight_grad = call(
        unpack_kernel,
        2,
        jax.ShapeDtypeStruct((512, width), F32),
        (g.reshape(1), code, early, *parts[4:7]),
        8 * CAP * 4096,
        scratch=(
            pltpu.VMEM((512, width), F32),
            pltpu.SemaphoreType.DMA((4,)),
        ),
        out_space=pl.BlockSpec(memory_space=pl.ANY),
    )
    return (act.reshape(512, width), x_grad, weight_grad)


def solution(mesh):
    return jax.shard_map(
        layer,
        mesh=mesh,
        in_specs=(P(("dp", "tensor"), None), P(None, "tensor"), P(), P("dp", "tensor")),
        out_specs=(P("dp", "tensor"), P(("dp", "tensor"), None), P("dp", "tensor")),
        check_vma=False,
    )
```

```python
import functools

import jax
import jax.numpy as jnp
from jax import lax
from jax.experimental import pallas as pl
from jax.experimental.pallas import tpu as pltpu
from jax.sharding import PartitionSpec as P


BLOCK = 64
CAP = 70
PAIRS = CAP // 2
NZ = 8
NY = 4
F32 = jnp.float32
BF16 = jnp.bfloat16


VMEM = pl.BlockSpec(memory_space=pltpu.VMEM)
SMEM = pl.BlockSpec(memory_space=pltpu.SMEM)


def tensor_perm(dz, dx, dc, split=False):
    pairs = []
    for z in range(NZ):
        for xh in range(2):
            for core in range(2):
                shift = -dz if split and core else dz
                source = (z * 2 + xh) * 2 + core
                target = (((z + shift) % NZ) * 2 + (xh ^ dx)) * 2 + (core ^ dc)
                pairs.append((source, target))
    return pairs


def dp_perm(dx, dy):
    return [
        (xl * NY + y, (xl ^ dx) * NY + (y + dy) % NY) for xl in range(2) for y in range(NY)
    ]


def move(x, dz=0, dx=0, dc=0):
    return lax.ppermute(x, "tensor", tensor_perm(dz, dx, dc, split=True))


def move_dp(x, dx, dy):
    return lax.ppermute(x, "dp", dp_perm(dx, dy))


def call(
    kernel, n_scalar, out_shape, args, flops, scratch=(), after=(), limit=12, out_space=VMEM,
    space=VMEM,
):
    n_args, n_after = len(args), len(after)

    def run(*refs):
        kernel(*refs[:n_args], *refs[n_args + n_after :])

    n_out = len(out_shape) if isinstance(out_shape, (tuple, list)) else 1
    out_specs = [VMEM] * n_out if isinstance(out_shape, (tuple, list)) else out_space
    moved = sum(a.size * a.dtype.itemsize for a in args)
    return pl.pallas_call(
        run,
        out_shape=out_shape,
        in_specs=[SMEM] * n_scalar
        + [space] * (n_args - n_scalar)
        + [pl.BlockSpec(memory_space=pl.ANY)] * n_after,
        out_specs=out_specs,
        scratch_shapes=list(scratch),
        compiler_params=pltpu.CompilerParams(vmem_limit_bytes=limit << 20),
        cost_estimate=pl.CostEstimate(flops=flops, bytes_accessed=moved, transcendentals=0),
    )(*args, *after)


def tick_kernel(*refs):
    refs[-1][...] = jnp.zeros_like(refs[-1])


def join_kernel(*refs):
    parts, out = refs[:-1], refs[-1]
    at = 0
    for part in parts:
        out[at : at + part.shape[0], :] = part[...]
        at += part.shape[0]


def join(*parts):
    rows = sum(part.shape[0] for part in parts)
    shape = jax.ShapeDtypeStruct((rows, parts[0].shape[1]), BF16)
    return call(join_kernel, 0, shape, parts, 0)


def head_kernel(x_ref, o_ref):
    o_ref[...] = x_ref[0 : o_ref.shape[0], :]


def mask_kernel(t_ref, w_hbm, m_hbm, o_ref, m_ref, e_ref, sems):
    n_rows, blocks = m_ref.shape
    width = o_ref.shape[1]
    groups = n_rows // 8

    def part(g):
        rows = pl.ds(pl.multiple_of(g * 512, 512), 512)
        return pltpu.make_async_copy(w_hbm.at[rows], o_ref.at[rows], sems.at[g])

    mask_copy = pltpu.make_async_copy(m_hbm, m_ref, sems.at[groups])
    mask_copy.start()
    for g in range(groups):
        part(g).start()
    rows = lax.broadcasted_iota(jnp.int32, (blocks, width), 0)
    cols = lax.broadcasted_iota(jnp.int32, (blocks, width), 1)
    pick = (rows == t_ref[0] + lax.div(cols, BLOCK)).astype(BF16)
    mask_copy.wait()
    e_ref[...] = jnp.dot(m_ref[...].astype(F32).astype(BF16), pick, preferred_element_type=F32)

    @pl.loop(0, groups)
    def _(g):
        part(g).wait()
        eight = e_ref[pl.ds(pl.multiple_of(g * 8, 8), 8), :]
        for i in range(8):
            at = pl.ds(pl.multiple_of(g * 512 + i * BLOCK, BLOCK), BLOCK)
            row = jnp.broadcast_to(eight[i : i + 1, :], (BLOCK, width)).astype(BF16)
            o_ref[at, :] = o_ref[at, :] * row


def forward_kernel(first, idx_ref, xa, xb, w_ref, g_ref, act_ref, p_ref, acc_ref):
    d = w_ref.shape[0]
    kb = 1024

    def product(s):
        cols = pl.ds(pl.multiple_of(s * kb, kb), kb)
        x = jnp.concatenate([xa[:, cols], xb[:, cols]], axis=0)
        return jnp.dot(x, w_ref[cols, :], preferred_element_type=F32)

    acc_ref[...] = product(0)

    @pl.loop(1, d // kb)
    def _(s):
        acc_ref[...] += product(s)

    def finish(n, carry):
        rows = pl.ds(pl.multiple_of(n * 16, 16), 16)
        pre = acc_ref[rows, :]
        s = jax.nn.sigmoid(pre)
        act_ref[n] = (pre * s).astype(BF16)
        grad = g_ref[idx_ref[first + n]].astype(F32) * s * (1.0 + pre * (1.0 - s))
        p_ref[rows, :] = grad.astype(BF16)
        return carry

    lax.fori_loop(0, act_ref.shape[0], finish, 0, unroll=2)


def forward(first, idx, xa, xb, masked, act_grad, after=()):
    d, width = masked.shape
    return call(
        functools.partial(forward_kernel, first),
        1,
        (
            jax.ShapeDtypeStruct((16, 16, width), BF16),
            jax.ShapeDtypeStruct((256, width), BF16),
        ),
        (idx, xa, xb, masked, act_grad),
        2 * 256 * d * width,
        scratch=(pltpu.VMEM((256, width), F32),),
        after=after,
    )


def act_join_kernel(idx_ref, a_ref, b_ref, out, tick):
    tick[...] = jnp.zeros_like(tick)

    @pl.loop(0, 16)
    def _(n):
        out[idx_ref[n]] = a_ref[n]
        out[idx_ref[16 + n]] = b_ref[n]


def last_kernel(kept, received, out, tick):
    tick[...] = jnp.zeros_like(tick)
    out[...] = (kept[...] + received[...].astype(F32)).astype(BF16)


def xgrad_kernel(p_ref, w_ref, own_ref, other_ref):
    @pl.loop(0, w_ref.shape[0] // 512)
    def _(s):
        cols = pl.ds(pl.multiple_of(s * 512, 512), 512)
        part = lax.dot_general(
            p_ref[...], w_ref[cols, :], (((1,), (1,)), ((), ())), preferred_element_type=F32
        )
        own_ref[:, cols] = part[:128, :]
        other_ref[:, cols] = part[128:, :].astype(BF16)


def xgrad(p, masked, after=()):
    d, width = masked.shape
    return call(
        xgrad_kernel,
        0,
        (jax.ShapeDtypeStruct((128, d), F32), jax.ShapeDtypeStruct((128, d), BF16)),
        (p, masked),
        2 * 256 * d * width,
        after=after,
    )


def mix_kernel(own_ref, r_ref, near1, near2, near3, far, home):
    @pl.loop(0, own_ref.shape[1] // 512)
    def _(s):
        cols = pl.ds(pl.multiple_of(s * 512, 512), 512)
        total = (own_ref[:, cols] + r_ref[:, cols].astype(F32)).astype(BF16)
        home[:, cols] = total[0:16, :]
        far[:, cols] = total[16:32, :]
        near1[:, cols] = total[32:64, :]
        near2[:, cols] = total[64:96, :]
        near3[:, cols] = total[96:128, :]


def mix(own, received, after):
    d = own.shape[1]
    return call(
        mix_kernel,
        0,
        [jax.ShapeDtypeStruct((32, d), BF16)] * 3 + [jax.ShapeDtypeStruct((16, d), BF16)] * 2,
        (own, received),
        128 * d,
        after=after,
    )


def hop_kernel(near, received, out):
    @pl.loop(0, near.shape[1] // 512)
    def _(s):
        cols = pl.ds(pl.multiple_of(s * 512, 512), 512)
        out[:, cols] = (near[:, cols].astype(F32) + received[:, cols].astype(F32)).astype(BF16)


def hop_far_kernel(near, received, out):
    @pl.loop(0, near.shape[1] // 512)
    def _(s):
        cols = pl.ds(pl.multiple_of(s * 512, 512), 512)
        total = near[0:16, cols].astype(F32) + received[:, cols].astype(F32)
        out[0:16, cols] = total.astype(BF16)
        out[16:32, cols] = near[16:32, cols]


def hop(near, received, after):
    shape = jax.ShapeDtypeStruct(near.shape, BF16)
    kernel = hop_kernel if near.shape == received.shape else hop_far_kernel
    return call(kernel, 0, shape, (near, received), near.size, after=after)


def sum_kernel(*refs):
    halves, to_core, kept = (refs[0:2], refs[2:4]), refs[4], refs[5]

    @pl.loop(0, kept.shape[1] // 512)
    def _(s):
        cols = pl.ds(pl.multiple_of(s * 512, 512), 512)
        for q, (near, home) in enumerate(halves):
            rows = slice(q * 16, q * 16 + 16)
            kept[rows, cols] = home[:, cols].astype(F32) + near[0:16, cols].astype(F32)
            to_core[rows, cols] = near[16:32, cols]


def sum_core_kernel(kept, received, to_x, out):
    @pl.loop(0, kept.shape[1] // 512)
    def _(s):
        cols = pl.ds(pl.multiple_of(s * 512, 512), 512)
        total = kept[:, cols] + received[:, cols].astype(F32)
        out[:, cols] = total[0:16, :]
        to_x[:, cols] = total[16:32, :].astype(BF16)


def place_of(code):
    return (
        pl.multiple_of(code & 1023, BLOCK),
        pl.multiple_of((code >> 10) & 1023, 128),
        code >> 20,
    )


def wgrad_kernel(first, dest_ref, code_ref, odd_ref, pa, pb, x0, x1, x2, x3, *rest):
    outs, acc_ref = rest[:-1], rest[-1]
    left = lax.broadcasted_iota(jnp.int32, (BLOCK, 128), 1) < BLOCK
    over_rows = (((0,), (0,)), ((), ()))
    for n, out in enumerate(outs):
        dest = dest_ref[first + n]
        cols = pl.ds(pl.multiple_of(dest * 512, 512), 512)
        xa = jnp.concatenate([x0[:, cols], x2[:, cols]], axis=0)
        xb = jnp.concatenate([x1[:, cols], x3[:, cols]], axis=0)
        acc_ref[...] = lax.dot_general(
            xa, pa[...], over_rows, preferred_element_type=F32
        ) + lax.dot_general(xb, pb[...], over_rows, preferred_element_type=F32)

        def tiles(s):
            row, lane, h = place_of(code_ref[dest, s])
            row2, lane2, h2 = place_of(code_ref[dest, PAIRS + s])
            return (
                acc_ref[pl.ds(row, BLOCK), pl.ds(lane, 128)],
                acc_ref[pl.ds(row2, BLOCK), pl.ds(lane2, 128)],
                h & 1,
                h2 & 1,
            )

        def pack(s, carry):
            one, two, _, _ = tiles(s)
            out[s] = jnp.where(left, one, two).astype(BF16)
            return carry

        def repack(n, carry):
            s = PAIRS - 1 - n
            one, two, h, h2 = tiles(s)
            one = pltpu.roll(one, h * BLOCK, 1)
            two = pltpu.roll(two, (1 - h2) * BLOCK, 1)
            out[s] = jnp.where(left, one, two).astype(BF16)
            return carry

        lax.fori_loop(0, PAIRS, pack, 0, unroll=5)
        lax.fori_loop(0, odd_ref[dest], repack, 0)


def wgrad(first, count, scalars, pa, pb, xs, after):
    width = pa.shape[1]
    return call(
        functools.partial(wgrad_kernel, first),
        3,
        [jax.ShapeDtypeStruct((PAIRS, BLOCK, 128), BF16)] * count,
        (*scalars, pa, pb, *xs),
        2 * 512 * 512 * width * count,
        scratch=(pltpu.VMEM((512, width), F32),),
        after=after,
    )


def presum_kernel(*refs):
    parts, out = refs[:-1], refs[-1]

    @pl.loop(0, PAIRS)
    def _(s):
        total = parts[0][s].astype(F32)
        for part in parts[1:]:
            total = total + part[s].astype(F32)
        out[s] = total


def unpack_kernel(own_ref, code_ref, *refs):
    parts, (out, buf, sems) = refs[:-3], refs[-3:]
    own = own_ref[0]
    buf[...] = jnp.zeros_like(buf)
    half = lax.broadcasted_iota(jnp.int32, (BLOCK, 128), 1) // BLOCK

    def place(s, carry):
        total = parts[0][s]
        for part in parts[1:]:
            total = total + part[s].astype(F32)
        other = pltpu.roll(total, BLOCK, 1)
        for side in range(2):
            row, lane, h = place_of(code_ref[own, side * PAIRS + s])
            value = jnp.where(h == side, total, other)
            at = buf.at[pl.ds(row, BLOCK), pl.ds(lane, 128)]
            pltpu.store(at, value, mask=half == h)
        return carry

    lax.fori_loop(0, PAIRS, place, 0, unroll=5)
    copies = []
    for c in range(4):
        rows = slice(c * 128, (c + 1) * 128)
        copies.append(pltpu.make_async_copy(buf.at[rows], out.at[rows], sems.at[c]))
        copies[-1].start()
    for copy in copies:
        copy.wait()


def slots_of(block_mask, t):
    mask = lax.dynamic_slice(block_mask, (0, t * 14), (64, 14)).reshape(8, 112)
    kept = mask != 0
    at = jnp.arange(112, dtype=jnp.int32)
    h = jnp.array([b % 14 % 2 for b in range(112)], jnp.int32)
    before = (at[:, None] <= at[None, :]) & (h[:, None] == h[None, :])
    rank = jnp.dot(kept.astype(BF16), before.astype(BF16), preferred_element_type=F32)
    rank = rank.astype(jnp.int32) - 1
    extra = rank >= PAIRS
    slot = jnp.where(extra, 3 * PAIRS - 1 - PAIRS * h - rank, rank + PAIRS * h)
    odd = jnp.sum((kept & extra).astype(jnp.int32), axis=1, dtype=jnp.int32)
    return jnp.where(kept, slot, -1), odd


def codes_of(slot):
    i = jnp.array([b // 14 for b in range(112)], jnp.int32)
    j = jnp.array([b % 14 for b in range(112)], jnp.int32)
    hit = slot[:, None, :] == jnp.arange(CAP, dtype=jnp.int32)[None, :, None]
    code = i * BLOCK + (j >> 1) * (128 << 10) + (((j & 1) - 2) << 20)
    return jnp.sum(jnp.where(hit, code[None, None, :], 0), axis=2, dtype=jnp.int32) + (2 << 20)


def layer(tokens, weight, block_mask, act_grad):
    d, width = weight.shape
    t = lax.axis_index("tensor").astype(jnp.int32)
    g = lax.axis_index("dp").astype(jnp.int32)

    partner = move(tokens, dc=1)
    home = move(tokens, dx=1)
    chip = join(tokens, partner)
    t, g, chip = lax.optimization_barrier((t, g, chip))
    z, xh, core = t >> 2, (t >> 1) & 1, t & 1
    xl, y = g >> 2, g & 3

    n = jnp.arange(32, dtype=jnp.int32)
    slot = n & 7
    dist = jnp.where(slot == 0, 0, jnp.where(slot == 1, 4, slot >> 1))
    flip = jnp.where(slot > 1, slot & 1, 0)
    gather_core = core ^ ((n >> 3) & 1)
    zk = (z - (1 - 2 * gather_core) * dist) & (NZ - 1)
    idx = zk * 4 + (xh ^ (n >> 4)) * 2 + (gather_core ^ flip)
    order = [(1, 1), (0, 3), (1, 3), (0, 1), (1, 2), (1, 0), (0, 2), (0, 0)]
    dx = jnp.array([o[0] for o in order], jnp.int32)
    dy = jnp.array([o[1] for o in order], jnp.int32)
    dests = (xl ^ dx) * NY + ((y + dy) & (NY - 1))

    def tick():
        return call(tick_kernel, 0, jax.ShapeDtypeStruct((8, 128), F32), (), 0)

    ticks = [tick() for _ in range(4)]
    near1, near2 = move(chip, dz=1), move(chip, dz=2)
    t_slot, ticks[0] = lax.optimization_barrier((t, ticks[0]))
    slot, odd = slots_of(block_mask, t_slot)
    slot, odd, idx, dests, near1 = lax.optimization_barrier((slot, odd, idx, dests, near1))
    slot, ticks[1] = lax.optimization_barrier((slot, ticks[1]))
    code, near2 = lax.optimization_barrier((codes_of(slot), near2))
    scalars = (dests, code, odd)

    near3 = move(near2, dz=1)
    head = call(head_kernel, 0, jax.ShapeDtypeStruct((16, d), BF16), (near2,), 0)
    far = move(head, dz=2)
    t_mask, ticks[2] = lax.optimization_barrier((t, ticks[2]))
    masked = call(
        mask_kernel,
        1,
        jax.ShapeDtypeStruct((d, width), BF16),
        ((t_mask * 14).reshape(1), weight, block_mask),
        d * width,
        scratch=(
            pltpu.VMEM(block_mask.shape, jnp.int32),
            pltpu.VMEM((block_mask.shape[0], width), F32),
            pltpu.SemaphoreType.DMA((9,)),
        ),
        space=pl.BlockSpec(memory_space=pl.ANY),
        limit=44,
    )
    near3, masked = lax.optimization_barrier((near3, masked))

    cross = [move(v, dx=1) for v in (near1, near2, near3, far)]
    x0 = join(tokens, far, near1, near2, near3)
    x2 = move(x0, dc=1)
    x1 = join(home, cross[3], *cross[:3])
    x3 = move(x1, dc=1)
    xs = (x0, x1, x2, x3)

    grads = act_grad.reshape(32, 16, width)
    act_a, pa = forward(0, idx, x0, x2, masked, grads, after=ticks)
    own_a, other_a = xgrad(pa, masked)
    received_a = move(other_a, dc=1)
    act_b, pb = forward(16, idx, x1, x3, masked, grads, after=(other_a,))

    parts = []

    def pack(first, count, after):
        packed = wgrad(first, count, scalars, pa, pb, xs, (after,))
        for v, o in zip(packed, order[first : first + count]):
            parts.append(v if o == (0, 0) else move_dp(v, *o))
        return packed[0]

    def back(x):
        return move(x, dz=NZ - 1)

    done = pack(0, 1, other_a)
    done = pack(1, 2, done)
    a1, a2, a3, a4, home_a = mix(own_a, received_a, (done,))
    ring_a = back(a4)
    done = pack(3, 2, a4)
    done = hop(a3, ring_a, (done,))
    ring_a = back(done)
    own_b, other_b = xgrad(pb, masked, (done,))
    received_b = move(other_b, dc=1)
    done = pack(5, 2, other_b)
    b1, b2, b3, b4, home_b = mix(own_b, received_b, (done,))
    ring_b = back(b4)
    done = hop(a2, ring_a, (b4,))
    ring_a = back(done)
    done = hop(b3, ring_b, (done,))
    ring_b = back(done)
    done = hop(a1, ring_a, (done,))
    ring_a = back(done)
    done = hop(b2, ring_b, (done,))
    ring_b = back(done)
    done = pack(7, 1, done)
    done = hop(b1, ring_b, (done,))
    ring_b = back(done)
    order_after = jax.ShapeDtypeStruct((8, 128), F32)
    act, done = call(
        act_join_kernel,
        1,
        (jax.ShapeDtypeStruct((32, 16, width), BF16), order_after),
        (idx, act_a, act_b),
        0,
        after=(done,),
    )

    early = call(
        presum_kernel,
        0,
        jax.ShapeDtypeStruct((PAIRS, BLOCK, 128), F32),
        (parts[7], *parts[:4]),
        5 * CAP * 4096,
        after=(done,),
    )
    to_core, kept = call(
        sum_kernel,
        0,
        (jax.ShapeDtypeStruct((32, d), BF16), jax.ShapeDtypeStruct((32, d), F32)),
        (ring_a, home_a, ring_b, home_b),
        4 * 32 * d,
        after=(early,),
    )
    to_x, kept = call(
        sum_core_kernel,
        0,
        (jax.ShapeDtypeStruct((16, d), BF16), jax.ShapeDtypeStruct((16, d), F32)),
        (kept, move(to_core, dc=1)),
        32 * d,
    )
    x_grad, done = call(
        last_kernel,
        0,
        (jax.ShapeDtypeStruct((16, d), BF16), order_after),
        (kept, move(to_x, dx=1)),
        16 * d,
    )

    weight_grad = call(
        unpack_kernel,
        2,
        jax.ShapeDtypeStruct((512, width), F32),
        (g.reshape(1), code, early, *parts[4:7]),
        8 * CAP * 4096,
        scratch=(
            pltpu.VMEM((512, width), F32),
            pltpu.SemaphoreType.DMA((4,)),
        ),
        after=(done,),
        out_space=pl.BlockSpec(memory_space=pl.ANY),
    )
    return (act.reshape(512, width), x_grad, weight_grad)


def solution(mesh):
    return jax.shard_map(
        layer,
        mesh=mesh,
        in_specs=(P(("dp", "tensor"), None), P(None, "tensor"), P(), P("dp", "tensor")),
        out_specs=(P("dp", "tensor"), P(("dp", "tensor"), None), P("dp", "tensor")),
        check_vma=False,
    )
```

```python
import functools

import jax
import jax.numpy as jnp
from jax import lax
from jax.experimental import pallas as pl
from jax.experimental.pallas import tpu as pltpu
from jax.sharding import PartitionSpec as P


BLOCK = 64
CAP = 70
PAIRS = CAP // 2
NZ = 8
NY = 4
F32 = jnp.float32
BF16 = jnp.bfloat16


VMEM = pl.BlockSpec(memory_space=pltpu.VMEM)
SMEM = pl.BlockSpec(memory_space=pltpu.SMEM)


def tensor_perm(dz, dx, dc, split=False):
    pairs = []
    for z in range(NZ):
        for xh in range(2):
            for core in range(2):
                shift = -dz if split and core else dz
                source = (z * 2 + xh) * 2 + core
                target = (((z + shift) % NZ) * 2 + (xh ^ dx)) * 2 + (core ^ dc)
                pairs.append((source, target))
    return pairs


def dp_perm(dx, dy):
    return [
        (xl * NY + y, (xl ^ dx) * NY + (y + dy) % NY) for xl in range(2) for y in range(NY)
    ]


def move(x, dz=0, dx=0, dc=0):
    return lax.ppermute(x, "tensor", tensor_perm(dz, dx, dc, split=True))


def move_dp(x, dx, dy):
    return lax.ppermute(x, "dp", dp_perm(dx, dy))


def call(
    kernel, n_scalar, out_shape, args, flops, scratch=(), after=(), limit=12, out_space=VMEM,
    space=VMEM,
):
    n_args, n_after = len(args), len(after)

    def run(*refs):
        kernel(*refs[:n_args], *refs[n_args + n_after :])

    n_out = len(out_shape) if isinstance(out_shape, (tuple, list)) else 1
    out_specs = [VMEM] * n_out if isinstance(out_shape, (tuple, list)) else out_space
    moved = sum(a.size * a.dtype.itemsize for a in args)
    return pl.pallas_call(
        run,
        out_shape=out_shape,
        in_specs=[SMEM] * n_scalar
        + [space] * (n_args - n_scalar)
        + [pl.BlockSpec(memory_space=pl.ANY)] * n_after,
        out_specs=out_specs,
        scratch_shapes=list(scratch),
        compiler_params=pltpu.CompilerParams(vmem_limit_bytes=limit << 20),
        cost_estimate=pl.CostEstimate(flops=flops, bytes_accessed=moved, transcendentals=0),
    )(*args, *after)


def tick_kernel(*refs):
    refs[-1][...] = jnp.zeros_like(refs[-1])


def join_kernel(*refs):
    parts, out = refs[:-1], refs[-1]
    at = 0
    for part in parts:
        out[at : at + part.shape[0], :] = part[...]
        at += part.shape[0]


def join(*parts):
    rows = sum(part.shape[0] for part in parts)
    shape = jax.ShapeDtypeStruct((rows, parts[0].shape[1]), BF16)
    return call(join_kernel, 0, shape, parts, 0)


def head_kernel(x_ref, o_ref):
    o_ref[...] = x_ref[0 : o_ref.shape[0], :]


def mask_kernel(t_ref, w_hbm, m_hbm, o_ref, m_ref, e_ref, sems):
    n_rows, blocks = m_ref.shape
    width = o_ref.shape[1]
    groups = n_rows // 8

    def part(g):
        rows = pl.ds(pl.multiple_of(g * 512, 512), 512)
        return pltpu.make_async_copy(w_hbm.at[rows], o_ref.at[rows], sems.at[g])

    mask_copy = pltpu.make_async_copy(m_hbm, m_ref, sems.at[groups])
    mask_copy.start()
    for g in range(groups):
        part(g).start()
    rows = lax.broadcasted_iota(jnp.int32, (blocks, width), 0)
    cols = lax.broadcasted_iota(jnp.int32, (blocks, width), 1)
    pick = (rows == t_ref[0] + lax.div(cols, BLOCK)).astype(BF16)
    mask_copy.wait()
    e_ref[...] = jnp.dot(m_ref[...].astype(F32).astype(BF16), pick, preferred_element_type=F32)

    @pl.loop(0, groups)
    def _(g):
        part(g).wait()
        eight = e_ref[pl.ds(pl.multiple_of(g * 8, 8), 8), :]
        for i in range(8):
            at = pl.ds(pl.multiple_of(g * 512 + i * BLOCK, BLOCK), BLOCK)
            row = jnp.broadcast_to(eight[i : i + 1, :], (BLOCK, width)).astype(BF16)
            o_ref[at, :] = o_ref[at, :] * row


def forward_kernel(first, idx_ref, xa, xb, w_ref, g_ref, act_ref, p_ref, acc_ref):
    d = w_ref.shape[0]
    kb = 1024

    def product(s):
        cols = pl.ds(pl.multiple_of(s * kb, kb), kb)
        x = jnp.concatenate([xa[:, cols], xb[:, cols]], axis=0)
        return jnp.dot(x, w_ref[cols, :], preferred_element_type=F32)

    acc_ref[...] = product(0)

    @pl.loop(1, d // kb)
    def _(s):
        acc_ref[...] += product(s)

    def finish(n, carry):
        rows = pl.ds(pl.multiple_of(n * 16, 16), 16)
        pre = acc_ref[rows, :]
        s = jax.nn.sigmoid(pre)
        act_ref[n] = (pre * s).astype(BF16)
        grad = g_ref[idx_ref[first + n]].astype(F32) * s * (1.0 + pre * (1.0 - s))
        p_ref[rows, :] = grad.astype(BF16)
        return carry

    lax.fori_loop(0, act_ref.shape[0], finish, 0, unroll=2)


def forward(first, idx, xa, xb, masked, act_grad, after=()):
    d, width = masked.shape
    return call(
        functools.partial(forward_kernel, first),
        1,
        (
            jax.ShapeDtypeStruct((16, 16, width), BF16),
            jax.ShapeDtypeStruct((256, width), BF16),
        ),
        (idx, xa, xb, masked, act_grad),
        2 * 256 * d * width,
        scratch=(pltpu.VMEM((256, width), F32),),
        after=after,
    )


def act_join_kernel(idx_ref, a_ref, b_ref, out, tick):
    tick[...] = jnp.zeros_like(tick)

    @pl.loop(0, 16)
    def _(n):
        out[idx_ref[n]] = a_ref[n]
        out[idx_ref[16 + n]] = b_ref[n]


def last_kernel(kept, received, out, tick):
    tick[...] = jnp.zeros_like(tick)
    out[...] = (kept[...] + received[...].astype(F32)).astype(BF16)


def xgrad_kernel(p_ref, w_ref, own_ref, other_ref):
    @pl.loop(0, w_ref.shape[0] // 512)
    def _(s):
        cols = pl.ds(pl.multiple_of(s * 512, 512), 512)
        part = lax.dot_general(
            p_ref[...], w_ref[cols, :], (((1,), (1,)), ((), ())), preferred_element_type=F32
        )
        own_ref[:, cols] = part[:128, :]
        other_ref[:, cols] = part[128:, :].astype(BF16)


def xgrad(p, masked, after=()):
    d, width = masked.shape
    return call(
        xgrad_kernel,
        0,
        (jax.ShapeDtypeStruct((128, d), F32), jax.ShapeDtypeStruct((128, d), BF16)),
        (p, masked),
        2 * 256 * d * width,
        after=after,
    )


def mix_kernel(own_ref, r_ref, near1, near2, near3, far, home):
    @pl.loop(0, own_ref.shape[1] // 512)
    def _(s):
        cols = pl.ds(pl.multiple_of(s * 512, 512), 512)
        total = (own_ref[:, cols] + r_ref[:, cols].astype(F32)).astype(BF16)
        home[:, cols] = total[0:16, :]
        far[:, cols] = total[16:32, :]
        near1[:, cols] = total[32:64, :]
        near2[:, cols] = total[64:96, :]
        near3[:, cols] = total[96:128, :]


def mix(own, received, after):
    d = own.shape[1]
    return call(
        mix_kernel,
        0,
        [jax.ShapeDtypeStruct((32, d), BF16)] * 3 + [jax.ShapeDtypeStruct((16, d), BF16)] * 2,
        (own, received),
        128 * d,
        after=after,
    )


def hop_kernel(near, one, two, out):
    @pl.loop(0, near.shape[1] // 512)
    def _(s):
        cols = pl.ds(pl.multiple_of(s * 512, 512), 512)
        total = near[:, cols].astype(F32) + one[:, cols].astype(F32)
        out[0:16, cols] = (total[0:16] + two[:, cols].astype(F32)).astype(BF16)
        out[16:32, cols] = total[16:32].astype(BF16)


def hop(near, one, two, after):
    shape = jax.ShapeDtypeStruct(near.shape, BF16)
    return call(hop_kernel, 0, shape, (near, one, two), 2 * near.size, after=after)


def sum_kernel(*refs):
    halves, to_core, kept = (refs[0:3], refs[3:6]), refs[6], refs[7]

    @pl.loop(0, kept.shape[1] // 512)
    def _(s):
        cols = pl.ds(pl.multiple_of(s * 512, 512), 512)
        for q, (one, two, home) in enumerate(halves):
            rows = slice(q * 16, q * 16 + 16)
            total = one[:, cols].astype(F32) + two[:, cols].astype(F32)
            kept[rows, cols] = home[:, cols].astype(F32) + total[0:16]
            to_core[rows, cols] = total[16:32].astype(BF16)


def sum_core_kernel(kept, received, to_x, out):
    @pl.loop(0, kept.shape[1] // 512)
    def _(s):
        cols = pl.ds(pl.multiple_of(s * 512, 512), 512)
        total = kept[:, cols] + received[:, cols].astype(F32)
        out[:, cols] = total[0:16, :]
        to_x[:, cols] = total[16:32, :].astype(BF16)


def place_of(code):
    return (
        pl.multiple_of(code & 1023, BLOCK),
        pl.multiple_of((code >> 10) & 1023, 128),
        code >> 20,
    )


def wgrad_kernel(first, dest_ref, code_ref, odd_ref, pa, pb, x0, x1, x2, x3, *rest):
    outs, acc_ref = rest[:-1], rest[-1]
    left = lax.broadcasted_iota(jnp.int32, (BLOCK, 128), 1) < BLOCK
    over_rows = (((0,), (0,)), ((), ()))
    for n, out in enumerate(outs):
        dest = dest_ref[first + n]
        cols = pl.ds(pl.multiple_of(dest * 512, 512), 512)
        xa = jnp.concatenate([x0[:, cols], x2[:, cols]], axis=0)
        xb = jnp.concatenate([x1[:, cols], x3[:, cols]], axis=0)
        acc_ref[...] = lax.dot_general(
            xa, pa[...], over_rows, preferred_element_type=F32
        ) + lax.dot_general(xb, pb[...], over_rows, preferred_element_type=F32)

        def tiles(s):
            row, lane, h = place_of(code_ref[dest, s])
            row2, lane2, h2 = place_of(code_ref[dest, PAIRS + s])
            return (
                acc_ref[pl.ds(row, BLOCK), pl.ds(lane, 128)],
                acc_ref[pl.ds(row2, BLOCK), pl.ds(lane2, 128)],
                h & 1,
                h2 & 1,
            )

        def pack(s, carry):
            one, two, _, _ = tiles(s)
            out[s] = jnp.where(left, one, two).astype(BF16)
            return carry

        def repack(n, carry):
            s = PAIRS - 1 - n
            one, two, h, h2 = tiles(s)
            one = pltpu.roll(one, h * BLOCK, 1)
            two = pltpu.roll(two, (1 - h2) * BLOCK, 1)
            out[s] = jnp.where(left, one, two).astype(BF16)
            return carry

        lax.fori_loop(0, PAIRS, pack, 0, unroll=5)
        lax.fori_loop(0, odd_ref[dest], repack, 0)


def wgrad(first, count, scalars, pa, pb, xs, after):
    width = pa.shape[1]
    return call(
        functools.partial(wgrad_kernel, first),
        3,
        [jax.ShapeDtypeStruct((PAIRS, BLOCK, 128), BF16)] * count,
        (*scalars, pa, pb, *xs),
        2 * 512 * 512 * width * count,
        scratch=(pltpu.VMEM((512, width), F32),),
        after=after,
    )


def presum_kernel(*refs):
    parts, out = refs[:-1], refs[-1]

    @pl.loop(0, PAIRS)
    def _(s):
        total = parts[0][s].astype(F32)
        for part in parts[1:]:
            total = total + part[s].astype(F32)
        out[s] = total


def unpack_kernel(own_ref, code_ref, *refs):
    parts, (out, buf, sems) = refs[:-3], refs[-3:]
    own = own_ref[0]
    buf[...] = jnp.zeros_like(buf)
    half = lax.broadcasted_iota(jnp.int32, (BLOCK, 128), 1) // BLOCK

    def place(s, carry):
        total = parts[0][s]
        for part in parts[1:]:
            total = total + part[s].astype(F32)
        other = pltpu.roll(total, BLOCK, 1)
        for side in range(2):
            row, lane, h = place_of(code_ref[own, side * PAIRS + s])
            value = jnp.where(h == side, total, other)
            at = buf.at[pl.ds(row, BLOCK), pl.ds(lane, 128)]
            pltpu.store(at, value, mask=half == h)
        return carry

    lax.fori_loop(0, PAIRS, place, 0, unroll=5)
    copies = []
    for c in range(4):
        rows = slice(c * 128, (c + 1) * 128)
        copies.append(pltpu.make_async_copy(buf.at[rows], out.at[rows], sems.at[c]))
        copies[-1].start()
    for copy in copies:
        copy.wait()


def slots_of(block_mask, t):
    mask = lax.dynamic_slice(block_mask, (0, t * 14), (64, 14)).reshape(8, 112)
    kept = mask != 0
    at = jnp.arange(112, dtype=jnp.int32)
    h = jnp.array([b % 14 % 2 for b in range(112)], jnp.int32)
    before = (at[:, None] <= at[None, :]) & (h[:, None] == h[None, :])
    rank = jnp.dot(kept.astype(BF16), before.astype(BF16), preferred_element_type=F32)
    rank = rank.astype(jnp.int32) - 1
    extra = rank >= PAIRS
    slot = jnp.where(extra, 3 * PAIRS - 1 - PAIRS * h - rank, rank + PAIRS * h)
    odd = jnp.sum((kept & extra).astype(jnp.int32), axis=1, dtype=jnp.int32)
    return jnp.where(kept, slot, -1), odd


def codes_of(slot):
    i = jnp.array([b // 14 for b in range(112)], jnp.int32)
    j = jnp.array([b % 14 for b in range(112)], jnp.int32)
    hit = slot[:, None, :] == jnp.arange(CAP, dtype=jnp.int32)[None, :, None]
    code = i * BLOCK + (j >> 1) * (128 << 10) + (((j & 1) - 2) << 20)
    return jnp.sum(jnp.where(hit, code[None, None, :], 0), axis=2, dtype=jnp.int32) + (2 << 20)


def layer(tokens, weight, block_mask, act_grad):
    d, width = weight.shape
    t = lax.axis_index("tensor").astype(jnp.int32)
    g = lax.axis_index("dp").astype(jnp.int32)

    partner = move(tokens, dc=1)
    home = move(tokens, dx=1)
    chip = join(tokens, partner)
    t, g, chip = lax.optimization_barrier((t, g, chip))
    z, xh, core = t >> 2, (t >> 1) & 1, t & 1
    xl, y = g >> 2, g & 3

    n = jnp.arange(32, dtype=jnp.int32)
    slot = n & 7
    dist = jnp.where(slot == 0, 0, jnp.where(slot == 1, 4, slot >> 1))
    flip = jnp.where(slot > 1, slot & 1, 0)
    gather_core = core ^ ((n >> 3) & 1)
    zk = (z - (1 - 2 * gather_core) * dist) & (NZ - 1)
    idx = zk * 4 + (xh ^ (n >> 4)) * 2 + (gather_core ^ flip)
    order = [(1, 1), (0, 3), (1, 2), (1, 3), (0, 1), (1, 0), (0, 2), (0, 0)]
    dx = jnp.array([o[0] for o in order], jnp.int32)
    dy = jnp.array([o[1] for o in order], jnp.int32)
    dests = (xl ^ dx) * NY + ((y + dy) & (NY - 1))

    def tick():
        return call(tick_kernel, 0, jax.ShapeDtypeStruct((8, 128), F32), (), 0)

    ticks = [tick() for _ in range(4)]
    near1, near2 = move(chip, dz=1), move(chip, dz=2)
    t_slot, ticks[0] = lax.optimization_barrier((t, ticks[0]))
    slot, odd = slots_of(block_mask, t_slot)
    slot, odd, idx, dests, near1 = lax.optimization_barrier((slot, odd, idx, dests, near1))
    slot, ticks[1] = lax.optimization_barrier((slot, ticks[1]))
    code, near2 = lax.optimization_barrier((codes_of(slot), near2))
    scalars = (dests, code, odd)

    near3 = move(near2, dz=1)
    head = call(head_kernel, 0, jax.ShapeDtypeStruct((16, d), BF16), (near2,), 0)
    far = move(head, dz=2)
    t_mask, ticks[2] = lax.optimization_barrier((t, ticks[2]))
    masked = call(
        mask_kernel,
        1,
        jax.ShapeDtypeStruct((d, width), BF16),
        ((t_mask * 14).reshape(1), weight, block_mask),
        d * width,
        scratch=(
            pltpu.VMEM(block_mask.shape, jnp.int32),
            pltpu.VMEM((block_mask.shape[0], width), F32),
            pltpu.SemaphoreType.DMA((9,)),
        ),
        space=pl.BlockSpec(memory_space=pl.ANY),
        limit=44,
    )
    near3, masked = lax.optimization_barrier((near3, masked))

    cross = [move(v, dx=1) for v in (near1, near2, near3, far)]
    x0 = join(tokens, far, near1, near2, near3)
    x2 = move(x0, dc=1)
    x1 = join(home, cross[3], *cross[:3])
    x3 = move(x1, dc=1)
    xs = (x0, x1, x2, x3)

    grads = act_grad.reshape(32, 16, width)
    act_a, pa = forward(0, idx, x0, x2, masked, grads, after=ticks)
    own_a, other_a = xgrad(pa, masked)
    received_a = move(other_a, dc=1)
    act_b, pb = forward(16, idx, x1, x3, masked, grads, after=(other_a,))

    parts = []

    def pack(first, count, after):
        packed = wgrad(first, count, scalars, pa, pb, xs, (after,))
        for v, o in zip(packed, order[first : first + count]):
            parts.append(v if o == (0, 0) else move_dp(v, *o))
        return packed[0]

    def back(x, hops):
        return move(x, dz=NZ - hops)

    done = pack(0, 1, other_a)
    done = pack(1, 2, done)
    a1, a2, a3, a4, home_a = mix(own_a, received_a, (done,))
    from_a3, from_a4 = back(a3, 1), back(a4, 2)
    own_b, other_b = xgrad(pb, masked, (a4,))
    received_b = move(other_b, dc=1)
    done = pack(3, 2, other_b)
    b1, b2, b3, b4, home_b = mix(own_b, received_b, (done,))
    from_b3, from_b4, from_b1 = back(b3, 1), back(b4, 2), back(b1, 1)
    done = hop(a2, from_a3, from_a4, (b4,))
    from_a2 = back(done, 2)
    done = pack(5, 2, done)
    done = hop(b2, from_b3, from_b4, (done,))
    a1, done = lax.optimization_barrier((a1, done))
    from_b2, from_a1 = back(done, 2), back(a1, 1)
    done = pack(7, 1, done)
    order_after = jax.ShapeDtypeStruct((8, 128), F32)
    act, done = call(
        act_join_kernel,
        1,
        (jax.ShapeDtypeStruct((32, 16, width), BF16), order_after),
        (idx, act_a, act_b),
        0,
        after=(done,),
    )

    early = call(
        presum_kernel,
        0,
        jax.ShapeDtypeStruct((PAIRS, BLOCK, 128), F32),
        (parts[7], *parts[:4]),
        5 * CAP * 4096,
        after=(done,),
    )
    to_core, kept = call(
        sum_kernel,
        0,
        (jax.ShapeDtypeStruct((32, d), BF16), jax.ShapeDtypeStruct((32, d), F32)),
        (from_a1, from_a2, home_a, from_b1, from_b2, home_b),
        6 * 32 * d,
    )
    to_x, kept = call(
        sum_core_kernel,
        0,
        (jax.ShapeDtypeStruct((16, d), BF16), jax.ShapeDtypeStruct((16, d), F32)),
        (kept, move(to_core, dc=1)),
        32 * d,
    )
    x_grad, done = call(
        last_kernel,
        0,
        (jax.ShapeDtypeStruct((16, d), BF16), order_after),
        (kept, move(to_x, dx=1)),
        16 * d,
    )

    weight_grad = call(
        unpack_kernel,
        2,
        jax.ShapeDtypeStruct((512, width), F32),
        (g.reshape(1), code, early, *parts[4:7]),
        8 * CAP * 4096,
        scratch=(
            pltpu.VMEM((512, width), F32),
            pltpu.SemaphoreType.DMA((4,)),
        ),
        after=(done,),
        out_space=pl.BlockSpec(memory_space=pl.ANY),
    )
    return (act.reshape(512, width), x_grad, weight_grad)


def solution(mesh):
    return jax.shard_map(
        layer,
        mesh=mesh,
        in_specs=(P(("dp", "tensor"), None), P(None, "tensor"), P(), P("dp", "tensor")),
        out_specs=(P("dp", "tensor"), P(("dp", "tensor"), None), P("dp", "tensor")),
        check_vma=False,
    )
```

```python
import functools

import jax
import jax.numpy as jnp
from jax import lax
from jax.experimental import pallas as pl
from jax.experimental.pallas import tpu as pltpu
from jax.sharding import PartitionSpec as P


BLOCK = 64
CAP = 70
PAIRS = CAP // 2
NZ = 8
NY = 4
F32 = jnp.float32
BF16 = jnp.bfloat16


VMEM = pl.BlockSpec(memory_space=pltpu.VMEM)
SMEM = pl.BlockSpec(memory_space=pltpu.SMEM)


def tensor_perm(dz, dx, dc, split=False):
    pairs = []
    for z in range(NZ):
        for xh in range(2):
            for core in range(2):
                shift = -dz if split and core else dz
                source = (z * 2 + xh) * 2 + core
                target = (((z + shift) % NZ) * 2 + (xh ^ dx)) * 2 + (core ^ dc)
                pairs.append((source, target))
    return pairs


def dp_perm(dx, dy):
    return [
        (xl * NY + y, (xl ^ dx) * NY + (y + dy) % NY) for xl in range(2) for y in range(NY)
    ]


def move(x, dz=0, dx=0, dc=0):
    return lax.ppermute(x, "tensor", tensor_perm(dz, dx, dc, split=True))


def move_dp(x, dx, dy):
    return lax.ppermute(x, "dp", dp_perm(dx, dy))


def call(
    kernel, n_scalar, out_shape, args, flops, scratch=(), after=(), limit=12, out_space=VMEM,
    space=VMEM,
):
    n_args, n_after = len(args), len(after)

    def run(*refs):
        kernel(*refs[:n_args], *refs[n_args + n_after :])

    n_out = len(out_shape) if isinstance(out_shape, (tuple, list)) else 1
    out_specs = [VMEM] * n_out if isinstance(out_shape, (tuple, list)) else out_space
    moved = sum(a.size * a.dtype.itemsize for a in args)
    return pl.pallas_call(
        run,
        out_shape=out_shape,
        in_specs=[SMEM] * n_scalar
        + [space] * (n_args - n_scalar)
        + [pl.BlockSpec(memory_space=pl.ANY)] * n_after,
        out_specs=out_specs,
        scratch_shapes=list(scratch),
        compiler_params=pltpu.CompilerParams(vmem_limit_bytes=limit << 20),
        cost_estimate=pl.CostEstimate(flops=flops, bytes_accessed=moved, transcendentals=0),
    )(*args, *after)


def tick_kernel(*refs):
    refs[-1][...] = jnp.zeros_like(refs[-1])


def join_kernel(*refs):
    parts, out = refs[:-1], refs[-1]
    at = 0
    for part in parts:
        out[at : at + part.shape[0], :] = part[...]
        at += part.shape[0]


def join(*parts):
    rows = sum(part.shape[0] for part in parts)
    shape = jax.ShapeDtypeStruct((rows, parts[0].shape[1]), BF16)
    return call(join_kernel, 0, shape, parts, 0)


def head_kernel(x_ref, o_ref):
    o_ref[...] = x_ref[0 : o_ref.shape[0], :]


def mask_kernel(t_ref, w_hbm, m_hbm, o_ref, m_ref, e_ref, sems):
    n_rows, blocks = m_ref.shape
    width = o_ref.shape[1]
    groups = n_rows // 8

    def part(g):
        rows = pl.ds(pl.multiple_of(g * 512, 512), 512)
        return pltpu.make_async_copy(w_hbm.at[rows], o_ref.at[rows], sems.at[g])

    mask_copy = pltpu.make_async_copy(m_hbm, m_ref, sems.at[groups])
    mask_copy.start()
    for g in range(groups):
        part(g).start()
    rows = lax.broadcasted_iota(jnp.int32, (blocks, width), 0)
    cols = lax.broadcasted_iota(jnp.int32, (blocks, width), 1)
    pick = (rows == t_ref[0] + lax.div(cols, BLOCK)).astype(BF16)
    mask_copy.wait()
    e_ref[...] = jnp.dot(m_ref[...].astype(F32).astype(BF16), pick, preferred_element_type=F32)

    @pl.loop(0, groups)
    def _(g):
        part(g).wait()
        eight = e_ref[pl.ds(pl.multiple_of(g * 8, 8), 8), :]
        for i in range(8):
            at = pl.ds(pl.multiple_of(g * 512 + i * BLOCK, BLOCK), BLOCK)
            row = jnp.broadcast_to(eight[i : i + 1, :], (BLOCK, width)).astype(BF16)
            o_ref[at, :] = o_ref[at, :] * row


def forward_kernel(first, idx_ref, xa, xb, w_ref, g_ref, act_ref, p_ref, acc_ref):
    d = w_ref.shape[0]
    kb = 1024

    def product(s):
        cols = pl.ds(pl.multiple_of(s * kb, kb), kb)
        x = jnp.concatenate([xa[:, cols], xb[:, cols]], axis=0)
        return jnp.dot(x, w_ref[cols, :], preferred_element_type=F32)

    acc_ref[...] = product(0)

    @pl.loop(1, d // kb)
    def _(s):
        acc_ref[...] += product(s)

    def finish(n, carry):
        rows = pl.ds(pl.multiple_of(n * 16, 16), 16)
        pre = acc_ref[rows, :]
        s = jax.nn.sigmoid(pre)
        act_ref[n] = (pre * s).astype(BF16)
        grad = g_ref[idx_ref[first + n]].astype(F32) * s * (1.0 + pre * (1.0 - s))
        p_ref[rows, :] = grad.astype(BF16)
        return carry

    lax.fori_loop(0, act_ref.shape[0], finish, 0, unroll=2)


def forward(first, idx, xa, xb, masked, act_grad, after=()):
    d, width = masked.shape
    return call(
        functools.partial(forward_kernel, first),
        1,
        (
            jax.ShapeDtypeStruct((16, 16, width), BF16),
            jax.ShapeDtypeStruct((256, width), BF16),
        ),
        (idx, xa, xb, masked, act_grad),
        2 * 256 * d * width,
        scratch=(pltpu.VMEM((256, width), F32),),
        after=after,
    )


def act_join_kernel(idx_ref, a_ref, b_ref, out, tick):
    tick[...] = jnp.zeros_like(tick)

    @pl.loop(0, 16)
    def _(n):
        out[idx_ref[n]] = a_ref[n]
        out[idx_ref[16 + n]] = b_ref[n]


def last_kernel(kept, received, out):
    out[...] = (kept[...] + received[...].astype(F32)).astype(BF16)


def xgrad_kernel(p_ref, w_ref, own_ref, other_ref):
    @pl.loop(0, w_ref.shape[0] // 512)
    def _(s):
        cols = pl.ds(pl.multiple_of(s * 512, 512), 512)
        part = lax.dot_general(
            p_ref[...], w_ref[cols, :], (((1,), (1,)), ((), ())), preferred_element_type=F32
        )
        own_ref[:, cols] = part[:128, :]
        other_ref[:, cols] = part[128:, :].astype(BF16)


def xgrad(p, masked, after=()):
    d, width = masked.shape
    return call(
        xgrad_kernel,
        0,
        (jax.ShapeDtypeStruct((128, d), F32), jax.ShapeDtypeStruct((128, d), BF16)),
        (p, masked),
        2 * 256 * d * width,
        after=after,
    )


def mix_kernel(own_ref, r_ref, near1, near2, near3, far, home):
    @pl.loop(0, own_ref.shape[1] // 512)
    def _(s):
        cols = pl.ds(pl.multiple_of(s * 512, 512), 512)
        total = (own_ref[:, cols] + r_ref[:, cols].astype(F32)).astype(BF16)
        home[:, cols] = total[0:16, :]
        far[:, cols] = total[16:32, :]
        near1[:, cols] = total[32:64, :]
        near2[:, cols] = total[64:96, :]
        near3[:, cols] = total[96:128, :]


def mix(own, received, after):
    d = own.shape[1]
    return call(
        mix_kernel,
        0,
        [jax.ShapeDtypeStruct((32, d), BF16)] * 3 + [jax.ShapeDtypeStruct((16, d), BF16)] * 2,
        (own, received),
        128 * d,
        after=after,
    )


def hop_kernel(near, one, two, out):
    @pl.loop(0, near.shape[1] // 512)
    def _(s):
        cols = pl.ds(pl.multiple_of(s * 512, 512), 512)
        total = near[:, cols].astype(F32) + one[:, cols].astype(F32)
        out[0:16, cols] = (total[0:16] + two[:, cols].astype(F32)).astype(BF16)
        out[16:32, cols] = total[16:32].astype(BF16)


def hop(near, one, two, after):
    shape = jax.ShapeDtypeStruct(near.shape, BF16)
    return call(hop_kernel, 0, shape, (near, one, two), 2 * near.size, after=after)


def sum_kernel(*refs):
    halves, to_core, kept = (refs[0:3], refs[3:6]), refs[6], refs[7]

    @pl.loop(0, kept.shape[1] // 512)
    def _(s):
        cols = pl.ds(pl.multiple_of(s * 512, 512), 512)
        for q, (one, two, home) in enumerate(halves):
            rows = slice(q * 16, q * 16 + 16)
            total = one[:, cols].astype(F32) + two[:, cols].astype(F32)
            kept[rows, cols] = home[:, cols].astype(F32) + total[0:16]
            to_core[rows, cols] = total[16:32].astype(BF16)


def sum_core_kernel(kept, received, to_x, out):
    @pl.loop(0, kept.shape[1] // 512)
    def _(s):
        cols = pl.ds(pl.multiple_of(s * 512, 512), 512)
        total = kept[:, cols] + received[:, cols].astype(F32)
        out[:, cols] = total[0:16, :]
        to_x[:, cols] = total[16:32, :].astype(BF16)


def place_of(code):
    return (
        pl.multiple_of(code & 1023, BLOCK),
        pl.multiple_of((code >> 10) & 1023, 128),
        code >> 20,
    )


def wgrad_kernel(first, dest_ref, code_ref, odd_ref, pa, pb, x0, x1, x2, x3, *rest):
    outs, acc_ref = rest[:-1], rest[-1]
    left = lax.broadcasted_iota(jnp.int32, (BLOCK, 128), 1) < BLOCK
    over_rows = (((0,), (0,)), ((), ()))
    for n, out in enumerate(outs):
        dest = dest_ref[first + n]
        cols = pl.ds(pl.multiple_of(dest * 512, 512), 512)
        xa = jnp.concatenate([x0[:, cols], x2[:, cols]], axis=0)
        xb = jnp.concatenate([x1[:, cols], x3[:, cols]], axis=0)
        acc_ref[...] = lax.dot_general(
            xa, pa[...], over_rows, preferred_element_type=F32
        ) + lax.dot_general(xb, pb[...], over_rows, preferred_element_type=F32)

        def tiles(s):
            row, lane, h = place_of(code_ref[dest, s])
            row2, lane2, h2 = place_of(code_ref[dest, PAIRS + s])
            return (
                acc_ref[pl.ds(row, BLOCK), pl.ds(lane, 128)],
                acc_ref[pl.ds(row2, BLOCK), pl.ds(lane2, 128)],
                h & 1,
                h2 & 1,
            )

        def pack(s, carry):
            one, two, _, _ = tiles(s)
            out[s] = jnp.where(left, one, two).astype(BF16)
            return carry

        def repack(n, carry):
            s = PAIRS - 1 - n
            one, two, h, h2 = tiles(s)
            one = pltpu.roll(one, h * BLOCK, 1)
            two = pltpu.roll(two, (1 - h2) * BLOCK, 1)
            out[s] = jnp.where(left, one, two).astype(BF16)
            return carry

        lax.fori_loop(0, PAIRS, pack, 0, unroll=5)
        lax.fori_loop(0, odd_ref[dest], repack, 0)


def wgrad(first, count, scalars, pa, pb, xs, after):
    width = pa.shape[1]
    return call(
        functools.partial(wgrad_kernel, first),
        3,
        [jax.ShapeDtypeStruct((PAIRS, BLOCK, 128), BF16)] * count,
        (*scalars, pa, pb, *xs),
        2 * 512 * 512 * width * count,
        scratch=(pltpu.VMEM((512, width), F32),),
        after=after,
    )


def presum_kernel(*refs):
    parts, out = refs[:-1], refs[-1]

    @pl.loop(0, PAIRS)
    def _(s):
        total = parts[0][s].astype(F32)
        for part in parts[1:]:
            total = total + part[s].astype(F32)
        out[s] = total


def unpack_kernel(own_ref, code_ref, *refs):
    parts, (out, buf, sems) = refs[:-3], refs[-3:]
    own = own_ref[0]
    buf[...] = jnp.zeros_like(buf)
    half = lax.broadcasted_iota(jnp.int32, (BLOCK, 128), 1) // BLOCK

    def place(s, carry):
        total = parts[0][s]
        for part in parts[1:]:
            total = total + part[s].astype(F32)
        other = pltpu.roll(total, BLOCK, 1)
        for side in range(2):
            row, lane, h = place_of(code_ref[own, side * PAIRS + s])
            value = jnp.where(h == side, total, other)
            at = buf.at[pl.ds(row, BLOCK), pl.ds(lane, 128)]
            pltpu.store(at, value, mask=half == h)
        return carry

    lax.fori_loop(0, PAIRS, place, 0, unroll=5)
    copies = []
    for c in range(4):
        rows = slice(c * 128, (c + 1) * 128)
        copies.append(pltpu.make_async_copy(buf.at[rows], out.at[rows], sems.at[c]))
        copies[-1].start()
    for copy in copies:
        copy.wait()


def slots_of(block_mask, t):
    mask = lax.dynamic_slice(block_mask, (0, t * 14), (64, 14)).reshape(8, 112)
    kept = mask != 0
    at = jnp.arange(112, dtype=jnp.int32)
    h = jnp.array([b % 14 % 2 for b in range(112)], jnp.int32)
    before = (at[:, None] <= at[None, :]) & (h[:, None] == h[None, :])
    rank = jnp.dot(kept.astype(BF16), before.astype(BF16), preferred_element_type=F32)
    rank = rank.astype(jnp.int32) - 1
    extra = rank >= PAIRS
    slot = jnp.where(extra, 3 * PAIRS - 1 - PAIRS * h - rank, rank + PAIRS * h)
    odd = jnp.sum((kept & extra).astype(jnp.int32), axis=1, dtype=jnp.int32)
    return jnp.where(kept, slot, -1), odd


def codes_of(slot):
    i = jnp.array([b // 14 for b in range(112)], jnp.int32)
    j = jnp.array([b % 14 for b in range(112)], jnp.int32)
    hit = slot[:, None, :] == jnp.arange(CAP, dtype=jnp.int32)[None, :, None]
    code = i * BLOCK + (j >> 1) * (128 << 10) + (((j & 1) - 2) << 20)
    return jnp.sum(jnp.where(hit, code[None, None, :], 0), axis=2, dtype=jnp.int32) + (2 << 20)


def layer(tokens, weight, block_mask, act_grad):
    d, width = weight.shape
    t = lax.axis_index("tensor").astype(jnp.int32)
    g = lax.axis_index("dp").astype(jnp.int32)

    partner = move(tokens, dc=1)
    home = move(tokens, dx=1)
    chip = join(tokens, partner)
    t, g, chip = lax.optimization_barrier((t, g, chip))
    z, xh, core = t >> 2, (t >> 1) & 1, t & 1
    xl, y = g >> 2, g & 3

    n = jnp.arange(32, dtype=jnp.int32)
    slot = n & 7
    dist = jnp.where(slot == 0, 0, jnp.where(slot == 1, 4, slot >> 1))
    flip = jnp.where(slot > 1, slot & 1, 0)
    gather_core = core ^ ((n >> 3) & 1)
    zk = (z - (1 - 2 * gather_core) * dist) & (NZ - 1)
    idx = zk * 4 + (xh ^ (n >> 4)) * 2 + (gather_core ^ flip)
    order = [(1, 1), (0, 3), (1, 2), (1, 3), (0, 1), (1, 0), (0, 2), (0, 0)]
    dx = jnp.array([o[0] for o in order], jnp.int32)
    dy = jnp.array([o[1] for o in order], jnp.int32)
    dests = (xl ^ dx) * NY + ((y + dy) & (NY - 1))

    def tick():
        return call(tick_kernel, 0, jax.ShapeDtypeStruct((8, 128), F32), (), 0)

    ticks = [tick() for _ in range(4)]
    near1, near2 = move(chip, dz=1), move(chip, dz=2)
    t_slot, ticks[0] = lax.optimization_barrier((t, ticks[0]))
    slot, odd = slots_of(block_mask, t_slot)
    slot, odd, idx, dests, near1 = lax.optimization_barrier((slot, odd, idx, dests, near1))
    slot, ticks[1] = lax.optimization_barrier((slot, ticks[1]))
    code, near2 = lax.optimization_barrier((codes_of(slot), near2))
    scalars = (dests, code, odd)

    near3 = move(near2, dz=1)
    head = call(head_kernel, 0, jax.ShapeDtypeStruct((16, d), BF16), (near2,), 0)
    far = move(head, dz=2)
    t_mask, ticks[2] = lax.optimization_barrier((t, ticks[2]))
    masked = call(
        mask_kernel,
        1,
        jax.ShapeDtypeStruct((d, width), BF16),
        ((t_mask * 14).reshape(1), weight, block_mask),
        d * width,
        scratch=(
            pltpu.VMEM(block_mask.shape, jnp.int32),
            pltpu.VMEM((block_mask.shape[0], width), F32),
            pltpu.SemaphoreType.DMA((9,)),
        ),
        space=pl.BlockSpec(memory_space=pl.ANY),
        limit=44,
    )
    near3, masked = lax.optimization_barrier((near3, masked))

    cross = [move(v, dx=1) for v in (near1, near2, near3, far)]
    x0 = join(tokens, far, near1, near2, near3)
    x2 = move(x0, dc=1)
    x1 = join(home, cross[3], *cross[:3])
    x3 = move(x1, dc=1)
    xs = (x0, x1, x2, x3)

    grads = act_grad.reshape(32, 16, width)
    act_a, pa = forward(0, idx, x0, x2, masked, grads, after=ticks)
    own_a, other_a = xgrad(pa, masked)
    received_a = move(other_a, dc=1)
    act_b, pb = forward(16, idx, x1, x3, masked, grads, after=(other_a,))

    parts = []

    def pack(first, count, after):
        packed = wgrad(first, count, scalars, pa, pb, xs, (after,))
        for v, o in zip(packed, order[first : first + count]):
            parts.append(v if o == (0, 0) else move_dp(v, *o))
        return packed[0]

    def back(x, hops):
        return move(x, dz=NZ - hops)

    done = pack(0, 1, other_a)
    done = pack(1, 2, done)
    a1, a2, a3, a4, home_a = mix(own_a, received_a, (done,))
    from_a3, from_a4, from_a1 = back(a3, 1), back(a4, 2), back(a1, 1)
    own_b, other_b = xgrad(pb, masked, (a4,))
    received_b = move(other_b, dc=1)
    done = hop(a2, from_a3, from_a4, (other_b,))
    from_a2 = back(done, 2)
    done = pack(3, 2, done)
    b1, b2, b3, b4, home_b = mix(own_b, received_b, (done,))
    from_b3, from_b4 = back(b3, 1), back(b4, 2)
    done = pack(5, 2, b4)
    done = hop(b2, from_b3, from_b4, (done,))
    b1, done = lax.optimization_barrier((b1, done))
    from_b2, from_b1 = back(done, 2), back(b1, 1)
    done = pack(7, 1, done)
    order_after = jax.ShapeDtypeStruct((8, 128), F32)
    act, done = call(
        act_join_kernel,
        1,
        (jax.ShapeDtypeStruct((32, 16, width), BF16), order_after),
        (idx, act_a, act_b),
        0,
        after=(done,),
    )

    early = call(
        presum_kernel,
        0,
        jax.ShapeDtypeStruct((PAIRS, BLOCK, 128), F32),
        (parts[7], *parts[:4]),
        5 * CAP * 4096,
        after=(done,),
    )
    to_core, kept = call(
        sum_kernel,
        0,
        (jax.ShapeDtypeStruct((32, d), BF16), jax.ShapeDtypeStruct((32, d), F32)),
        (from_a1, from_a2, home_a, from_b1, from_b2, home_b),
        6 * 32 * d,
    )
    to_x, kept = call(
        sum_core_kernel,
        0,
        (jax.ShapeDtypeStruct((16, d), BF16), jax.ShapeDtypeStruct((16, d), F32)),
        (kept, move(to_core, dc=1)),
        32 * d,
    )
    x_grad = call(
        last_kernel, 0, jax.ShapeDtypeStruct((16, d), BF16), (kept, move(to_x, dx=1)), 16 * d
    )

    weight_grad = call(
        unpack_kernel,
        2,
        jax.ShapeDtypeStruct((512, width), F32),
        (g.reshape(1), code, early, *parts[4:7]),
        8 * CAP * 4096,
        scratch=(
            pltpu.VMEM((512, width), F32),
            pltpu.SemaphoreType.DMA((4,)),
        ),
        out_space=pl.BlockSpec(memory_space=pl.ANY),
    )
    return (act.reshape(512, width), x_grad, weight_grad)


def solution(mesh):
    return jax.shard_map(
        layer,
        mesh=mesh,
        in_specs=(P(("dp", "tensor"), None), P(None, "tensor"), P(), P("dp", "tensor")),
        out_specs=(P("dp", "tensor"), P(("dp", "tensor"), None), P("dp", "tensor")),
        check_vma=False,
    )
```

```python
import functools

import jax
import jax.numpy as jnp
from jax import lax
from jax.experimental import pallas as pl
from jax.experimental.pallas import tpu as pltpu
from jax.sharding import PartitionSpec as P


BLOCK = 64
CAP = 70
PAIRS = CAP // 2
NZ = 8
NY = 4
F32 = jnp.float32
BF16 = jnp.bfloat16


VMEM = pl.BlockSpec(memory_space=pltpu.VMEM)
SMEM = pl.BlockSpec(memory_space=pltpu.SMEM)


def tensor_perm(dz, dx, dc, split=False):
    pairs = []
    for z in range(NZ):
        for xh in range(2):
            for core in range(2):
                shift = -dz if split and core else dz
                source = (z * 2 + xh) * 2 + core
                target = (((z + shift) % NZ) * 2 + (xh ^ dx)) * 2 + (core ^ dc)
                pairs.append((source, target))
    return pairs


def dp_perm(dx, dy):
    return [
        (xl * NY + y, (xl ^ dx) * NY + (y + dy) % NY) for xl in range(2) for y in range(NY)
    ]


def move(x, dz=0, dx=0, dc=0):
    return lax.ppermute(x, "tensor", tensor_perm(dz, dx, dc, split=True))


def move_dp(x, dx, dy):
    return lax.ppermute(x, "dp", dp_perm(dx, dy))


def call(
    kernel, n_scalar, out_shape, args, flops, scratch=(), after=(), limit=12, out_space=VMEM,
    space=VMEM,
):
    n_args, n_after = len(args), len(after)

    def run(*refs):
        kernel(*refs[:n_args], *refs[n_args + n_after :])

    n_out = len(out_shape) if isinstance(out_shape, (tuple, list)) else 1
    out_specs = [VMEM] * n_out if isinstance(out_shape, (tuple, list)) else out_space
    moved = sum(a.size * a.dtype.itemsize for a in args)
    return pl.pallas_call(
        run,
        out_shape=out_shape,
        in_specs=[SMEM] * n_scalar
        + [space] * (n_args - n_scalar)
        + [pl.BlockSpec(memory_space=pl.ANY)] * n_after,
        out_specs=out_specs,
        scratch_shapes=list(scratch),
        compiler_params=pltpu.CompilerParams(vmem_limit_bytes=limit << 20),
        cost_estimate=pl.CostEstimate(flops=flops, bytes_accessed=moved, transcendentals=0),
    )(*args, *after)


def tick_kernel(*refs):
    refs[-1][...] = jnp.zeros_like(refs[-1])


def join_kernel(*refs):
    parts, out = refs[:-1], refs[-1]
    at = 0
    for part in parts:
        out[at : at + part.shape[0], :] = part[...]
        at += part.shape[0]


def join(*parts):
    rows = sum(part.shape[0] for part in parts)
    shape = jax.ShapeDtypeStruct((rows, parts[0].shape[1]), BF16)
    return call(join_kernel, 0, shape, parts, 0)


def head_kernel(x_ref, o_ref):
    o_ref[...] = x_ref[0 : o_ref.shape[0], :]


def mask_kernel(t_ref, w_hbm, m_hbm, o_ref, m_ref, e_ref, sems):
    n_rows, blocks = m_ref.shape
    width = o_ref.shape[1]
    groups = n_rows // 8

    def part(g):
        rows = pl.ds(pl.multiple_of(g * 512, 512), 512)
        return pltpu.make_async_copy(w_hbm.at[rows], o_ref.at[rows], sems.at[g])

    mask_copy = pltpu.make_async_copy(m_hbm, m_ref, sems.at[groups])
    mask_copy.start()
    for g in range(groups):
        part(g).start()
    rows = lax.broadcasted_iota(jnp.int32, (blocks, width), 0)
    cols = lax.broadcasted_iota(jnp.int32, (blocks, width), 1)
    pick = (rows == t_ref[0] + lax.div(cols, BLOCK)).astype(BF16)
    mask_copy.wait()
    e_ref[...] = jnp.dot(m_ref[...].astype(F32).astype(BF16), pick, preferred_element_type=F32)

    @pl.loop(0, groups)
    def _(g):
        part(g).wait()
        eight = e_ref[pl.ds(pl.multiple_of(g * 8, 8), 8), :]
        for i in range(8):
            at = pl.ds(pl.multiple_of(g * 512 + i * BLOCK, BLOCK), BLOCK)
            row = jnp.broadcast_to(eight[i : i + 1, :], (BLOCK, width)).astype(BF16)
            o_ref[at, :] = o_ref[at, :] * row


def forward_kernel(first, idx_ref, xa, xb, w_ref, g_ref, act_ref, p_ref, acc_ref):
    d = w_ref.shape[0]
    kb = 1024

    def product(s):
        cols = pl.ds(pl.multiple_of(s * kb, kb), kb)
        x = jnp.concatenate([xa[:, cols], xb[:, cols]], axis=0)
        return jnp.dot(x, w_ref[cols, :], preferred_element_type=F32)

    acc_ref[...] = product(0)

    @pl.loop(1, d // kb)
    def _(s):
        acc_ref[...] += product(s)

    def finish(n, carry):
        rows = pl.ds(pl.multiple_of(n * 16, 16), 16)
        pre = acc_ref[rows, :]
        s = jax.nn.sigmoid(pre)
        act_ref[n] = (pre * s).astype(BF16)
        grad = g_ref[idx_ref[first + n]].astype(F32) * s * (1.0 + pre * (1.0 - s))
        p_ref[rows, :] = grad.astype(BF16)
        return carry

    lax.fori_loop(0, act_ref.shape[0], finish, 0, unroll=2)


def forward(first, idx, xa, xb, masked, act_grad, after=()):
    d, width = masked.shape
    return call(
        functools.partial(forward_kernel, first),
        1,
        (
            jax.ShapeDtypeStruct((16, 16, width), BF16),
            jax.ShapeDtypeStruct((256, width), BF16),
        ),
        (idx, xa, xb, masked, act_grad),
        2 * 256 * d * width,
        scratch=(pltpu.VMEM((256, width), F32),),
        after=after,
    )


def act_join_kernel(idx_ref, a_ref, b_ref, out, tick):
    tick[...] = jnp.zeros_like(tick)

    @pl.loop(0, 16)
    def _(n):
        out[idx_ref[n]] = a_ref[n]
        out[idx_ref[16 + n]] = b_ref[n]


def last_kernel(kept, received, out):
    out[...] = (kept[...] + received[...].astype(F32)).astype(BF16)


def xgrad_kernel(p_ref, w_ref, own_ref, other_ref):
    @pl.loop(0, w_ref.shape[0] // 512)
    def _(s):
        cols = pl.ds(pl.multiple_of(s * 512, 512), 512)
        part = lax.dot_general(
            p_ref[...], w_ref[cols, :], (((1,), (1,)), ((), ())), preferred_element_type=F32
        )
        own_ref[:, cols] = part[:128, :]
        other_ref[:, cols] = part[128:, :].astype(BF16)


def xgrad(p, masked, after=()):
    d, width = masked.shape
    return call(
        xgrad_kernel,
        0,
        (jax.ShapeDtypeStruct((128, d), F32), jax.ShapeDtypeStruct((128, d), BF16)),
        (p, masked),
        2 * 256 * d * width,
        after=after,
    )


def mix_kernel(own_ref, r_ref, near1, near2, near3, far, home):
    @pl.loop(0, own_ref.shape[1] // 512)
    def _(s):
        cols = pl.ds(pl.multiple_of(s * 512, 512), 512)
        total = (own_ref[:, cols] + r_ref[:, cols].astype(F32)).astype(BF16)
        home[:, cols] = total[0:16, :]
        far[:, cols] = total[16:32, :]
        near1[:, cols] = total[32:64, :]
        near2[:, cols] = total[64:96, :]
        near3[:, cols] = total[96:128, :]


def mix(own, received, after):
    d = own.shape[1]
    return call(
        mix_kernel,
        0,
        [jax.ShapeDtypeStruct((32, d), BF16)] * 3 + [jax.ShapeDtypeStruct((16, d), BF16)] * 2,
        (own, received),
        128 * d,
        after=after,
    )


def hop_kernel(near, one, two, out):
    @pl.loop(0, near.shape[1] // 512)
    def _(s):
        cols = pl.ds(pl.multiple_of(s * 512, 512), 512)
        total = near[:, cols].astype(F32) + one[:, cols].astype(F32)
        out[0:16, cols] = (total[0:16] + two[:, cols].astype(F32)).astype(BF16)
        out[16:32, cols] = total[16:32].astype(BF16)


def hop(near, one, two, after):
    shape = jax.ShapeDtypeStruct(near.shape, BF16)
    return call(hop_kernel, 0, shape, (near, one, two), 2 * near.size, after=after)


def sum_kernel(*refs):
    halves, to_core, kept = (refs[0:3], refs[3:6]), refs[6], refs[7]

    @pl.loop(0, kept.shape[1] // 512)
    def _(s):
        cols = pl.ds(pl.multiple_of(s * 512, 512), 512)
        for q, (one, two, home) in enumerate(halves):
            rows = slice(q * 16, q * 16 + 16)
            total = one[:, cols].astype(F32) + two[:, cols].astype(F32)
            kept[rows, cols] = home[:, cols].astype(F32) + total[0:16]
            to_core[rows, cols] = total[16:32].astype(BF16)


def sum_core_kernel(kept, received, to_x, out):
    @pl.loop(0, kept.shape[1] // 512)
    def _(s):
        cols = pl.ds(pl.multiple_of(s * 512, 512), 512)
        total = kept[:, cols] + received[:, cols].astype(F32)
        out[:, cols] = total[0:16, :]
        to_x[:, cols] = total[16:32, :].astype(BF16)


def place_of(code):
    return (
        pl.multiple_of(code & 1023, BLOCK),
        pl.multiple_of((code >> 10) & 1023, 128),
        code >> 20,
    )


def wgrad_kernel(first, dest_ref, code_ref, odd_ref, pa, pb, x0, x1, x2, x3, *rest):
    outs, acc_ref = rest[:-1], rest[-1]
    left = lax.broadcasted_iota(jnp.int32, (BLOCK, 128), 1) < BLOCK
    over_rows = (((0,), (0,)), ((), ()))
    for n, out in enumerate(outs):
        dest = dest_ref[first + n]
        cols = pl.ds(pl.multiple_of(dest * 512, 512), 512)
        xa = jnp.concatenate([x0[:, cols], x2[:, cols]], axis=0)
        xb = jnp.concatenate([x1[:, cols], x3[:, cols]], axis=0)
        acc_ref[...] = lax.dot_general(
            xa, pa[...], over_rows, preferred_element_type=F32
        ) + lax.dot_general(xb, pb[...], over_rows, preferred_element_type=F32)

        def tiles(s):
            row, lane, h = place_of(code_ref[dest, s])
            row2, lane2, h2 = place_of(code_ref[dest, PAIRS + s])
            return (
                acc_ref[pl.ds(row, BLOCK), pl.ds(lane, 128)],
                acc_ref[pl.ds(row2, BLOCK), pl.ds(lane2, 128)],
                h & 1,
                h2 & 1,
            )

        def pack(s, carry):
            one, two, _, _ = tiles(s)
            out[s] = jnp.where(left, one, two).astype(BF16)
            return carry

        def repack(n, carry):
            s = PAIRS - 1 - n
            one, two, h, h2 = tiles(s)
            one = pltpu.roll(one, h * BLOCK, 1)
            two = pltpu.roll(two, (1 - h2) * BLOCK, 1)
            out[s] = jnp.where(left, one, two).astype(BF16)
            return carry

        lax.fori_loop(0, PAIRS, pack, 0, unroll=5)
        lax.fori_loop(0, odd_ref[dest], repack, 0)


def wgrad(first, count, scalars, pa, pb, xs, after):
    width = pa.shape[1]
    return call(
        functools.partial(wgrad_kernel, first),
        3,
        [jax.ShapeDtypeStruct((PAIRS, BLOCK, 128), BF16)] * count,
        (*scalars, pa, pb, *xs),
        2 * 512 * 512 * width * count,
        scratch=(pltpu.VMEM((512, width), F32),),
        after=after,
    )


def presum_kernel(*refs):
    parts, out = refs[:-1], refs[-1]

    @pl.loop(0, PAIRS)
    def _(s):
        total = parts[0][s].astype(F32)
        for part in parts[1:]:
            total = total + part[s].astype(F32)
        out[s] = total


def unpack_kernel(own_ref, code_ref, *refs):
    parts, (out, buf, sems) = refs[:-3], refs[-3:]
    own = own_ref[0]
    buf[...] = jnp.zeros_like(buf)
    half = lax.broadcasted_iota(jnp.int32, (BLOCK, 128), 1) // BLOCK

    def place(s, carry):
        total = parts[0][s]
        for part in parts[1:]:
            total = total + part[s].astype(F32)
        other = pltpu.roll(total, BLOCK, 1)
        for side in range(2):
            row, lane, h = place_of(code_ref[own, side * PAIRS + s])
            value = jnp.where(h == side, total, other)
            at = buf.at[pl.ds(row, BLOCK), pl.ds(lane, 128)]
            pltpu.store(at, value, mask=half == h)
        return carry

    lax.fori_loop(0, PAIRS, place, 0, unroll=5)
    copies = []
    for c in range(4):
        rows = slice(c * 128, (c + 1) * 128)
        copies.append(pltpu.make_async_copy(buf.at[rows], out.at[rows], sems.at[c]))
        copies[-1].start()
    for copy in copies:
        copy.wait()


def slots_of(block_mask, t):
    mask = lax.dynamic_slice(block_mask, (0, t * 14), (64, 14)).reshape(8, 112)
    kept = mask != 0
    at = jnp.arange(112, dtype=jnp.int32)
    h = jnp.array([b % 14 % 2 for b in range(112)], jnp.int32)
    before = (at[:, None] <= at[None, :]) & (h[:, None] == h[None, :])
    rank = jnp.dot(kept.astype(BF16), before.astype(BF16), preferred_element_type=F32)
    rank = rank.astype(jnp.int32) - 1
    extra = rank >= PAIRS
    slot = jnp.where(extra, 3 * PAIRS - 1 - PAIRS * h - rank, rank + PAIRS * h)
    odd = jnp.sum((kept & extra).astype(jnp.int32), axis=1, dtype=jnp.int32)
    return jnp.where(kept, slot, -1), odd


def codes_of(slot):
    i = jnp.array([b // 14 for b in range(112)], jnp.int32)
    j = jnp.array([b % 14 for b in range(112)], jnp.int32)
    hit = slot[:, None, :] == jnp.arange(CAP, dtype=jnp.int32)[None, :, None]
    code = i * BLOCK + (j >> 1) * (128 << 10) + (((j & 1) - 2) << 20)
    return jnp.sum(jnp.where(hit, code[None, None, :], 0), axis=2, dtype=jnp.int32) + (2 << 20)


def layer(tokens, weight, block_mask, act_grad):
    d, width = weight.shape
    t = lax.axis_index("tensor").astype(jnp.int32)
    g = lax.axis_index("dp").astype(jnp.int32)

    partner = move(tokens, dc=1)
    home = move(tokens, dx=1)
    chip = join(tokens, partner)
    t, g, chip = lax.optimization_barrier((t, g, chip))
    z, xh, core = t >> 2, (t >> 1) & 1, t & 1
    xl, y = g >> 2, g & 3

    n = jnp.arange(32, dtype=jnp.int32)
    slot = n & 7
    dist = jnp.where(slot == 0, 0, jnp.where(slot == 1, 4, slot >> 1))
    flip = jnp.where(slot > 1, slot & 1, 0)
    gather_core = core ^ ((n >> 3) & 1)
    zk = (z - (1 - 2 * gather_core) * dist) & (NZ - 1)
    idx = zk * 4 + (xh ^ (n >> 4)) * 2 + (gather_core ^ flip)
    order = [(1, 1), (0, 3), (1, 2), (1, 3), (0, 1), (1, 0), (0, 2), (0, 0)]
    dx = jnp.array([o[0] for o in order], jnp.int32)
    dy = jnp.array([o[1] for o in order], jnp.int32)
    dests = (xl ^ dx) * NY + ((y + dy) & (NY - 1))

    def tick():
        return call(tick_kernel, 0, jax.ShapeDtypeStruct((8, 128), F32), (), 0)

    ticks = [tick() for _ in range(4)]
    near1, near2 = move(chip, dz=1), move(chip, dz=2)
    t_slot, ticks[0] = lax.optimization_barrier((t, ticks[0]))
    slot, odd = slots_of(block_mask, t_slot)
    slot, odd, idx, dests, near1 = lax.optimization_barrier((slot, odd, idx, dests, near1))
    slot, ticks[1] = lax.optimization_barrier((slot, ticks[1]))
    code, near2 = lax.optimization_barrier((codes_of(slot), near2))
    scalars = (dests, code, odd)

    near3 = move(near2, dz=1)
    head = call(head_kernel, 0, jax.ShapeDtypeStruct((16, d), BF16), (near2,), 0)
    far = move(head, dz=2)
    t_mask, ticks[2] = lax.optimization_barrier((t, ticks[2]))
    masked = call(
        mask_kernel,
        1,
        jax.ShapeDtypeStruct((d, width), BF16),
        ((t_mask * 14).reshape(1), weight, block_mask),
        d * width,
        scratch=(
            pltpu.VMEM(block_mask.shape, jnp.int32),
            pltpu.VMEM((block_mask.shape[0], width), F32),
            pltpu.SemaphoreType.DMA((9,)),
        ),
        space=pl.BlockSpec(memory_space=pl.ANY),
        limit=44,
    )
    near3, masked = lax.optimization_barrier((near3, masked))

    cross = [move(v, dx=1) for v in (near1, near2, near3, far)]
    x0 = join(tokens, far, near1, near2, near3)
    x2 = move(x0, dc=1)
    x1 = join(home, cross[3], *cross[:3])
    x3 = move(x1, dc=1)
    xs = (x0, x1, x2, x3)

    grads = act_grad.reshape(32, 16, width)
    act_a, pa = forward(0, idx, x0, x2, masked, grads, after=ticks)
    own_a, other_a = xgrad(pa, masked)
    received_a = move(other_a, dc=1)
    act_b, pb = forward(16, idx, x1, x3, masked, grads, after=(other_a,))

    parts = []

    def pack(first, count, after):
        packed = wgrad(first, count, scalars, pa, pb, xs, (after,))
        for v, o in zip(packed, order[first : first + count]):
            parts.append(v if o == (0, 0) else move_dp(v, *o))
        return packed[0]

    def back(x, hops):
        return move(x, dz=NZ - hops)

    done = pack(0, 1, other_a)
    done = pack(1, 2, done)
    a1, a2, a3, a4, home_a = mix(own_a, received_a, (done,))
    from_a3, from_a4 = back(a3, 1), back(a4, 2)
    own_b, other_b = xgrad(pb, masked, (a4,))
    received_b = move(other_b, dc=1)
    done = pack(3, 2, other_b)
    b1, b2, b3, b4, home_b = mix(own_b, received_b, (done,))
    from_b3, from_b4, from_b1 = back(b3, 1), back(b4, 2), back(b1, 1)
    done = hop(a2, from_a3, from_a4, (b4,))
    from_a2 = back(done, 2)
    done = pack(5, 2, done)
    done = hop(b2, from_b3, from_b4, (done,))
    a1, done = lax.optimization_barrier((a1, done))
    from_b2, from_a1 = back(done, 2), back(a1, 1)
    done = pack(7, 1, done)
    order_after = jax.ShapeDtypeStruct((8, 128), F32)
    act, done = call(
        act_join_kernel,
        1,
        (jax.ShapeDtypeStruct((32, 16, width), BF16), order_after),
        (idx, act_a, act_b),
        0,
        after=(done,),
    )

    early = call(
        presum_kernel,
        0,
        jax.ShapeDtypeStruct((PAIRS, BLOCK, 128), F32),
        (parts[7], *parts[:4]),
        5 * CAP * 4096,
        after=(done,),
    )
    to_core, kept = call(
        sum_kernel,
        0,
        (jax.ShapeDtypeStruct((32, d), BF16), jax.ShapeDtypeStruct((32, d), F32)),
        (from_a1, from_a2, home_a, from_b1, from_b2, home_b),
        6 * 32 * d,
    )
    to_x, kept = call(
        sum_core_kernel,
        0,
        (jax.ShapeDtypeStruct((16, d), BF16), jax.ShapeDtypeStruct((16, d), F32)),
        (kept, move(to_core, dc=1)),
        32 * d,
    )
    x_grad = call(
        last_kernel, 0, jax.ShapeDtypeStruct((16, d), BF16), (kept, move(to_x, dx=1)), 16 * d
    )

    weight_grad = call(
        unpack_kernel,
        2,
        jax.ShapeDtypeStruct((512, width), F32),
        (g.reshape(1), code, early, *parts[4:7]),
        8 * CAP * 4096,
        scratch=(
            pltpu.VMEM((512, width), F32),
            pltpu.SemaphoreType.DMA((4,)),
        ),
        out_space=pl.BlockSpec(memory_space=pl.ANY),
    )
    return (act.reshape(512, width), x_grad, weight_grad)


def solution(mesh):
    return jax.shard_map(
        layer,
        mesh=mesh,
        in_specs=(P(("dp", "tensor"), None), P(None, "tensor"), P(), P("dp", "tensor")),
        out_specs=(P("dp", "tensor"), P(("dp", "tensor"), None), P("dp", "tensor")),
        check_vma=False,
    )
```

```python
import functools

import jax
import jax.numpy as jnp
from jax import lax
from jax.experimental import pallas as pl
from jax.experimental.pallas import tpu as pltpu
from jax.sharding import PartitionSpec as P


BLOCK = 64
CAP = 70
PAIRS = CAP // 2
NZ = 8
NY = 4
F32 = jnp.float32
BF16 = jnp.bfloat16


VMEM = pl.BlockSpec(memory_space=pltpu.VMEM)
SMEM = pl.BlockSpec(memory_space=pltpu.SMEM)


def tensor_perm(dz, dx, dc, split=False):
    pairs = []
    for z in range(NZ):
        for xh in range(2):
            for core in range(2):
                shift = -dz if split and core else dz
                source = (z * 2 + xh) * 2 + core
                target = (((z + shift) % NZ) * 2 + (xh ^ dx)) * 2 + (core ^ dc)
                pairs.append((source, target))
    return pairs


def dp_perm(dx, dy):
    return [
        (xl * NY + y, (xl ^ dx) * NY + (y + dy) % NY) for xl in range(2) for y in range(NY)
    ]


def move(x, dz=0, dx=0, dc=0):
    return lax.ppermute(x, "tensor", tensor_perm(dz, dx, dc, split=True))


def move_dp(x, dx, dy):
    return lax.ppermute(x, "dp", dp_perm(dx, dy))


def call(
    kernel, n_scalar, out_shape, args, flops, scratch=(), after=(), limit=12, out_space=VMEM,
    space=VMEM,
):
    n_args, n_after = len(args), len(after)

    def run(*refs):
        kernel(*refs[:n_args], *refs[n_args + n_after :])

    n_out = len(out_shape) if isinstance(out_shape, (tuple, list)) else 1
    out_specs = [VMEM] * n_out if isinstance(out_shape, (tuple, list)) else out_space
    moved = sum(a.size * a.dtype.itemsize for a in args)
    return pl.pallas_call(
        run,
        out_shape=out_shape,
        in_specs=[SMEM] * n_scalar
        + [space] * (n_args - n_scalar)
        + [pl.BlockSpec(memory_space=pl.ANY)] * n_after,
        out_specs=out_specs,
        scratch_shapes=list(scratch),
        compiler_params=pltpu.CompilerParams(vmem_limit_bytes=limit << 20),
        cost_estimate=pl.CostEstimate(flops=flops, bytes_accessed=moved, transcendentals=0),
    )(*args, *after)


def tick_kernel(*refs):
    refs[-1][...] = jnp.zeros_like(refs[-1])


def join_kernel(*refs):
    parts, out = refs[:-1], refs[-1]
    at = 0
    for part in parts:
        out[at : at + part.shape[0], :] = part[...]
        at += part.shape[0]


def join(*parts):
    rows = sum(part.shape[0] for part in parts)
    shape = jax.ShapeDtypeStruct((rows, parts[0].shape[1]), BF16)
    return call(join_kernel, 0, shape, parts, 0)


def head_kernel(x_ref, o_ref):
    o_ref[...] = x_ref[0 : o_ref.shape[0], :]


def mask_kernel(t_ref, w_hbm, m_hbm, o_ref, m_ref, e_ref, sems):
    n_rows, blocks = m_ref.shape
    width = o_ref.shape[1]
    groups = n_rows // 8

    def part(g):
        rows = pl.ds(pl.multiple_of(g * 512, 512), 512)
        return pltpu.make_async_copy(w_hbm.at[rows], o_ref.at[rows], sems.at[g])

    mask_copy = pltpu.make_async_copy(m_hbm, m_ref, sems.at[groups])
    mask_copy.start()
    for g in range(groups):
        part(g).start()
    rows = lax.broadcasted_iota(jnp.int32, (blocks, width), 0)
    cols = lax.broadcasted_iota(jnp.int32, (blocks, width), 1)
    pick = (rows == t_ref[0] + lax.div(cols, BLOCK)).astype(BF16)
    mask_copy.wait()
    e_ref[...] = jnp.dot(m_ref[...].astype(F32).astype(BF16), pick, preferred_element_type=F32)

    @pl.loop(0, groups)
    def _(g):
        part(g).wait()
        eight = e_ref[pl.ds(pl.multiple_of(g * 8, 8), 8), :]
        for i in range(8):
            at = pl.ds(pl.multiple_of(g * 512 + i * BLOCK, BLOCK), BLOCK)
            row = jnp.broadcast_to(eight[i : i + 1, :], (BLOCK, width)).astype(BF16)
            o_ref[at, :] = o_ref[at, :] * row


def forward_kernel(first, idx_ref, xa, xb, w_ref, g_ref, act_ref, p_ref, acc_ref):
    d = w_ref.shape[0]
    kb = 2048

    def product(s):
        cols = pl.ds(pl.multiple_of(s * kb, kb), kb)
        x = jnp.concatenate([xa[:, cols], xb[:, cols]], axis=0)
        return jnp.dot(x, w_ref[cols, :], preferred_element_type=F32)

    acc_ref[...] = product(0)

    @pl.loop(1, d // kb)
    def _(s):
        acc_ref[...] += product(s)

    def finish(n, carry):
        rows = pl.ds(pl.multiple_of(n * 16, 16), 16)
        pre = acc_ref[rows, :]
        s = jax.nn.sigmoid(pre)
        act_ref[n] = (pre * s).astype(BF16)
        grad = g_ref[idx_ref[first + n]].astype(F32) * s * (1.0 + pre * (1.0 - s))
        p_ref[rows, :] = grad.astype(BF16)
        return carry

    lax.fori_loop(0, act_ref.shape[0], finish, 0, unroll=4)


def forward(first, idx, xa, xb, masked, act_grad, after=()):
    d, width = masked.shape
    return call(
        functools.partial(forward_kernel, first),
        1,
        (
            jax.ShapeDtypeStruct((16, 16, width), BF16),
            jax.ShapeDtypeStruct((256, width), BF16),
        ),
        (idx, xa, xb, masked, act_grad),
        2 * 256 * d * width,
        scratch=(pltpu.VMEM((256, width), F32),),
        after=after,
    )


def act_join_kernel(idx_ref, a_ref, b_ref, out, tick):
    tick[...] = jnp.zeros_like(tick)

    @pl.loop(0, 16)
    def _(n):
        out[idx_ref[n]] = a_ref[n]
        out[idx_ref[16 + n]] = b_ref[n]


def last_kernel(kept, received, out):
    out[...] = (kept[...] + received[...].astype(F32)).astype(BF16)


def xgrad_kernel(p_ref, w_ref, own_ref, other_ref):
    @pl.loop(0, w_ref.shape[0] // 512)
    def _(s):
        cols = pl.ds(pl.multiple_of(s * 512, 512), 512)
        part = lax.dot_general(
            p_ref[...], w_ref[cols, :], (((1,), (1,)), ((), ())), preferred_element_type=F32
        )
        own_ref[:, cols] = part[:128, :]
        other_ref[:, cols] = part[128:, :].astype(BF16)


def xgrad(p, masked, after=()):
    d, width = masked.shape
    return call(
        xgrad_kernel,
        0,
        (jax.ShapeDtypeStruct((128, d), F32), jax.ShapeDtypeStruct((128, d), BF16)),
        (p, masked),
        2 * 256 * d * width,
        after=after,
    )


def mix_kernel(own_ref, r_ref, near1, near2, near3, far, home):
    @pl.loop(0, own_ref.shape[1] // 512)
    def _(s):
        cols = pl.ds(pl.multiple_of(s * 512, 512), 512)
        total = (own_ref[:, cols] + r_ref[:, cols].astype(F32)).astype(BF16)
        home[:, cols] = total[0:16, :]
        far[:, cols] = total[16:32, :]
        near1[:, cols] = total[32:64, :]
        near2[:, cols] = total[64:96, :]
        near3[:, cols] = total[96:128, :]


def mix(own, received, after):
    d = own.shape[1]
    return call(
        mix_kernel,
        0,
        [jax.ShapeDtypeStruct((32, d), BF16)] * 3 + [jax.ShapeDtypeStruct((16, d), BF16)] * 2,
        (own, received),
        128 * d,
        after=after,
    )


def hop_kernel(near, one, two, out):
    @pl.loop(0, near.shape[1] // 512)
    def _(s):
        cols = pl.ds(pl.multiple_of(s * 512, 512), 512)
        total = near[:, cols].astype(F32) + one[:, cols].astype(F32)
        out[0:16, cols] = (total[0:16] + two[:, cols].astype(F32)).astype(BF16)
        out[16:32, cols] = total[16:32].astype(BF16)


def hop(near, one, two, after):
    shape = jax.ShapeDtypeStruct(near.shape, BF16)
    return call(hop_kernel, 0, shape, (near, one, two), 2 * near.size, after=after)


def sum_kernel(*refs):
    halves, to_core, kept = (refs[0:3], refs[3:6]), refs[6], refs[7]

    @pl.loop(0, kept.shape[1] // 512)
    def _(s):
        cols = pl.ds(pl.multiple_of(s * 512, 512), 512)
        for q, (one, two, home) in enumerate(halves):
            rows = slice(q * 16, q * 16 + 16)
            total = one[:, cols].astype(F32) + two[:, cols].astype(F32)
            kept[rows, cols] = home[:, cols].astype(F32) + total[0:16]
            to_core[rows, cols] = total[16:32].astype(BF16)


def sum_core_kernel(kept, received, to_x, out):
    @pl.loop(0, kept.shape[1] // 512)
    def _(s):
        cols = pl.ds(pl.multiple_of(s * 512, 512), 512)
        total = kept[:, cols] + received[:, cols].astype(F32)
        out[:, cols] = total[0:16, :]
        to_x[:, cols] = total[16:32, :].astype(BF16)


def place_of(code):
    return (
        pl.multiple_of(code & 1023, BLOCK),
        pl.multiple_of((code >> 10) & 1023, 128),
        code >> 20,
    )


def wgrad_kernel(first, dest_ref, code_ref, odd_ref, pa, pb, x0, x1, x2, x3, *rest):
    outs, acc_ref = rest[:-1], rest[-1]
    left = lax.broadcasted_iota(jnp.int32, (BLOCK, 128), 1) < BLOCK
    over_rows = (((0,), (0,)), ((), ()))
    for n, out in enumerate(outs):
        dest = dest_ref[first + n]
        cols = pl.ds(pl.multiple_of(dest * 512, 512), 512)
        xa = jnp.concatenate([x0[:, cols], x2[:, cols]], axis=0)
        xb = jnp.concatenate([x1[:, cols], x3[:, cols]], axis=0)
        acc_ref[...] = lax.dot_general(
            xa, pa[...], over_rows, preferred_element_type=F32
        ) + lax.dot_general(xb, pb[...], over_rows, preferred_element_type=F32)

        def tiles(s):
            row, lane, h = place_of(code_ref[dest, s])
            row2, lane2, h2 = place_of(code_ref[dest, PAIRS + s])
            return (
                acc_ref[pl.ds(row, BLOCK), pl.ds(lane, 128)],
                acc_ref[pl.ds(row2, BLOCK), pl.ds(lane2, 128)],
                h & 1,
                h2 & 1,
            )

        def pack(s, carry):
            one, two, _, _ = tiles(s)
            out[s] = jnp.where(left, one, two).astype(BF16)
            return carry

        def repack(n, carry):
            s = PAIRS - 1 - n
            one, two, h, h2 = tiles(s)
            one = pltpu.roll(one, h * BLOCK, 1)
            two = pltpu.roll(two, (1 - h2) * BLOCK, 1)
            out[s] = jnp.where(left, one, two).astype(BF16)
            return carry

        lax.fori_loop(0, PAIRS, pack, 0, unroll=5)
        lax.fori_loop(0, odd_ref[dest], repack, 0)


def wgrad(first, count, scalars, pa, pb, xs, after):
    width = pa.shape[1]
    return call(
        functools.partial(wgrad_kernel, first),
        3,
        [jax.ShapeDtypeStruct((PAIRS, BLOCK, 128), BF16)] * count,
        (*scalars, pa, pb, *xs),
        2 * 512 * 512 * width * count,
        scratch=(pltpu.VMEM((512, width), F32),),
        after=after,
    )


def presum_kernel(*refs):
    parts, out = refs[:-1], refs[-1]

    @pl.loop(0, PAIRS)
    def _(s):
        total = parts[0][s].astype(F32)
        for part in parts[1:]:
            total = total + part[s].astype(F32)
        out[s] = total


def unpack_kernel(own_ref, code_ref, *refs):
    parts, (out, buf, sems) = refs[:-3], refs[-3:]
    own = own_ref[0]
    buf[...] = jnp.zeros_like(buf)
    half = lax.broadcasted_iota(jnp.int32, (BLOCK, 128), 1) // BLOCK

    def place(s, carry):
        total = parts[0][s]
        for part in parts[1:]:
            total = total + part[s].astype(F32)
        other = pltpu.roll(total, BLOCK, 1)
        for side in range(2):
            row, lane, h = place_of(code_ref[own, side * PAIRS + s])
            value = jnp.where(h == side, total, other)
            at = buf.at[pl.ds(row, BLOCK), pl.ds(lane, 128)]
            pltpu.store(at, value, mask=half == h)
        return carry

    lax.fori_loop(0, PAIRS, place, 0, unroll=5)
    copies = []
    for c in range(4):
        rows = slice(c * 128, (c + 1) * 128)
        copies.append(pltpu.make_async_copy(buf.at[rows], out.at[rows], sems.at[c]))
        copies[-1].start()
    for copy in copies:
        copy.wait()


def slots_of(block_mask, t):
    mask = lax.dynamic_slice(block_mask, (0, t * 14), (64, 14)).reshape(8, 112)
    kept = mask != 0
    at = jnp.arange(112, dtype=jnp.int32)
    h = jnp.array([b % 14 % 2 for b in range(112)], jnp.int32)
    before = (at[:, None] <= at[None, :]) & (h[:, None] == h[None, :])
    rank = jnp.dot(kept.astype(BF16), before.astype(BF16), preferred_element_type=F32)
    rank = rank.astype(jnp.int32) - 1
    extra = rank >= PAIRS
    slot = jnp.where(extra, 3 * PAIRS - 1 - PAIRS * h - rank, rank + PAIRS * h)
    odd = jnp.sum((kept & extra).astype(jnp.int32), axis=1, dtype=jnp.int32)
    return jnp.where(kept, slot, -1), odd


def codes_of(slot):
    i = jnp.array([b // 14 for b in range(112)], jnp.int32)
    j = jnp.array([b % 14 for b in range(112)], jnp.int32)
    hit = slot[:, None, :] == jnp.arange(CAP, dtype=jnp.int32)[None, :, None]
    code = i * BLOCK + (j >> 1) * (128 << 10) + (((j & 1) - 2) << 20)
    return jnp.sum(jnp.where(hit, code[None, None, :], 0), axis=2, dtype=jnp.int32) + (2 << 20)


def layer(tokens, weight, block_mask, act_grad):
    d, width = weight.shape
    t = lax.axis_index("tensor").astype(jnp.int32)
    g = lax.axis_index("dp").astype(jnp.int32)

    partner = move(tokens, dc=1)
    home = move(tokens, dx=1)
    lifted = call(head_kernel, 0, jax.ShapeDtypeStruct(tokens.shape, BF16), (tokens,), 0)
    chip = join(lifted, partner)
    t, g, chip = lax.optimization_barrier((t, g, chip))
    z, xh, core = t >> 2, (t >> 1) & 1, t & 1
    xl, y = g >> 2, g & 3

    n = jnp.arange(32, dtype=jnp.int32)
    slot = n & 7
    dist = jnp.where(slot == 0, 0, jnp.where(slot == 1, 4, slot >> 1))
    flip = jnp.where(slot > 1, slot & 1, 0)
    gather_core = core ^ ((n >> 3) & 1)
    zk = (z - (1 - 2 * gather_core) * dist) & (NZ - 1)
    idx = zk * 4 + (xh ^ (n >> 4)) * 2 + (gather_core ^ flip)
    order = [(1, 1), (0, 3), (1, 2), (1, 3), (0, 1), (1, 0), (0, 2), (0, 0)]
    dx = jnp.array([o[0] for o in order], jnp.int32)
    dy = jnp.array([o[1] for o in order], jnp.int32)
    dests = (xl ^ dx) * NY + ((y + dy) & (NY - 1))

    def tick():
        return call(tick_kernel, 0, jax.ShapeDtypeStruct((8, 128), F32), (), 0)

    ticks = [tick() for _ in range(4)]
    near1, near2 = move(chip, dz=1), move(chip, dz=2)
    t_slot, ticks[0] = lax.optimization_barrier((t, ticks[0]))
    slot, odd = slots_of(block_mask, t_slot)
    slot, odd, idx, dests, near1 = lax.optimization_barrier((slot, odd, idx, dests, near1))
    slot, ticks[1] = lax.optimization_barrier((slot, ticks[1]))
    code, near2 = lax.optimization_barrier((codes_of(slot), near2))
    scalars = (dests, code, odd)

    near3 = move(near2, dz=1)
    head = call(head_kernel, 0, jax.ShapeDtypeStruct((16, d), BF16), (near2,), 0)
    far = move(head, dz=2)
    t_mask, ticks[2] = lax.optimization_barrier((t, ticks[2]))
    masked = call(
        mask_kernel,
        1,
        jax.ShapeDtypeStruct((d, width), BF16),
        ((t_mask * 14).reshape(1), weight, block_mask),
        d * width,
        scratch=(
            pltpu.VMEM(block_mask.shape, jnp.int32),
            pltpu.VMEM((block_mask.shape[0], width), F32),
            pltpu.SemaphoreType.DMA((9,)),
        ),
        space=pl.BlockSpec(memory_space=pl.ANY),
        limit=44,
    )
    near3, masked = lax.optimization_barrier((near3, masked))

    cross = [move(v, dx=1) for v in (near1, near2, near3, far)]
    x0 = join(lifted, far, near1, near2, near3)
    x2 = move(x0, dc=1)
    x1 = join(home, cross[3], *cross[:3])
    x3 = move(x1, dc=1)
    xs = (x0, x1, x2, x3)

    grads = act_grad.reshape(32, 16, width)
    act_a, pa = forward(0, idx, x0, x2, masked, grads, after=ticks)
    own_a, other_a = xgrad(pa, masked)
    received_a = move(other_a, dc=1)
    act_b, pb = forward(16, idx, x1, x3, masked, grads, after=(other_a,))

    parts = []

    def pack(first, count, after):
        packed = wgrad(first, count, scalars, pa, pb, xs, (after,))
        for v, o in zip(packed, order[first : first + count]):
            parts.append(v if o == (0, 0) else move_dp(v, *o))
        return packed[0]

    def back(x, hops):
        return move(x, dz=NZ - hops)

    done = pack(0, 1, other_a)
    done = pack(1, 2, done)
    a1, a2, a3, a4, home_a = mix(own_a, received_a, (done,))
    from_a3, from_a4 = back(a3, 1), back(a4, 2)
    own_b, other_b = xgrad(pb, masked, (a4,))
    received_b = move(other_b, dc=1)
    done = pack(3, 2, other_b)
    b1, b2, b3, b4, home_b = mix(own_b, received_b, (done,))
    from_b3, from_b4, from_b1 = back(b3, 1), back(b4, 2), back(b1, 1)
    done = hop(a2, from_a3, from_a4, (b4,))
    from_a2 = back(done, 2)
    done = pack(5, 2, done)
    done = hop(b2, from_b3, from_b4, (done,))
    a1, done = lax.optimization_barrier((a1, done))
    from_b2, from_a1 = back(done, 2), back(a1, 1)
    done = pack(7, 1, done)
    order_after = jax.ShapeDtypeStruct((8, 128), F32)
    act, done = call(
        act_join_kernel,
        1,
        (jax.ShapeDtypeStruct((32, 16, width), BF16), order_after),
        (idx, act_a, act_b),
        0,
        after=(done,),
    )

    early = call(
        presum_kernel,
        0,
        jax.ShapeDtypeStruct((PAIRS, BLOCK, 128), F32),
        (parts[7], *parts[:4]),
        5 * CAP * 4096,
        after=(done,),
    )
    to_core, kept = call(
        sum_kernel,
        0,
        (jax.ShapeDtypeStruct((32, d), BF16), jax.ShapeDtypeStruct((32, d), F32)),
        (from_a1, from_a2, home_a, from_b1, from_b2, home_b),
        6 * 32 * d,
    )
    to_x, kept = call(
        sum_core_kernel,
        0,
        (jax.ShapeDtypeStruct((16, d), BF16), jax.ShapeDtypeStruct((16, d), F32)),
        (kept, move(to_core, dc=1)),
        32 * d,
    )
    x_grad = call(
        last_kernel, 0, jax.ShapeDtypeStruct((16, d), BF16), (kept, move(to_x, dx=1)), 16 * d
    )

    weight_grad = call(
        unpack_kernel,
        2,
        jax.ShapeDtypeStruct((512, width), F32),
        (g.reshape(1), code, early, *parts[4:7]),
        8 * CAP * 4096,
        scratch=(
            pltpu.VMEM((512, width), F32),
            pltpu.SemaphoreType.DMA((4,)),
        ),
        out_space=pl.BlockSpec(memory_space=pl.ANY),
    )
    return (act.reshape(512, width), x_grad, weight_grad)


def solution(mesh):
    return jax.shard_map(
        layer,
        mesh=mesh,
        in_specs=(P(("dp", "tensor"), None), P(None, "tensor"), P(), P("dp", "tensor")),
        out_specs=(P("dp", "tensor"), P(("dp", "tensor"), None), P("dp", "tensor")),
        check_vma=False,
    )
```

```python
import functools

import jax
import jax.numpy as jnp
from jax import lax
from jax.experimental import pallas as pl
from jax.experimental.pallas import tpu as pltpu
from jax.sharding import PartitionSpec as P


BLOCK = 64
CAP = 70
PAIRS = CAP // 2
NZ = 8
NY = 4
F32 = jnp.float32
BF16 = jnp.bfloat16


VMEM = pl.BlockSpec(memory_space=pltpu.VMEM)
SMEM = pl.BlockSpec(memory_space=pltpu.SMEM)


def tensor_perm(dz, dx, dc, split=False):
    pairs = []
    for z in range(NZ):
        for xh in range(2):
            for core in range(2):
                shift = -dz if split and core else dz
                source = (z * 2 + xh) * 2 + core
                target = (((z + shift) % NZ) * 2 + (xh ^ dx)) * 2 + (core ^ dc)
                pairs.append((source, target))
    return pairs


def dp_perm(dx, dy):
    return [
        (xl * NY + y, (xl ^ dx) * NY + (y + dy) % NY) for xl in range(2) for y in range(NY)
    ]


def move(x, dz=0, dx=0, dc=0):
    return lax.ppermute(x, "tensor", tensor_perm(dz, dx, dc, split=True))


def move_dp(x, dx, dy):
    return lax.ppermute(x, "dp", dp_perm(dx, dy))


def call(
    kernel, n_scalar, out_shape, args, flops, scratch=(), after=(), limit=12, out_space=VMEM,
    space=VMEM,
):
    n_args, n_after = len(args), len(after)

    def run(*refs):
        kernel(*refs[:n_args], *refs[n_args + n_after :])

    n_out = len(out_shape) if isinstance(out_shape, (tuple, list)) else 1
    out_specs = [VMEM] * n_out if isinstance(out_shape, (tuple, list)) else out_space
    moved = sum(a.size * a.dtype.itemsize for a in args)
    return pl.pallas_call(
        run,
        out_shape=out_shape,
        in_specs=[SMEM] * n_scalar
        + [space] * (n_args - n_scalar)
        + [pl.BlockSpec(memory_space=pl.ANY)] * n_after,
        out_specs=out_specs,
        scratch_shapes=list(scratch),
        compiler_params=pltpu.CompilerParams(vmem_limit_bytes=limit << 20),
        cost_estimate=pl.CostEstimate(flops=flops, bytes_accessed=moved, transcendentals=0),
    )(*args, *after)


def tick_kernel(*refs):
    refs[-1][...] = jnp.zeros_like(refs[-1])


def join_kernel(*refs):
    parts, out = refs[:-1], refs[-1]
    at = 0
    for part in parts:
        out[at : at + part.shape[0], :] = part[...]
        at += part.shape[0]


def join(*parts):
    rows = sum(part.shape[0] for part in parts)
    shape = jax.ShapeDtypeStruct((rows, parts[0].shape[1]), BF16)
    return call(join_kernel, 0, shape, parts, 0)


def head_kernel(x_ref, o_ref):
    o_ref[...] = x_ref[0 : o_ref.shape[0], :]


def mask_kernel(t_ref, w_hbm, m_hbm, o_ref, m_ref, e_ref, sems):
    n_rows, blocks = m_ref.shape
    width = o_ref.shape[1]
    groups = n_rows // 8

    def part(g):
        rows = pl.ds(pl.multiple_of(g * 512, 512), 512)
        return pltpu.make_async_copy(w_hbm.at[rows], o_ref.at[rows], sems.at[g])

    mask_copy = pltpu.make_async_copy(m_hbm, m_ref, sems.at[groups])
    mask_copy.start()
    for g in range(groups):
        part(g).start()
    rows = lax.broadcasted_iota(jnp.int32, (blocks, width), 0)
    cols = lax.broadcasted_iota(jnp.int32, (blocks, width), 1)
    pick = (rows == t_ref[0] + lax.div(cols, BLOCK)).astype(BF16)
    mask_copy.wait()
    e_ref[...] = jnp.dot(m_ref[...].astype(F32).astype(BF16), pick, preferred_element_type=F32)

    @pl.loop(0, groups)
    def _(g):
        part(g).wait()
        eight = e_ref[pl.ds(pl.multiple_of(g * 8, 8), 8), :]
        for i in range(8):
            at = pl.ds(pl.multiple_of(g * 512 + i * BLOCK, BLOCK), BLOCK)
            row = jnp.broadcast_to(eight[i : i + 1, :], (BLOCK, width)).astype(BF16)
            o_ref[at, :] = o_ref[at, :] * row


def forward_kernel(first, idx_ref, xa, xb, w_ref, g_ref, act_ref, p_ref, acc_ref):
    d = w_ref.shape[0]
    kb = 2048

    def product(s):
        cols = pl.ds(pl.multiple_of(s * kb, kb), kb)
        x = jnp.concatenate([xa[:, cols], xb[:, cols]], axis=0)
        return jnp.dot(x, w_ref[cols, :], preferred_element_type=F32)

    acc_ref[...] = product(0)

    @pl.loop(1, d // kb)
    def _(s):
        acc_ref[...] += product(s)

    def finish(n, carry):
        rows = pl.ds(pl.multiple_of(n * 16, 16), 16)
        pre = acc_ref[rows, :]
        s = jax.nn.sigmoid(pre)
        act_ref[n] = (pre * s).astype(BF16)
        grad = g_ref[idx_ref[first + n]].astype(F32) * s * (1.0 + pre * (1.0 - s))
        p_ref[rows, :] = grad.astype(BF16)
        return carry

    lax.fori_loop(0, act_ref.shape[0], finish, 0, unroll=4)


def forward(first, idx, xa, xb, masked, act_grad, after=()):
    d, width = masked.shape
    return call(
        functools.partial(forward_kernel, first),
        1,
        (
            jax.ShapeDtypeStruct((16, 16, width), BF16),
            jax.ShapeDtypeStruct((256, width), BF16),
        ),
        (idx, xa, xb, masked, act_grad),
        2 * 256 * d * width,
        scratch=(pltpu.VMEM((256, width), F32),),
        after=after,
    )


def act_join_kernel(idx_ref, a_ref, b_ref, out, tick):
    tick[...] = jnp.zeros_like(tick)

    @pl.loop(0, 16)
    def _(n):
        out[idx_ref[n]] = a_ref[n]
        out[idx_ref[16 + n]] = b_ref[n]


def last_kernel(kept, received, out):
    out[...] = (kept[...] + received[...].astype(F32)).astype(BF16)


def xgrad_kernel(p_ref, w_ref, own_ref, other_ref):
    @pl.loop(0, w_ref.shape[0] // 512)
    def _(s):
        cols = pl.ds(pl.multiple_of(s * 512, 512), 512)
        part = lax.dot_general(
            p_ref[...], w_ref[cols, :], (((1,), (1,)), ((), ())), preferred_element_type=F32
        )
        own_ref[:, cols] = part[:128, :]
        other_ref[:, cols] = part[128:, :].astype(BF16)


def xgrad(p, masked, after=()):
    d, width = masked.shape
    return call(
        xgrad_kernel,
        0,
        (jax.ShapeDtypeStruct((128, d), F32), jax.ShapeDtypeStruct((128, d), BF16)),
        (p, masked),
        2 * 256 * d * width,
        after=after,
    )


def mix_kernel(own_ref, r_ref, near1, near2, near3, far, home):
    @pl.loop(0, own_ref.shape[1] // 512)
    def _(s):
        cols = pl.ds(pl.multiple_of(s * 512, 512), 512)
        total = (own_ref[:, cols] + r_ref[:, cols].astype(F32)).astype(BF16)
        home[:, cols] = total[0:16, :]
        far[:, cols] = total[16:32, :]
        near1[:, cols] = total[32:64, :]
        near2[:, cols] = total[64:96, :]
        near3[:, cols] = total[96:128, :]


def mix(own, received, after):
    d = own.shape[1]
    return call(
        mix_kernel,
        0,
        [jax.ShapeDtypeStruct((32, d), BF16)] * 3 + [jax.ShapeDtypeStruct((16, d), BF16)] * 2,
        (own, received),
        128 * d,
        after=after,
    )


def hop_kernel(near, one, two, out):
    @pl.loop(0, near.shape[1] // 512)
    def _(s):
        cols = pl.ds(pl.multiple_of(s * 512, 512), 512)
        total = near[:, cols].astype(F32) + one[:, cols].astype(F32)
        out[0:16, cols] = (total[0:16] + two[:, cols].astype(F32)).astype(BF16)
        out[16:32, cols] = total[16:32].astype(BF16)


def hop(near, one, two, after):
    shape = jax.ShapeDtypeStruct(near.shape, BF16)
    return call(hop_kernel, 0, shape, (near, one, two), 2 * near.size, after=after)


def sum_kernel(*refs):
    halves, to_core, kept = (refs[0:3], refs[3:6]), refs[6], refs[7]

    @pl.loop(0, kept.shape[1] // 512)
    def _(s):
        cols = pl.ds(pl.multiple_of(s * 512, 512), 512)
        for q, (one, two, home) in enumerate(halves):
            rows = slice(q * 16, q * 16 + 16)
            total = one[:, cols].astype(F32) + two[:, cols].astype(F32)
            kept[rows, cols] = home[:, cols].astype(F32) + total[0:16]
            to_core[rows, cols] = total[16:32].astype(BF16)


def sum_core_kernel(kept, received, to_x, out):
    @pl.loop(0, kept.shape[1] // 512)
    def _(s):
        cols = pl.ds(pl.multiple_of(s * 512, 512), 512)
        total = kept[:, cols] + received[:, cols].astype(F32)
        out[:, cols] = total[0:16, :]
        to_x[:, cols] = total[16:32, :].astype(BF16)


def place_of(code):
    return (
        pl.multiple_of(code & 1023, BLOCK),
        pl.multiple_of((code >> 10) & 1023, 128),
        code >> 20,
    )


def wgrad_kernel(first, dest_ref, code_ref, odd_ref, pa, pb, x0, x1, x2, x3, *rest):
    outs, acc_ref = rest[:-1], rest[-1]
    left = lax.broadcasted_iota(jnp.int32, (BLOCK, 128), 1) < BLOCK
    over_rows = (((0,), (0,)), ((), ()))
    for n, out in enumerate(outs):
        dest = dest_ref[first + n]
        cols = pl.ds(pl.multiple_of(dest * 512, 512), 512)
        xa = jnp.concatenate([x0[:, cols], x2[:, cols]], axis=0)
        xb = jnp.concatenate([x1[:, cols], x3[:, cols]], axis=0)
        acc_ref[...] = lax.dot_general(
            xa, pa[...], over_rows, preferred_element_type=F32
        ) + lax.dot_general(xb, pb[...], over_rows, preferred_element_type=F32)

        def tiles(s):
            row, lane, h = place_of(code_ref[dest, s])
            row2, lane2, h2 = place_of(code_ref[dest, PAIRS + s])
            return (
                acc_ref[pl.ds(row, BLOCK), pl.ds(lane, 128)],
                acc_ref[pl.ds(row2, BLOCK), pl.ds(lane2, 128)],
                h & 1,
                h2 & 1,
            )

        def pack(s, carry):
            one, two, _, _ = tiles(s)
            out[s] = jnp.where(left, one, two).astype(BF16)
            return carry

        def repack(n, carry):
            s = PAIRS - 1 - n
            one, two, h, h2 = tiles(s)
            one = pltpu.roll(one, h * BLOCK, 1)
            two = pltpu.roll(two, (1 - h2) * BLOCK, 1)
            out[s] = jnp.where(left, one, two).astype(BF16)
            return carry

        lax.fori_loop(0, PAIRS, pack, 0, unroll=5)
        lax.fori_loop(0, odd_ref[dest], repack, 0)


def wgrad(first, count, scalars, pa, pb, xs, after):
    width = pa.shape[1]
    return call(
        functools.partial(wgrad_kernel, first),
        3,
        [jax.ShapeDtypeStruct((PAIRS, BLOCK, 128), BF16)] * count,
        (*scalars, pa, pb, *xs),
        2 * 512 * 512 * width * count,
        scratch=(pltpu.VMEM((512, width), F32),),
        after=after,
    )


def presum_kernel(*refs):
    parts, out = refs[:-1], refs[-1]

    @pl.loop(0, PAIRS)
    def _(s):
        total = parts[0][s].astype(F32)
        for part in parts[1:]:
            total = total + part[s].astype(F32)
        out[s] = total


def unpack_kernel(own_ref, code_ref, *refs):
    parts, (out, buf, sems) = refs[:-3], refs[-3:]
    own = own_ref[0]
    buf[...] = jnp.zeros_like(buf)
    half = lax.broadcasted_iota(jnp.int32, (BLOCK, 128), 1) // BLOCK

    def place(s, carry):
        total = parts[0][s]
        for part in parts[1:]:
            total = total + part[s].astype(F32)
        other = pltpu.roll(total, BLOCK, 1)
        for side in range(2):
            row, lane, h = place_of(code_ref[own, side * PAIRS + s])
            value = jnp.where(h == side, total, other)
            at = buf.at[pl.ds(row, BLOCK), pl.ds(lane, 128)]
            pltpu.store(at, value, mask=half == h)
        return carry

    lax.fori_loop(0, PAIRS, place, 0, unroll=5)
    copies = []
    for c in range(4):
        rows = slice(c * 128, (c + 1) * 128)
        copies.append(pltpu.make_async_copy(buf.at[rows], out.at[rows], sems.at[c]))
        copies[-1].start()
    for copy in copies:
        copy.wait()


def slots_of(block_mask, t):
    mask = lax.dynamic_slice(block_mask, (0, t * 14), (64, 14)).reshape(8, 112)
    kept = mask != 0
    at = jnp.arange(112, dtype=jnp.int32)
    h = jnp.array([b % 14 % 2 for b in range(112)], jnp.int32)
    before = (at[:, None] <= at[None, :]) & (h[:, None] == h[None, :])
    rank = jnp.dot(kept.astype(BF16), before.astype(BF16), preferred_element_type=F32)
    rank = rank.astype(jnp.int32) - 1
    extra = rank >= PAIRS
    slot = jnp.where(extra, 3 * PAIRS - 1 - PAIRS * h - rank, rank + PAIRS * h)
    odd = jnp.sum((kept & extra).astype(jnp.int32), axis=1, dtype=jnp.int32)
    return jnp.where(kept, slot, -1), odd


def codes_of(slot):
    i = jnp.array([b // 14 for b in range(112)], jnp.int32)
    j = jnp.array([b % 14 for b in range(112)], jnp.int32)
    hit = slot[:, None, :] == jnp.arange(CAP, dtype=jnp.int32)[None, :, None]
    code = i * BLOCK + (j >> 1) * (128 << 10) + (((j & 1) - 2) << 20)
    return jnp.sum(jnp.where(hit, code[None, None, :], 0), axis=2, dtype=jnp.int32) + (2 << 20)


def layer(tokens, weight, block_mask, act_grad):
    d, width = weight.shape
    t = lax.axis_index("tensor").astype(jnp.int32)
    g = lax.axis_index("dp").astype(jnp.int32)

    partner = move(tokens, dc=1)
    home = move(tokens, dx=1)
    lifted = call(head_kernel, 0, jax.ShapeDtypeStruct(tokens.shape, BF16), (tokens,), 0)
    chip = join(lifted, partner)
    t, g, chip = lax.optimization_barrier((t, g, chip))
    z, xh, core = t >> 2, (t >> 1) & 1, t & 1
    xl, y = g >> 2, g & 3

    n = jnp.arange(32, dtype=jnp.int32)
    slot = n & 7
    dist = jnp.where(slot == 0, 0, jnp.where(slot == 1, 4, slot >> 1))
    flip = jnp.where(slot > 1, slot & 1, 0)
    gather_core = core ^ ((n >> 3) & 1)
    zk = (z - (1 - 2 * gather_core) * dist) & (NZ - 1)
    idx = zk * 4 + (xh ^ (n >> 4)) * 2 + (gather_core ^ flip)
    order = [(1, 1), (0, 3), (1, 2), (0, 1), (1, 3), (1, 0), (0, 2), (0, 0)]
    dx = jnp.array([o[0] for o in order], jnp.int32)
    dy = jnp.array([o[1] for o in order], jnp.int32)
    dests = (xl ^ dx) * NY + ((y + dy) & (NY - 1))

    def tick():
        return call(tick_kernel, 0, jax.ShapeDtypeStruct((8, 128), F32), (), 0)

    ticks = [tick() for _ in range(4)]
    near1, near2 = move(chip, dz=1), move(chip, dz=2)
    t_slot, ticks[0] = lax.optimization_barrier((t, ticks[0]))
    slot, odd = slots_of(block_mask, t_slot)
    slot, odd, idx, dests, near1 = lax.optimization_barrier((slot, odd, idx, dests, near1))
    slot, ticks[1] = lax.optimization_barrier((slot, ticks[1]))
    code, near2 = lax.optimization_barrier((codes_of(slot), near2))
    scalars = (dests, code, odd)

    near3 = move(near2, dz=1)
    head = call(head_kernel, 0, jax.ShapeDtypeStruct((16, d), BF16), (near2,), 0)
    far = move(head, dz=2)
    t_mask, ticks[2] = lax.optimization_barrier((t, ticks[2]))
    masked = call(
        mask_kernel,
        1,
        jax.ShapeDtypeStruct((d, width), BF16),
        ((t_mask * 14).reshape(1), weight, block_mask),
        d * width,
        scratch=(
            pltpu.VMEM(block_mask.shape, jnp.int32),
            pltpu.VMEM((block_mask.shape[0], width), F32),
            pltpu.SemaphoreType.DMA((9,)),
        ),
        space=pl.BlockSpec(memory_space=pl.ANY),
        limit=44,
    )
    near3, masked = lax.optimization_barrier((near3, masked))

    cross = [move(v, dx=1) for v in (near1, near2, near3, far)]
    x0 = join(lifted, far, near1, near2, near3)
    x2 = move(x0, dc=1)
    x1 = join(home, cross[3], *cross[:3])
    x3 = move(x1, dc=1)
    xs = (x0, x1, x2, x3)

    grads = act_grad.reshape(32, 16, width)
    act_a, pa = forward(0, idx, x0, x2, masked, grads, after=ticks)
    own_a, other_a = xgrad(pa, masked)
    received_a = move(other_a, dc=1)
    act_b, pb = forward(16, idx, x1, x3, masked, grads, after=(other_a,))

    parts = []

    def pack(first, count, after):
        packed = wgrad(first, count, scalars, pa, pb, xs, (after,))
        for v, o in zip(packed, order[first : first + count]):
            parts.append(v if o == (0, 0) else move_dp(v, *o))
        return packed[0]

    def back(x, hops):
        return move(x, dz=NZ - hops)

    done = pack(0, 2, other_a)
    done = pack(2, 2, done)
    a1, a2, a3, a4, home_a = mix(own_a, received_a, (done,))
    from_a3, from_a4 = back(a3, 1), back(a4, 2)
    own_b, other_b = xgrad(pb, masked, (a4,))
    received_b = move(other_b, dc=1)
    done = pack(4, 3, other_b)
    b1, b2, b3, b4, home_b = mix(own_b, received_b, (done,))
    from_b3, from_b4, from_b1 = back(b3, 1), back(b4, 2), back(b1, 1)
    done = hop(a2, from_a3, from_a4, (b4,))
    from_a2 = back(done, 2)
    done = hop(b2, from_b3, from_b4, (done,))
    a1, done = lax.optimization_barrier((a1, done))
    from_b2, from_a1 = back(done, 2), back(a1, 1)
    done = pack(7, 1, done)
    order_after = jax.ShapeDtypeStruct((8, 128), F32)
    act, done = call(
        act_join_kernel,
        1,
        (jax.ShapeDtypeStruct((32, 16, width), BF16), order_after),
        (idx, act_a, act_b),
        0,
        after=(done,),
    )

    early = call(
        presum_kernel,
        0,
        jax.ShapeDtypeStruct((PAIRS, BLOCK, 128), F32),
        (parts[7], *parts[:4]),
        5 * CAP * 4096,
        after=(done,),
    )
    to_core, kept = call(
        sum_kernel,
        0,
        (jax.ShapeDtypeStruct((32, d), BF16), jax.ShapeDtypeStruct((32, d), F32)),
        (from_a1, from_a2, home_a, from_b1, from_b2, home_b),
        6 * 32 * d,
    )
    to_x, kept = call(
        sum_core_kernel,
        0,
        (jax.ShapeDtypeStruct((16, d), BF16), jax.ShapeDtypeStruct((16, d), F32)),
        (kept, move(to_core, dc=1)),
        32 * d,
    )
    x_grad = call(
        last_kernel, 0, jax.ShapeDtypeStruct((16, d), BF16), (kept, move(to_x, dx=1)), 16 * d
    )

    weight_grad = call(
        unpack_kernel,
        2,
        jax.ShapeDtypeStruct((512, width), F32),
        (g.reshape(1), code, early, *parts[4:7]),
        8 * CAP * 4096,
        scratch=(
            pltpu.VMEM((512, width), F32),
            pltpu.SemaphoreType.DMA((4,)),
        ),
        out_space=pl.BlockSpec(memory_space=pl.ANY),
    )
    return (act.reshape(512, width), x_grad, weight_grad)


def solution(mesh):
    return jax.shard_map(
        layer,
        mesh=mesh,
        in_specs=(P(("dp", "tensor"), None), P(None, "tensor"), P(), P("dp", "tensor")),
        out_specs=(P("dp", "tensor"), P(("dp", "tensor"), None), P("dp", "tensor")),
        check_vma=False,
    )
```

```python
import functools

import jax
import jax.numpy as jnp
from jax import lax
from jax.experimental import pallas as pl
from jax.experimental.pallas import tpu as pltpu
from jax.sharding import PartitionSpec as P


BLOCK = 64
CAP = 70
PAIRS = CAP // 2
NZ = 8
NY = 4
F32 = jnp.float32
BF16 = jnp.bfloat16


VMEM = pl.BlockSpec(memory_space=pltpu.VMEM)
SMEM = pl.BlockSpec(memory_space=pltpu.SMEM)


def tensor_perm(dz, dx, dc, split=False):
    pairs = []
    for z in range(NZ):
        for xh in range(2):
            for core in range(2):
                shift = -dz if split and core else dz
                source = (z * 2 + xh) * 2 + core
                target = (((z + shift) % NZ) * 2 + (xh ^ dx)) * 2 + (core ^ dc)
                pairs.append((source, target))
    return pairs


def dp_perm(dx, dy):
    return [
        (xl * NY + y, (xl ^ dx) * NY + (y + dy) % NY) for xl in range(2) for y in range(NY)
    ]


def move(x, dz=0, dx=0, dc=0):
    return lax.ppermute(x, "tensor", tensor_perm(dz, dx, dc, split=True))


def move_dp(x, dx, dy):
    return lax.ppermute(x, "dp", dp_perm(dx, dy))


def call(
    kernel, n_scalar, out_shape, args, flops, scratch=(), after=(), limit=12, out_space=VMEM,
    space=VMEM,
):
    n_args, n_after = len(args), len(after)

    def run(*refs):
        kernel(*refs[:n_args], *refs[n_args + n_after :])

    n_out = len(out_shape) if isinstance(out_shape, (tuple, list)) else 1
    out_specs = [VMEM] * n_out if isinstance(out_shape, (tuple, list)) else out_space
    moved = sum(a.size * a.dtype.itemsize for a in args)
    return pl.pallas_call(
        run,
        out_shape=out_shape,
        in_specs=[SMEM] * n_scalar
        + [space] * (n_args - n_scalar)
        + [pl.BlockSpec(memory_space=pl.ANY)] * n_after,
        out_specs=out_specs,
        scratch_shapes=list(scratch),
        compiler_params=pltpu.CompilerParams(vmem_limit_bytes=limit << 20),
        cost_estimate=pl.CostEstimate(flops=flops, bytes_accessed=moved, transcendentals=0),
    )(*args, *after)


def tick_kernel(*refs):
    refs[-1][...] = jnp.zeros_like(refs[-1])


def join_kernel(*refs):
    parts, out = refs[:-1], refs[-1]
    at = 0
    for part in parts:
        out[at : at + part.shape[0], :] = part[...]
        at += part.shape[0]


def join(*parts):
    rows = sum(part.shape[0] for part in parts)
    shape = jax.ShapeDtypeStruct((rows, parts[0].shape[1]), BF16)
    return call(join_kernel, 0, shape, parts, 0)


def head_kernel(x_ref, o_ref):
    o_ref[...] = x_ref[0 : o_ref.shape[0], :]


def mask_kernel(t_ref, w_hbm, m_hbm, o_ref, m_ref, e_ref, sems):
    n_rows, blocks = m_ref.shape
    width = o_ref.shape[1]
    groups = n_rows // 8

    def part(g):
        rows = pl.ds(pl.multiple_of(g * 512, 512), 512)
        return pltpu.make_async_copy(w_hbm.at[rows], o_ref.at[rows], sems.at[g])

    mask_copy = pltpu.make_async_copy(m_hbm, m_ref, sems.at[groups])
    mask_copy.start()
    for g in range(groups):
        part(g).start()
    rows = lax.broadcasted_iota(jnp.int32, (blocks, width), 0)
    cols = lax.broadcasted_iota(jnp.int32, (blocks, width), 1)
    pick = (rows == t_ref[0] + lax.div(cols, BLOCK)).astype(BF16)
    mask_copy.wait()
    e_ref[...] = jnp.dot(m_ref[...].astype(F32).astype(BF16), pick, preferred_element_type=F32)

    @pl.loop(0, groups)
    def _(g):
        part(g).wait()
        eight = e_ref[pl.ds(pl.multiple_of(g * 8, 8), 8), :]
        for i in range(8):
            at = pl.ds(pl.multiple_of(g * 512 + i * BLOCK, BLOCK), BLOCK)
            row = jnp.broadcast_to(eight[i : i + 1, :], (BLOCK, width)).astype(BF16)
            o_ref[at, :] = o_ref[at, :] * row


def forward_kernel(first, idx_ref, xa, xb, w_ref, g_ref, act_ref, p_ref, acc_ref):
    d = w_ref.shape[0]
    kb = 2048

    def product(s):
        cols = pl.ds(pl.multiple_of(s * kb, kb), kb)
        x = jnp.concatenate([xa[:, cols], xb[:, cols]], axis=0)
        return jnp.dot(x, w_ref[cols, :], preferred_element_type=F32)

    acc_ref[...] = product(0)

    @pl.loop(1, d // kb)
    def _(s):
        acc_ref[...] += product(s)

    def finish(n, carry):
        rows = pl.ds(pl.multiple_of(n * 16, 16), 16)
        pre = acc_ref[rows, :]
        s = jax.nn.sigmoid(pre)
        act_ref[n] = (pre * s).astype(BF16)
        grad = g_ref[idx_ref[first + n]].astype(F32) * s * (1.0 + pre * (1.0 - s))
        p_ref[rows, :] = grad.astype(BF16)
        return carry

    lax.fori_loop(0, act_ref.shape[0], finish, 0, unroll=4)


def forward(first, idx, xa, xb, masked, act_grad, after=()):
    d, width = masked.shape
    return call(
        functools.partial(forward_kernel, first),
        1,
        (
            jax.ShapeDtypeStruct((16, 16, width), BF16),
            jax.ShapeDtypeStruct((256, width), BF16),
        ),
        (idx, xa, xb, masked, act_grad),
        2 * 256 * d * width,
        scratch=(pltpu.VMEM((256, width), F32),),
        after=after,
    )


def act_join_kernel(idx_ref, a_ref, b_ref, out, tick):
    tick[...] = jnp.zeros_like(tick)

    @pl.loop(0, 16)
    def _(n):
        out[idx_ref[n]] = a_ref[n]
        out[idx_ref[16 + n]] = b_ref[n]


def last_kernel(kept, received, out, tick):
    tick[...] = jnp.zeros_like(tick)
    out[...] = (kept[...] + received[...].astype(F32)).astype(BF16)


def xgrad_kernel(p_ref, w_ref, own_ref, other_ref):
    @pl.loop(0, w_ref.shape[0] // 512)
    def _(s):
        cols = pl.ds(pl.multiple_of(s * 512, 512), 512)
        part = lax.dot_general(
            p_ref[...], w_ref[cols, :], (((1,), (1,)), ((), ())), preferred_element_type=F32
        )
        own_ref[:, cols] = part[:128, :]
        other_ref[:, cols] = part[128:, :].astype(BF16)


def xgrad(p, masked, after=()):
    d, width = masked.shape
    return call(
        xgrad_kernel,
        0,
        (jax.ShapeDtypeStruct((128, d), F32), jax.ShapeDtypeStruct((128, d), BF16)),
        (p, masked),
        2 * 256 * d * width,
        after=after,
    )


def mix_kernel(own_ref, r_ref, near1, near2, near3, far, home):
    @pl.loop(0, own_ref.shape[1] // 512)
    def _(s):
        cols = pl.ds(pl.multiple_of(s * 512, 512), 512)
        total = (own_ref[:, cols] + r_ref[:, cols].astype(F32)).astype(BF16)
        home[:, cols] = total[0:16, :]
        far[:, cols] = total[16:32, :]
        near1[:, cols] = total[32:64, :]
        near2[:, cols] = total[64:96, :]
        near3[:, cols] = total[96:128, :]


def mix(own, received, after):
    d = own.shape[1]
    return call(
        mix_kernel,
        0,
        [jax.ShapeDtypeStruct((32, d), BF16)] * 3 + [jax.ShapeDtypeStruct((16, d), BF16)] * 2,
        (own, received),
        128 * d,
        after=after,
    )


def hop_kernel(near, one, two, out):
    @pl.loop(0, near.shape[1] // 512)
    def _(s):
        cols = pl.ds(pl.multiple_of(s * 512, 512), 512)
        total = near[:, cols].astype(F32) + one[:, cols].astype(F32)
        out[0:16, cols] = (total[0:16] + two[:, cols].astype(F32)).astype(BF16)
        out[16:32, cols] = total[16:32].astype(BF16)


def hop(near, one, two, after):
    shape = jax.ShapeDtypeStruct(near.shape, BF16)
    return call(hop_kernel, 0, shape, (near, one, two), 2 * near.size, after=after)


def sum_kernel(*refs):
    halves, to_core, kept = (refs[0:3], refs[3:6]), refs[6], refs[7]

    @pl.loop(0, kept.shape[1] // 512)
    def _(s):
        cols = pl.ds(pl.multiple_of(s * 512, 512), 512)
        for q, (one, two, home) in enumerate(halves):
            rows = slice(q * 16, q * 16 + 16)
            total = one[:, cols].astype(F32) + two[:, cols].astype(F32)
            kept[rows, cols] = home[:, cols].astype(F32) + total[0:16]
            to_core[rows, cols] = total[16:32].astype(BF16)


def sum_core_kernel(kept, received, to_x, out):
    @pl.loop(0, kept.shape[1] // 512)
    def _(s):
        cols = pl.ds(pl.multiple_of(s * 512, 512), 512)
        total = kept[:, cols] + received[:, cols].astype(F32)
        out[:, cols] = total[0:16, :]
        to_x[:, cols] = total[16:32, :].astype(BF16)


def place_of(code):
    return (
        pl.multiple_of(code & 1023, BLOCK),
        pl.multiple_of((code >> 10) & 1023, 128),
        code >> 20,
    )


def wgrad_kernel(first, dest_ref, code_ref, odd_ref, pa, pb, x0, x1, x2, x3, *rest):
    outs, acc_ref = rest[:-1], rest[-1]
    left = lax.broadcasted_iota(jnp.int32, (BLOCK, 128), 1) < BLOCK
    over_rows = (((0,), (0,)), ((), ()))
    for n, out in enumerate(outs):
        dest = dest_ref[first + n]
        cols = pl.ds(pl.multiple_of(dest * 512, 512), 512)
        xa = jnp.concatenate([x0[:, cols], x2[:, cols]], axis=0)
        xb = jnp.concatenate([x1[:, cols], x3[:, cols]], axis=0)
        acc_ref[...] = lax.dot_general(
            xa, pa[...], over_rows, preferred_element_type=F32
        ) + lax.dot_general(xb, pb[...], over_rows, preferred_element_type=F32)

        def tiles(s):
            row, lane, h = place_of(code_ref[dest, s])
            row2, lane2, h2 = place_of(code_ref[dest, PAIRS + s])
            return (
                acc_ref[pl.ds(row, BLOCK), pl.ds(lane, 128)],
                acc_ref[pl.ds(row2, BLOCK), pl.ds(lane2, 128)],
                h & 1,
                h2 & 1,
            )

        def pack(s, carry):
            one, two, _, _ = tiles(s)
            out[s] = jnp.where(left, one, two).astype(BF16)
            return carry

        def repack(n, carry):
            s = PAIRS - 1 - n
            one, two, h, h2 = tiles(s)
            one = pltpu.roll(one, h * BLOCK, 1)
            two = pltpu.roll(two, (1 - h2) * BLOCK, 1)
            out[s] = jnp.where(left, one, two).astype(BF16)
            return carry

        lax.fori_loop(0, PAIRS, pack, 0, unroll=5)
        lax.fori_loop(0, odd_ref[dest], repack, 0)


def wgrad(first, count, scalars, pa, pb, xs, after):
    width = pa.shape[1]
    return call(
        functools.partial(wgrad_kernel, first),
        3,
        [jax.ShapeDtypeStruct((PAIRS, BLOCK, 128), BF16)] * count,
        (*scalars, pa, pb, *xs),
        2 * 512 * 512 * width * count,
        scratch=(pltpu.VMEM((512, width), F32),),
        after=after,
    )


def presum_kernel(*refs):
    parts, out = refs[:-1], refs[-1]

    @pl.loop(0, PAIRS)
    def _(s):
        total = parts[0][s].astype(F32)
        for part in parts[1:]:
            total = total + part[s].astype(F32)
        out[s] = total


def unpack_kernel(own_ref, code_ref, *refs):
    parts, (out, buf, sems) = refs[:-3], refs[-3:]
    own = own_ref[0]
    buf[...] = jnp.zeros_like(buf)
    half = lax.broadcasted_iota(jnp.int32, (BLOCK, 128), 1) // BLOCK

    def place(s, carry):
        total = parts[0][s]
        for part in parts[1:]:
            total = total + part[s].astype(F32)
        other = pltpu.roll(total, BLOCK, 1)
        for side in range(2):
            row, lane, h = place_of(code_ref[own, side * PAIRS + s])
            value = jnp.where(h == side, total, other)
            at = buf.at[pl.ds(row, BLOCK), pl.ds(lane, 128)]
            pltpu.store(at, value, mask=half == h)
        return carry

    lax.fori_loop(0, PAIRS, place, 0, unroll=5)
    copies = []
    for c in range(4):
        rows = slice(c * 128, (c + 1) * 128)
        copies.append(pltpu.make_async_copy(buf.at[rows], out.at[rows], sems.at[c]))
        copies[-1].start()
    for copy in copies:
        copy.wait()


def slots_of(block_mask, t):
    mask = lax.dynamic_slice(block_mask, (0, t * 14), (64, 14)).reshape(8, 112)
    kept = mask != 0
    at = jnp.arange(112, dtype=jnp.int32)
    h = jnp.array([b % 14 % 2 for b in range(112)], jnp.int32)
    before = (at[:, None] <= at[None, :]) & (h[:, None] == h[None, :])
    rank = jnp.dot(kept.astype(BF16), before.astype(BF16), preferred_element_type=F32)
    rank = rank.astype(jnp.int32) - 1
    extra = rank >= PAIRS
    slot = jnp.where(extra, 3 * PAIRS - 1 - PAIRS * h - rank, rank + PAIRS * h)
    odd = jnp.sum((kept & extra).astype(jnp.int32), axis=1, dtype=jnp.int32)
    return jnp.where(kept, slot, -1), odd


def codes_of(slot):
    i = jnp.array([b // 14 for b in range(112)], jnp.int32)
    j = jnp.array([b % 14 for b in range(112)], jnp.int32)
    hit = slot[:, None, :] == jnp.arange(CAP, dtype=jnp.int32)[None, :, None]
    code = i * BLOCK + (j >> 1) * (128 << 10) + (((j & 1) - 2) << 20)
    return jnp.sum(jnp.where(hit, code[None, None, :], 0), axis=2, dtype=jnp.int32) + (2 << 20)


def layer(tokens, weight, block_mask, act_grad):
    d, width = weight.shape
    t = lax.axis_index("tensor").astype(jnp.int32)
    g = lax.axis_index("dp").astype(jnp.int32)

    partner = move(tokens, dc=1)
    home = move(tokens, dx=1)
    lifted = call(head_kernel, 0, jax.ShapeDtypeStruct(tokens.shape, BF16), (tokens,), 0)
    chip = join(lifted, partner)
    t, g, chip = lax.optimization_barrier((t, g, chip))
    z, xh, core = t >> 2, (t >> 1) & 1, t & 1
    xl, y = g >> 2, g & 3

    n = jnp.arange(32, dtype=jnp.int32)
    slot = n & 7
    dist = jnp.where(slot == 0, 0, jnp.where(slot == 1, 4, slot >> 1))
    flip = jnp.where(slot > 1, slot & 1, 0)
    gather_core = core ^ ((n >> 3) & 1)
    zk = (z - (1 - 2 * gather_core) * dist) & (NZ - 1)
    idx = zk * 4 + (xh ^ (n >> 4)) * 2 + (gather_core ^ flip)
    order = [(1, 1), (0, 3), (1, 2), (1, 3), (0, 1), (1, 0), (0, 2), (0, 0)]
    dx = jnp.array([o[0] for o in order], jnp.int32)
    dy = jnp.array([o[1] for o in order], jnp.int32)
    dests = (xl ^ dx) * NY + ((y + dy) & (NY - 1))

    def tick():
        return call(tick_kernel, 0, jax.ShapeDtypeStruct((8, 128), F32), (), 0)

    ticks = [tick() for _ in range(4)]
    near1, near2 = move(chip, dz=1), move(chip, dz=2)
    t_slot, ticks[0] = lax.optimization_barrier((t, ticks[0]))
    slot, odd = slots_of(block_mask, t_slot)
    slot, odd, idx, dests, near1 = lax.optimization_barrier((slot, odd, idx, dests, near1))
    slot, ticks[1] = lax.optimization_barrier((slot, ticks[1]))
    code, near2 = lax.optimization_barrier((codes_of(slot), near2))
    scalars = (dests, code, odd)

    near3 = move(near2, dz=1)
    head = call(head_kernel, 0, jax.ShapeDtypeStruct((16, d), BF16), (near2,), 0)
    far = move(head, dz=2)
    t_mask, ticks[2] = lax.optimization_barrier((t, ticks[2]))
    masked = call(
        mask_kernel,
        1,
        jax.ShapeDtypeStruct((d, width), BF16),
        ((t_mask * 14).reshape(1), weight, block_mask),
        d * width,
        scratch=(
            pltpu.VMEM(block_mask.shape, jnp.int32),
            pltpu.VMEM((block_mask.shape[0], width), F32),
            pltpu.SemaphoreType.DMA((9,)),
        ),
        space=pl.BlockSpec(memory_space=pl.ANY),
        limit=44,
    )
    near3, masked = lax.optimization_barrier((near3, masked))

    cross = [move(v, dx=1) for v in (near1, near2, near3, far)]
    x0 = join(lifted, far, near1, near2, near3)
    x2 = move(x0, dc=1)
    x1 = join(home, cross[3], *cross[:3])
    x3 = move(x1, dc=1)
    xs = (x0, x1, x2, x3)

    grads = act_grad.reshape(32, 16, width)
    act_a, pa = forward(0, idx, x0, x2, masked, grads, after=ticks)
    own_a, other_a = xgrad(pa, masked)
    received_a = move(other_a, dc=1)
    act_b, pb = forward(16, idx, x1, x3, masked, grads, after=(other_a,))

    parts = []

    def pack(first, count, after):
        packed = wgrad(first, count, scalars, pa, pb, xs, (after,))
        for v, o in zip(packed, order[first : first + count]):
            parts.append(v if o == (0, 0) else move_dp(v, *o))
        return packed[0]

    def back(x, hops):
        return move(x, dz=NZ - hops)

    done = pack(0, 1, other_a)
    done = pack(1, 2, done)
    a1, a2, a3, a4, home_a = mix(own_a, received_a, (done,))
    from_a3, from_a4 = back(a3, 1), back(a4, 2)
    own_b, other_b = xgrad(pb, masked, (a4,))
    received_b = move(other_b, dc=1)
    done = pack(3, 2, other_b)
    b1, b2, b3, b4, home_b = mix(own_b, received_b, (done,))
    from_b3, from_b4, from_b1 = back(b3, 1), back(b4, 2), back(b1, 1)
    done = hop(a2, from_a3, from_a4, (b4,))
    from_a2 = back(done, 2)
    done = pack(5, 2, done)
    done = hop(b2, from_b3, from_b4, (done,))
    a1, done = lax.optimization_barrier((a1, done))
    from_b2, from_a1 = back(done, 2), back(a1, 1)
    done = pack(7, 1, done)
    order_after = jax.ShapeDtypeStruct((8, 128), F32)
    act, done = call(
        act_join_kernel,
        1,
        (jax.ShapeDtypeStruct((32, 16, width), BF16), order_after),
        (idx, act_a, act_b),
        0,
        after=(done,),
    )

    early = call(
        presum_kernel,
        0,
        jax.ShapeDtypeStruct((PAIRS, BLOCK, 128), F32),
        (parts[7], *parts[:4]),
        5 * CAP * 4096,
        after=(done,),
    )
    to_core, kept = call(
        sum_kernel,
        0,
        (jax.ShapeDtypeStruct((32, d), BF16), jax.ShapeDtypeStruct((32, d), F32)),
        (from_a1, from_a2, home_a, from_b1, from_b2, home_b),
        6 * 32 * d,
    )
    to_x, kept = call(
        sum_core_kernel,
        0,
        (jax.ShapeDtypeStruct((16, d), BF16), jax.ShapeDtypeStruct((16, d), F32)),
        (kept, move(to_core, dc=1)),
        32 * d,
    )
    x_grad, done = call(
        last_kernel,
        0,
        (jax.ShapeDtypeStruct((16, d), BF16), order_after),
        (kept, move(to_x, dx=1)),
        16 * d,
    )

    weight_grad = call(
        unpack_kernel,
        2,
        jax.ShapeDtypeStruct((512, width), F32),
        (g.reshape(1), code, early, *parts[4:7]),
        8 * CAP * 4096,
        scratch=(
            pltpu.VMEM((512, width), F32),
            pltpu.SemaphoreType.DMA((4,)),
        ),
        after=(done,),
        out_space=pl.BlockSpec(memory_space=pl.ANY),
    )
    return (act.reshape(512, width), x_grad, weight_grad)


def solution(mesh):
    return jax.shard_map(
        layer,
        mesh=mesh,
        in_specs=(P(("dp", "tensor"), None), P(None, "tensor"), P(), P("dp", "tensor")),
        out_specs=(P("dp", "tensor"), P(("dp", "tensor"), None), P("dp", "tensor")),
        check_vma=False,
    )
```
